256 devices in a mesh: ctx: 16 (over x, z_hi, core), tp: 16 (over y, z_lo).
Axes of the slice: x: 4, y: 4, z: 8 (z_hi: 2, z_lo: 4; z = z_hi * 4 + z_lo), core: 2. Of those that a mesh axis runs over, the one named last changes fastest.
Arguments:
- inputs: bfloat16 [4096, 8192], P('tp', 'ctx'), may hold values from -6 to 6
- gates: bfloat16 [4096, 8192], P('tp', 'ctx'), may hold values from -6 to 6
- filters: bfloat16 [4096, 8192], P('tp', 'ctx'), may hold values from -6 to 6
- out_grad: bfloat16 [4096, 8192], P('tp', 'ctx'), may hold values from -6 to 6
- out_weight: bfloat16 [4096, 4096], P('ctx', 'tp'), may hold values from -0.09375 to 0.09375
Outputs:
- input_grad: bfloat16 [4096, 8192], P('tp', 'ctx')
- gate_grad: bfloat16 [4096, 8192], P('tp', 'ctx')
- filter_grad: bfloat16 [4096, 8192], P('tp', 'ctx')
- weight_grad: bfloat16 [4096, 4096], P('ctx', 'tp')
The draws below stay inside these ranges and needn't reach their ends.
All inputs are finite; a program needn't handle non-finite values.
Results may differ from the reference program's by a relative error of at most 0.019.
Values may be sent and summed in bfloat16 or wider, within the bound.
No kernel may reach another device: no remote copies, remote signals or barrier semaphores. Data moves between devices by JAX's collectives and lax.ppermute only.
A program may use at most 128 MiB of HBM per device.

```python
import jax
import jax.numpy as jnp
from jax import lax

D = 4096
SEQ = 8192


def spiked(array, stream_key, source, target, shards_of, factor):
    def block_of(dim):
        return (jnp.arange(array.shape[dim]) // (array.shape[dim] // shards_of)).reshape((-1,) + (1,) * (array.ndim - 1 - dim))

    near = jax.random.permutation(stream_key, shards_of)[block_of(target)]
    second = (block_of(target) + shards_of // 2) % shards_of
    return jnp.where((block_of(source) == near) | (block_of(source) == second), factor * array, array)


def shard_levels(rng, shape, split, low, top_value):
    def one(position, parts):
        heights = jax.random.uniform(jax.random.fold_in(jax.random.fold_in(rng, 6), position), (parts,), jnp.float32, low / len(split), top_value / len(split))
        return jnp.repeat(jnp.exp(heights), shape[position] // parts).reshape((-1,) + (1,) * (len(shape) - position - 1))

    loudness = one(*split[0])
    for cut in split[1:]:
        loudness = loudness * one(*cut)
    return loudness


def normal_values(stream_key, extent, scale, most, split=(), dtype=jnp.bfloat16):
    factor_of = shard_levels(stream_key, extent, split, -0.22, 0.18) if split else 1.0
    entries = jax.random.normal(stream_key, extent, jnp.float32) * scale * factor_of
    return jnp.minimum(jnp.maximum(entries, -most), most).astype(dtype)


def heavy_noise(rng, shape, scale, reach, pieces, heavy, held_as=jnp.bfloat16):
    drawn = scale * jax.random.normal(rng, shape, jnp.float32)
    if pieces:
        drawn = drawn * shard_levels(rng, shape, pieces, -0.22, 0.18)
    return jnp.clip(spiked(drawn, jax.random.fold_in(rng, 3), *heavy), -reach, reach).astype(held_as)


def setup_inputs(seed: int = 0) -> dict:
    splits = jax.random.split(jax.random.key(seed), 6)
    return {
        "inputs": normal_values(splits[0], (D, SEQ), 1.0, 6.0, ((0, 16), (1, 16))),
        "gates": normal_values(splits[1], (D, SEQ), 1.0, 6.0, ((0, 16), (1, 16))),
        "filters": normal_values(splits[2], (D, SEQ), 1.0, 6.0, ((0, 16), (1, 16))),
        "out_grad": heavy_noise(splits[3], (D, SEQ), 1.0, 6.0, ((0, 16), (1, 16)), (1, 0, 16, 2.0)),
        "out_weight": normal_values(splits[4], (D, D), D ** -0.5, 0.09375, ((0, 16), (1, 16))),
    }


def per_channels(operands):
    inputs_blk, gates_blk, filters_blk, slope_blk = operands
    span = 2 * SEQ
    factor = SEQ ** -0.5
    input_spec = jnp.fft.rfft(inputs_blk.astype(jnp.float32), n=span, axis=1)
    filter_spec = jnp.fft.rfft(filters_blk.astype(jnp.float32), n=span, axis=1)
    mixed = (jnp.fft.irfft(input_spec * filter_spec, n=span, axis=1)[:, :SEQ] * factor).astype(jnp.bfloat16)
    mixed_f = mixed.astype(jnp.float32)
    gates_f = gates_blk.astype(jnp.float32)
    slope_f = slope_blk.astype(jnp.float32)
    gated_out = (gates_f * mixed_f).astype(jnp.bfloat16)
    gate_grad = (slope_f * mixed_f).astype(jnp.bfloat16)
    product = (slope_f * gates_f).astype(jnp.bfloat16)
    product_spec = jnp.fft.rfft(product.astype(jnp.float32), n=span, axis=1)
    input_grad = (jnp.fft.irfft(product_spec * jnp.conj(filter_spec), n=span, axis=1)[:, :SEQ] * factor).astype(jnp.bfloat16)
    filter_grad = (jnp.fft.irfft(product_spec * jnp.conj(input_spec), n=span, axis=1)[:, :SEQ] * factor).astype(jnp.bfloat16)
    return gated_out, gate_grad, input_grad, filter_grad


def reference(inputs, gates, filters, out_grad, out_weight):
    slope = jnp.dot(out_weight.T, out_grad, preferred_element_type=jnp.float32).astype(jnp.bfloat16)
    group = min(256, D)
    stacked = lax.map(per_channels, tuple(arr.reshape(D // group, group, SEQ) for arr in (inputs, gates, filters, slope)))
    gated_out, gate_grad, input_grad, filter_grad = (arr.reshape(D, SEQ) for arr in stacked)
    weight_grad = (jnp.dot(out_grad, gated_out.T, preferred_element_type=jnp.float32) * (SEQ ** -0.5)).astype(jnp.bfloat16)
    return input_grad, gate_grad, filter_grad, weight_grad
```

```python
import functools

import jax
import jax.numpy as jnp
import ml_dtypes
import numpy as np
from jax import lax
from jax.experimental import pallas as pl
from jax.experimental.pallas import tpu as pltpu
from jax.sharding import PartitionSpec as P

CH = 256
TOK = 512
FEW = 16
SEQ = 8192
ROWS = 64
LANES = 128
GROUP = 4
BF = jnp.bfloat16
F32 = jnp.float32


def shift_pairs(stride, size, by):
    pairs = []
    for i in range(16):
        at = (i // stride) % size
        pairs.append((i, i + ((at + by) % size - at) * stride))
    return pairs


def send(value, axis, stride, size, by):
    return lax.ppermute(value, axis, shift_pairs(stride, size, by))


def split_hi_lo(matrix):
    hi = matrix.astype(ml_dtypes.bfloat16)
    lo = (matrix - hi.astype(np.float64)).astype(ml_dtypes.bfloat16)
    return hi, lo


@functools.cache
def constants():
    n1 = np.arange(ROWS)
    k1 = np.arange(ROWS)
    n2 = np.arange(LANES)
    k2 = np.arange(LANES)
    first = np.exp(-2j * np.pi * np.outer(k1 + 0.25, n1) / ROWS)
    turn = np.exp(-2j * np.pi * np.outer(k1 + 0.25, n2) / SEQ)
    second = np.exp(-2j * np.pi * np.outer(n2, k2) / LANES)
    lhs = np.concatenate([first.real, first.imag], axis=0)
    hi, lo = split_hi_lo(lhs)
    first_c = np.concatenate([hi, lo], axis=1)

    def square(m):
        full = np.block([[m.real, m.imag], [-m.imag, m.real]])
        hi, lo = split_hi_lo(full)
        return np.concatenate([hi, hi, lo], axis=0)

    second_c = square(second)
    back_c = square(np.conj(second))
    scale = SEQ**-0.5 / SEQ
    last = np.conj(first).T * scale
    hi, lo = split_hi_lo(np.concatenate([last.real, -last.imag], axis=1))
    last_c = np.concatenate([hi, lo, hi], axis=1)
    turn_c = np.stack([turn.real, turn.imag]).astype(np.float32)
    return first_c, second_c, back_c, last_c, turn_c


def hi_lo(value):
    hi = value.astype(BF)
    lo = (value - hi.astype(F32)).astype(BF)
    return hi, lo


def dot(a, b):
    return jnp.dot(a, b, preferred_element_type=F32)


def spread(load, rows_ref):
    for s in range(16):
        block = load(s).astype(F32)
        for q in range(4):
            rows_ref[pl.ds((4 * s + q) * FEW, FEW), :] = block[:, q * LANES : (q + 1) * LANES]


def collect(rows_ref, store):
    for s in range(16):
        parts = [rows_ref[pl.ds((4 * s + q) * FEW, FEW), :] for q in range(4)]
        store(s, jnp.concatenate(parts, axis=1).astype(BF))


def forward_group(rows_ref, base, first_ref, second_ref, turn_ref):
    turn_re = turn_ref[0]
    turn_im = turn_ref[1]
    pieces = []
    for c in range(0, GROUP, 2):
        pair = [rows_ref[pl.ds(base + c + i, ROWS, stride=FEW), :].astype(BF) for i in range(2)]
        both = jnp.concatenate(pair, axis=1)
        out = dot(first_ref[...], jnp.concatenate([both, both], axis=0))
        for i in range(2):
            re = out[:ROWS, i * LANES : (i + 1) * LANES]
            im = out[ROWS:, i * LANES : (i + 1) * LANES]
            pieces.append(
                jnp.concatenate([re * turn_re - im * turn_im, re * turn_im + im * turn_re], axis=1)
            )
    hi, lo = hi_lo(jnp.concatenate(pieces, axis=0))
    spec = dot(jnp.concatenate([hi, lo, hi], axis=1), second_ref[...])
    return spec[:, :LANES], spec[:, LANES:]


def inverse_group(re, im, base, rows_ref, back_ref, last_ref, turn_ref):
    turn_re = turn_ref[0]
    turn_im = turn_ref[1]
    hi, lo = hi_lo(jnp.concatenate([re, im], axis=1))
    out = dot(jnp.concatenate([hi, lo, hi], axis=1), back_ref[...])
    for c in range(0, GROUP, 2):
        cols = []
        for i in range(2):
            d = out[(c + i) * ROWS : (c + i + 1) * ROWS]
            d_re, d_im = d[:, :LANES], d[:, LANES:]
            cols.append(
                jnp.concatenate([d_re * turn_re + d_im * turn_im, d_im * turn_re - d_re * turn_im], axis=0)
            )
        hi, lo = hi_lo(jnp.concatenate(cols, axis=1))
        time = dot(last_ref[...], jnp.concatenate([hi, hi, lo], axis=0))
        for i in range(2):
            rows_ref[pl.ds(base + c + i, ROWS, stride=FEW), :] = time[:, i * LANES : (i + 1) * LANES]


def conv_kernel(xf_ref, first_ref, second_ref, back_ref, last_ref, turn_ref, mixed_ref, spec_ref, x_rows, f_rows, m_rows):
    spread(lambda s: xf_ref[s, :FEW], x_rows)
    spread(lambda s: xf_ref[s, FEW:], f_rows)
    for base in range(0, FEW, GROUP):
        x_re, x_im = forward_group(x_rows, base, first_ref, second_ref, turn_ref)
        f_re, f_im = forward_group(f_rows, base, first_ref, second_ref, turn_ref)
        here = pl.ds(base * ROWS, GROUP * ROWS)
        spec_ref[0, here, :] = x_re
        spec_ref[1, here, :] = x_im
        spec_ref[2, here, :] = f_re
        spec_ref[3, here, :] = f_im
        inverse_group(
            x_re * f_re - x_im * f_im, x_re * f_im + x_im * f_re, base, m_rows, back_ref, last_ref, turn_ref
        )

    def store(s, value):
        mixed_ref[s] = value

    collect(m_rows, store)


def grads_kernel(p_ref, spec_ref, first_ref, second_ref, back_ref, last_ref, turn_ref, out_ref, p_rows, i_rows, f_rows):
    spread(lambda s: p_ref[s], p_rows)
    for base in range(0, FEW, GROUP):
        p_re, p_im = forward_group(p_rows, base, first_ref, second_ref, turn_ref)
        here = pl.ds(base * ROWS, GROUP * ROWS)
        for slot, rows in ((2, i_rows), (0, f_rows)):
            o_re = spec_ref[slot, here, :]
            o_im = spec_ref[slot + 1, here, :]
            inverse_group(
                p_re * o_re + p_im * o_im, p_im * o_re - p_re * o_im, base, rows, back_ref, last_ref, turn_ref
            )

    def store_at(first):
        def store(s, value):
            out_ref[s, first : first + FEW] = value

        return store

    collect(i_rows, store_at(0))
    collect(f_rows, store_at(FEW))


def params(mib):
    return pltpu.CompilerParams(vmem_limit_bytes=mib << 20)


def whole_vmem():
    return pl.BlockSpec(memory_space=pltpu.VMEM)


ROWS_SCRATCH = pltpu.VMEM((ROWS * FEW, LANES), F32)


def transform_cost(count, moved):
    return pl.CostEstimate(flops=count * 3 * 10**8, bytes_accessed=moved, transcendentals=0)


def conv_call(xf):
    consts = constants()
    return pl.pallas_call(
        conv_kernel,
        out_shape=(
            jax.ShapeDtypeStruct((16, FEW, TOK), BF),
            jax.ShapeDtypeStruct((4, FEW * ROWS, LANES), F32),
        ),
        in_specs=[whole_vmem()] * 6,
        out_specs=(whole_vmem(), whole_vmem()),
        scratch_shapes=[ROWS_SCRATCH] * 3,
        compiler_params=params(32),
        cost_estimate=transform_cost(3, 4 << 20),
        name="conv",
    )(xf, *consts)


def grads_call(product, spec):
    consts = constants()
    return pl.pallas_call(
        grads_kernel,
        out_shape=jax.ShapeDtypeStruct((16, 2 * FEW, TOK), BF),
        in_specs=[whole_vmem()] * 7,
        out_specs=whole_vmem(),
        scratch_shapes=[ROWS_SCRATCH] * 3,
        compiler_params=params(32),
        cost_estimate=transform_cost(3, 4 << 20),
        name="grads",
    )(product, spec, *consts)


def place_of(where_ref, dy, dz):
    x, zh, core, y, zl = (where_ref[i] for i in range(5))
    y_from = jnp.bitwise_and(y + 4 - dy, 3)
    zl_from = jnp.bitwise_and(zl + 4 - dz, 3)
    zh_from = jnp.right_shift(zl_from, 1)
    core_from = jnp.bitwise_and(zl_from, 1)
    return jnp.bitwise_xor(core, core_from), (x, y_from), jnp.bitwise_xor(zh, zh_from)


def grad_blocks(refs):
    for dy in range(4):
        own, rest = refs[2 * dy], refs[2 * dy + 1]
        for dz in range(4):
            yield dy, dz, (own[...] if dz == 0 else rest[dz - 1])


def slope_kernel(where_ref, *refs):
    grads = refs[:8]
    w_same, w_other, gates_ref, slope_ref, product_ref = refs[8:]
    total = None
    for dy, dz, block in grad_blocks(grads):
        other, (x, x_from), dzh = place_of(where_ref, dy, dz)
        slot = jnp.bitwise_and(x + 4 - x_from, 3) * 2 + dzh
        weight = jnp.where(other == 0, w_same[slot], w_other[slot])
        part = dot(weight, block)
        total = part if total is None else total + part
    slope = total.astype(BF)
    slope_ref[...] = slope
    product_ref[...] = (slope.astype(F32) * gates_ref[...].astype(F32)).astype(BF)


def weight_kernel(where_ref, *refs):
    grads = refs[:8]
    gates_ref, mixed_ref, slope_ref, gate_grad_ref, out_ref = refs[8:]
    mixed = mixed_ref[...].astype(F32)
    gated = (gates_ref[...].astype(F32) * mixed).astype(BF)
    gate_grad_ref[...] = (slope_ref[...].astype(F32) * mixed).astype(BF)
    for dy, dz, block in grad_blocks(grads):
        other, (x, x_to), dzh = place_of(where_ref, dy, dz)
        slot = jnp.bitwise_and(x_to + 4 - x, 3) * 2 + dzh
        part = lax.dot_general(block, gated, (((1,), (1,)), ((), ())), preferred_element_type=F32)
        out_ref[other, slot] = (part * (SEQ**-0.5)).astype(BF)


def matmul_cost(moved):
    return pl.CostEstimate(flops=2 * CH * TOK * 4096, bytes_accessed=moved, transcendentals=0)


def slope_call(where, grads, w_same, w_other, gates):
    shape = jax.ShapeDtypeStruct((CH, TOK), BF)
    return pl.pallas_call(
        slope_kernel,
        out_shape=(shape, shape),
        in_specs=[pl.BlockSpec(memory_space=pltpu.SMEM)] + [whole_vmem()] * 11,
        out_specs=(whole_vmem(), whole_vmem()),
        compiler_params=params(32),
        cost_estimate=matmul_cost(7 << 20),
        name="slope",
    )(where, *grads, w_same, w_other, gates)


def weight_call(where, grads, gates, mixed, slope):
    return pl.pallas_call(
        weight_kernel,
        out_shape=(
            jax.ShapeDtypeStruct((CH, TOK), BF),
            jax.ShapeDtypeStruct((2, 8, 256, 256), BF),
        ),
        in_specs=[pl.BlockSpec(memory_space=pltpu.SMEM)] + [whole_vmem()] * 11,
        out_specs=(whole_vmem(), whole_vmem()),
        compiler_params=params(32),
        cost_estimate=matmul_cost(7 << 20),
        name="weight",
    )(where, *grads, gates, mixed, slope)


def exchange(value):
    return lax.all_to_all(value, "ctx", split_axis=0, concat_axis=0, tiled=True)


def add(*parts):
    total = parts[0].astype(F32)
    for part in parts[1:]:
        total = total + part.astype(F32)
    return total.astype(BF)


def on_device(inputs, gates, filters, out_grad, out_weight):
    ctx = lax.axis_index("ctx")
    tp = lax.axis_index("tp")
    where = jnp.stack([ctx // 4, (ctx // 2) % 2, ctx % 2, tp // 4, tp % 4]).astype(jnp.int32)

    own = [send(out_grad, "tp", 4, 4, dy) for dy in (1, 2, 3)]
    rest = jnp.stack([send(out_grad, "tp", 1, 4, dz) for dz in (1, 2, 3)])
    rests = [send(rest, "tp", 4, 4, dy) for dy in (1, 2, 3)]
    grads = [out_grad, rest]
    for o, r in zip(own, rests):
        grads += [o, r]

    w_own = out_weight.T
    w_pair = jnp.stack([w_own, send(w_own, "ctx", 2, 2, 1)])
    w_same = jnp.concatenate([w_pair] + [send(w_pair, "ctx", 4, 4, dx) for dx in (1, 2, 3)])
    w_other = send(w_same, "ctx", 1, 2, 1)

    both = jnp.concatenate([inputs.reshape(16, FEW, TOK), filters.reshape(16, FEW, TOK)], axis=1)
    mixed_rows, spec = conv_call(exchange(both))
    mixed = exchange(mixed_rows).reshape(CH, TOK)

    slope, product = slope_call(where, grads, w_same, w_other, gates)
    grad_rows = grads_call(exchange(product.reshape(16, FEW, TOK)), spec)
    gate_grad, partial = weight_call(where, grads, gates, mixed, slope)
    both_grads = exchange(grad_rows)
    input_grad = both_grads[:, :FEW].reshape(CH, TOK)
    filter_grad = both_grads[:, FEW:].reshape(CH, TOK)

    chip = add(partial[0], send(partial[1], "ctx", 1, 2, 1)).reshape(4, 2, 256, 256)
    line = add(chip[0], *[send(chip[dx], "ctx", 4, 4, dx) for dx in (1, 2, 3)])
    weight_grad = add(line[0], send(line[1], "ctx", 2, 2, 1))
    return (input_grad, gate_grad, filter_grad, weight_grad)


def solution(mesh):
    in_specs = (P("tp", "ctx"), P("tp", "ctx"), P("tp", "ctx"), P("tp", "ctx"), P("ctx", "tp"))
    out_specs = (P("tp", "ctx"), P("tp", "ctx"), P("tp", "ctx"), P("ctx", "tp"))
    return jax.shard_map(
        on_device, mesh=mesh, in_specs=in_specs, out_specs=out_specs, check_vma=False
    )
```

```python
import functools

import jax
import jax.numpy as jnp
import ml_dtypes
import numpy as np
from jax import lax
from jax.experimental import pallas as pl
from jax.experimental.pallas import tpu as pltpu
from jax.sharding import PartitionSpec as P

CH = 256
TOK = 512
FEW = 16
SEQ = 8192
ROWS = 64
LANES = 128
GROUP = 4
BF = jnp.bfloat16
F32 = jnp.float32


def shift_pairs(stride, size, by):
    pairs = []
    for i in range(16):
        at = (i // stride) % size
        pairs.append((i, i + ((at + by) % size - at) * stride))
    return pairs


def send(value, axis, stride, size, by):
    return lax.ppermute(value, axis, shift_pairs(stride, size, by))


LINES_X = [[4 * x + i for x in range(4)] for i in range(4)]


def split_hi_lo(matrix):
    hi = matrix.astype(ml_dtypes.bfloat16)
    lo = (matrix - hi.astype(np.float64)).astype(ml_dtypes.bfloat16)
    return hi, lo


@functools.cache
def constants():
    n1 = np.arange(ROWS)
    k1 = np.arange(ROWS)
    n2 = np.arange(LANES)
    k2 = np.arange(LANES)
    first = np.exp(-2j * np.pi * np.outer(k1 + 0.25, n1) / ROWS)
    turn = np.exp(-2j * np.pi * np.outer(k1 + 0.25, n2) / SEQ)
    second = np.exp(-2j * np.pi * np.outer(n2, k2) / LANES)
    lhs = np.concatenate([first.real, first.imag], axis=0)
    hi, lo = split_hi_lo(lhs)
    first_c = np.concatenate([hi, lo], axis=1)

    def square(m):
        full = np.block([[m.real, m.imag], [-m.imag, m.real]])
        hi, lo = split_hi_lo(full)
        return np.concatenate([hi, hi, lo], axis=0)

    second_c = square(second)
    back_c = square(np.conj(second))
    scale = SEQ**-0.5 / SEQ
    last = np.conj(first).T * scale
    hi, lo = split_hi_lo(np.concatenate([last.real, -last.imag], axis=1))
    last_c = np.concatenate([hi, lo, hi], axis=1)
    turn_c = np.stack([turn.real, turn.imag]).astype(np.float32)
    return first_c, second_c, back_c, last_c, turn_c


def hi_lo(value):
    hi = value.astype(BF)
    lo = (value - hi.astype(F32)).astype(BF)
    return hi, lo


def dot(a, b):
    return jnp.dot(a, b, preferred_element_type=F32)


def spread(load, rows_ref):
    for s in range(16):
        block = load(s).astype(F32)
        for q in range(4):
            rows_ref[pl.ds((4 * s + q) * FEW, FEW), :] = block[:, q * LANES : (q + 1) * LANES]


def collect(rows_ref, store):
    for s in range(16):
        parts = [rows_ref[pl.ds((4 * s + q) * FEW, FEW), :] for q in range(4)]
        store(s, jnp.concatenate(parts, axis=1).astype(BF))


def forward_group(rows_ref, base, first_ref, second_ref, turn_ref):
    turn_re = turn_ref[0]
    turn_im = turn_ref[1]
    pieces = []
    for c in range(0, GROUP, 2):
        pair = [rows_ref[pl.ds(base + c + i, ROWS, stride=FEW), :].astype(BF) for i in range(2)]
        both = jnp.concatenate(pair, axis=1)
        out = dot(first_ref[...], jnp.concatenate([both, both], axis=0))
        for i in range(2):
            re = out[:ROWS, i * LANES : (i + 1) * LANES]
            im = out[ROWS:, i * LANES : (i + 1) * LANES]
            pieces.append(
                jnp.concatenate([re * turn_re - im * turn_im, re * turn_im + im * turn_re], axis=1)
            )
    hi, lo = hi_lo(jnp.concatenate(pieces, axis=0))
    spec = dot(jnp.concatenate([hi, lo, hi], axis=1), second_ref[...])
    return spec[:, :LANES], spec[:, LANES:]


def inverse_group(re, im, base, rows_ref, back_ref, last_ref, turn_ref):
    turn_re = turn_ref[0]
    turn_im = turn_ref[1]
    hi, lo = hi_lo(jnp.concatenate([re, im], axis=1))
    out = dot(jnp.concatenate([hi, lo, hi], axis=1), back_ref[...])
    for c in range(0, GROUP, 2):
        cols = []
        for i in range(2):
            d = out[(c + i) * ROWS : (c + i + 1) * ROWS]
            d_re, d_im = d[:, :LANES], d[:, LANES:]
            cols.append(
                jnp.concatenate([d_re * turn_re + d_im * turn_im, d_im * turn_re - d_re * turn_im], axis=0)
            )
        hi, lo = hi_lo(jnp.concatenate(cols, axis=1))
        time = dot(last_ref[...], jnp.concatenate([hi, hi, lo], axis=0))
        for i in range(2):
            rows_ref[pl.ds(base + c + i, ROWS, stride=FEW), :] = time[:, i * LANES : (i + 1) * LANES]


CONSTS = 5


def fetch(sources, targets, sems):
    copies = [pltpu.make_async_copy(src, dst, sems.at[i]) for i, (src, dst) in enumerate(zip(sources, targets))]
    for copy in copies:
        copy.start()
    return copies


def conv_kernel(xf_ref, *refs):
    hbm, (mixed_out, spec_out) = refs[:CONSTS], refs[CONSTS : CONSTS + 2]
    consts, (mixed_ref, spec_ref, x_rows, f_rows, m_rows, sems, mixed_sem, spec_sems) = (
        refs[CONSTS + 2 : 2 * CONSTS + 2],
        refs[2 * CONSTS + 2 :],
    )
    first_ref, second_ref, back_ref, last_ref, turn_ref = consts
    copies = fetch(hbm, consts, sems)
    spread(lambda s: xf_ref[s, :FEW], x_rows)
    spread(lambda s: xf_ref[s, FEW:], f_rows)
    for copy in copies:
        copy.wait()
    outs = []
    for base in range(0, FEW, GROUP):
        x_re, x_im = forward_group(x_rows, base, first_ref, second_ref, turn_ref)
        f_re, f_im = forward_group(f_rows, base, first_ref, second_ref, turn_ref)
        here = pl.ds(base * ROWS, GROUP * ROWS)
        spec_ref[0, here, :] = x_re
        spec_ref[1, here, :] = x_im
        spec_ref[2, here, :] = f_re
        spec_ref[3, here, :] = f_im
        out = pltpu.make_async_copy(spec_ref.at[:, here, :], spec_out.at[:, here, :], spec_sems.at[base // GROUP])
        out.start()
        outs.append(out)
        inverse_group(
            x_re * f_re - x_im * f_im, x_re * f_im + x_im * f_re, base, m_rows, back_ref, last_ref, turn_ref
        )

    def store(s, value):
        mixed_ref[s] = value

    collect(m_rows, store)
    out = pltpu.make_async_copy(mixed_ref, mixed_out, mixed_sem)
    out.start()
    outs.append(out)
    for out in outs:
        out.wait()


def grads_kernel(p_ref, *refs):
    hbm, out_hbm = refs[: CONSTS + 1], refs[CONSTS + 1]
    held, (out_ref, p_rows, i_rows, f_rows, sems, out_sem) = refs[CONSTS + 2 : 2 * CONSTS + 3], refs[2 * CONSTS + 3 :]
    first_ref, second_ref, back_ref, last_ref, turn_ref, spec_ref = held
    copies = fetch(hbm, held, sems)
    spread(lambda s: p_ref[s], p_rows)
    for copy in copies:
        copy.wait()
    for base in range(0, FEW, GROUP):
        p_re, p_im = forward_group(p_rows, base, first_ref, second_ref, turn_ref)
        here = pl.ds(base * ROWS, GROUP * ROWS)
        for slot, rows in ((2, i_rows), (0, f_rows)):
            o_re = spec_ref[slot, here, :]
            o_im = spec_ref[slot + 1, here, :]
            inverse_group(
                p_re * o_re + p_im * o_im, p_im * o_re - p_re * o_im, base, rows, back_ref, last_ref, turn_ref
            )

    def store_at(first):
        def store(s, value):
            out_ref[s, first : first + FEW] = value

        return store

    collect(i_rows, store_at(0))
    collect(f_rows, store_at(FEW))
    out = pltpu.make_async_copy(out_ref, out_hbm, out_sem)
    out.start()
    out.wait()


def params(mib):
    return pltpu.CompilerParams(vmem_limit_bytes=mib << 20)


def whole_vmem():
    return pl.BlockSpec(memory_space=pltpu.VMEM)


def in_hbm():
    return pl.BlockSpec(memory_space=pltpu.HBM)


ROWS_SCRATCH = pltpu.VMEM((ROWS * FEW, LANES), F32)
SPEC_SHAPE = (4, FEW * ROWS, LANES)
DMA = pltpu.SemaphoreType.DMA


def const_scratch():
    return [pltpu.VMEM(c.shape, c.dtype) for c in constants()]


def conv_call(xf):
    return pl.pallas_call(
        conv_kernel,
        out_shape=(jax.ShapeDtypeStruct((16, FEW, TOK), BF), jax.ShapeDtypeStruct(SPEC_SHAPE, F32)),
        in_specs=[whole_vmem()] + [in_hbm()] * CONSTS,
        out_specs=(in_hbm(), in_hbm()),
        scratch_shapes=const_scratch()
        + [pltpu.VMEM((16, FEW, TOK), BF), pltpu.VMEM(SPEC_SHAPE, F32)]
        + [ROWS_SCRATCH] * 3
        + [DMA((CONSTS,)), DMA, DMA((FEW // GROUP,))],
        compiler_params=params(60),
        cost_estimate=pl.CostEstimate(flops=10**9, bytes_accessed=4 << 20, transcendentals=0),
        name="conv",
    )(xf, *constants())


def grads_call(product, spec):
    return pl.pallas_call(
        grads_kernel,
        out_shape=jax.ShapeDtypeStruct((16, 2 * FEW, TOK), BF),
        in_specs=[whole_vmem()] + [in_hbm()] * (CONSTS + 1),
        out_specs=in_hbm(),
        scratch_shapes=const_scratch()
        + [pltpu.VMEM(SPEC_SHAPE, F32), pltpu.VMEM((16, 2 * FEW, TOK), BF)]
        + [ROWS_SCRATCH] * 3
        + [DMA((CONSTS + 1,)), DMA],
        compiler_params=params(57),
        cost_estimate=pl.CostEstimate(flops=4 * 10**10, bytes_accessed=4 << 20, transcendentals=0),
        name="grads",
    )(product, *constants(), spec)


def place_of(where_ref, dy, dz):
    x, zh, core, y, zl = (where_ref[i] for i in range(5))
    y_from = jnp.bitwise_and(y + 4 - dy, 3)
    zl_from = jnp.bitwise_and(zl + 4 - dz, 3)
    zh_from = jnp.right_shift(zl_from, 1)
    core_from = jnp.bitwise_and(zl_from, 1)
    return jnp.bitwise_xor(core, core_from), (x, y_from), jnp.bitwise_xor(zh, zh_from)


def fetch_grads(grads, held, sems):
    copies = []
    for dy in range(4):
        for part, target in enumerate((held.at[4 * dy], held.at[pl.ds(4 * dy + 1, 3)])):
            copies.append(pltpu.make_async_copy(grads[2 * dy + part], target, sems.at[2 * dy + part]))
    for copy in copies:
        copy.start()
    return copies


def slots(copies):
    for dy in range(4):
        for dz in range(4):
            if dz < 2:
                copies[2 * dy + dz].wait()
            yield dy, dz, 4 * dy + dz


def slope_kernel(where_ref, *refs):
    grads, ins_hbm, (slope_hbm, product_hbm) = refs[:8], refs[8:13], refs[13:15]
    held, weights, gates_ref, slope_ref, product_ref, grad_sems, sems = refs[15:]
    ins = fetch(ins_hbm, [weights.at[pl.ds(4 * i, 4)] for i in range(4)] + [gates_ref], sems)
    copies = fetch_grads(grads, held, grad_sems)
    for copy in ins[:4]:
        copy.wait()
    total = None
    for dy, dz, at in slots(copies):
        other, (_, x_from), dzh = place_of(where_ref, dy, dz)
        slot = other * 8 + dzh * 4 + x_from
        part = dot(weights[slot], held[at])
        total = part if total is None else total + part
    slope = total.astype(BF)
    slope_ref[...] = slope
    ins[4].wait()
    product_ref[...] = (slope.astype(F32) * gates_ref[...].astype(F32)).astype(BF)
    outs = [
        pltpu.make_async_copy(product_ref, product_hbm, sems.at[5]),
        pltpu.make_async_copy(slope_ref, slope_hbm, sems.at[6]),
    ]
    for out in outs:
        out.start()
    for out in outs:
        out.wait()


def weight_kernel(where_ref, *refs):
    grads, ins_hbm, outs_hbm = refs[:8], refs[8:11], refs[11:14]
    held, gates_ref, mixed_ref, slope_ref, gate_grad_ref, sums, grad_sems, sems = refs[14:]
    ins = fetch(ins_hbm, (gates_ref, mixed_ref, slope_ref), sems)
    copies = fetch_grads(grads, held, grad_sems)
    for copy in ins:
        copy.wait()
    mixed = mixed_ref[...].astype(F32)
    gated = (gates_ref[...].astype(F32) * mixed).astype(BF)
    gate_grad_ref[...] = (slope_ref[...].astype(F32) * mixed).astype(BF)
    for dy, dz, at in slots(copies):
        other, (x, x_to), dzh = place_of(where_ref, dy, dz)
        slot = other * 8 + jnp.bitwise_and(x_to + 4 - x, 3) * 2 + dzh
        part = lax.dot_general(held[at], gated, (((1,), (1,)), ((), ())), preferred_element_type=F32)
        sums[slot] = (part * (SEQ**-0.5)).astype(BF)
    sources = (gate_grad_ref, sums.at[:8], sums.at[8:])
    outs = [pltpu.make_async_copy(src, dst, sems.at[3 + i]) for i, (src, dst) in enumerate(zip(sources, outs_hbm))]
    for out in outs:
        out.start()
    for out in outs:
        out.wait()


HELD = pltpu.VMEM((16, CH, TOK), BF)
SQUARES = pltpu.VMEM((16, 256, 256), BF)
TILE = pltpu.VMEM((CH, TOK), BF)


def matmul_cost():
    return pl.CostEstimate(flops=2 * CH * TOK * 4096, bytes_accessed=7 << 20, transcendentals=0)


def slope_call(where, grads, weights, gates):
    shape = jax.ShapeDtypeStruct((CH, TOK), BF)
    return pl.pallas_call(
        slope_kernel,
        out_shape=(shape, shape),
        in_specs=[pl.BlockSpec(memory_space=pltpu.SMEM)] + [in_hbm()] * 13,
        out_specs=(in_hbm(),) * 2,
        scratch_shapes=[HELD, SQUARES, TILE, TILE, TILE, DMA((8,)), DMA((7,))],
        compiler_params=params(57),
        cost_estimate=matmul_cost(),
        name="slope",
    )(where, *grads, *weights, gates)


def weight_call(where, grads, gates, mixed, slope):
    eight = jax.ShapeDtypeStruct((8, 256, 256), BF)
    return pl.pallas_call(
        weight_kernel,
        out_shape=(jax.ShapeDtypeStruct((CH, TOK), BF), eight, eight),
        in_specs=[pl.BlockSpec(memory_space=pltpu.SMEM)] + [in_hbm()] * 11,
        out_specs=(in_hbm(),) * 3,
        scratch_shapes=[HELD, TILE, TILE, TILE, TILE, SQUARES, DMA((8,)), DMA((6,))],
        compiler_params=params(57),
        cost_estimate=matmul_cost(),
        name="weight",
    )(where, *grads, gates, mixed, slope)


def exchange(value):
    return lax.all_to_all(value, "ctx", split_axis=0, concat_axis=0, tiled=True)


def add(*parts):
    total = parts[0].astype(F32)
    for part in parts[1:]:
        total = total + part.astype(F32)
    return total.astype(BF)


def on_device(inputs, gates, filters, out_grad, out_weight):
    ctx = lax.axis_index("ctx")
    tp = lax.axis_index("tp")
    where = jnp.stack([ctx // 4, (ctx // 2) % 2, ctx % 2, tp // 4, tp % 4]).astype(jnp.int32)

    w_line = lax.all_gather(out_weight.T, "ctx", axis_index_groups=LINES_X)

    rest = jnp.stack([send(out_grad, "tp", 1, 4, dz) for dz in (1, 2, 3)])
    up, down = send(out_grad, "tp", 4, 4, 1), send(out_grad, "tp", 4, 4, 3)
    up, w_line, own = lax.optimization_barrier((up, w_line, out_grad))
    near = [up, send(own, "tp", 4, 4, 2), down]
    rest, near, w_line, inputs, filters = lax.optimization_barrier((rest, near, w_line, inputs, filters))
    rests = [send(rest, "tp", 4, 4, dy) for dy in (1, 2, 3)]
    grads = [out_grad, rest]
    for n, r in zip(near, rests):
        grads += [n, r]

    w_far = send(w_line, "ctx", 2, 2, 1)
    weights = [w_line, w_far, send(w_line, "ctx", 1, 2, 1), send(w_far, "ctx", 1, 2, 1)]

    both = jnp.concatenate([inputs.reshape(16, FEW, TOK), filters.reshape(16, FEW, TOK)], axis=1)
    mixed_rows, spec = conv_call(exchange(both))
    mixed = exchange(mixed_rows).reshape(CH, TOK)

    slope, product = slope_call(where, grads, weights, gates)
    product_rows = exchange(product.reshape(16, FEW, TOK))
    gate_grad, part_same, part_other = weight_call(where, grads, gates, mixed, slope)
    product_rows, part_same = lax.optimization_barrier((product_rows, part_same))
    chip = add(part_same, send(part_other, "ctx", 1, 2, 1)).reshape(4, 2, 256, 256)
    grad_rows = grads_call(product_rows, spec)
    both_grads = exchange(grad_rows)
    input_grad = both_grads[:, :FEW].reshape(CH, TOK)
    filter_grad = both_grads[:, FEW:].reshape(CH, TOK)

    line = add(chip[0], *[send(chip[dx], "ctx", 4, 4, dx) for dx in (1, 2, 3)])
    weight_grad = add(line[0], send(line[1], "ctx", 2, 2, 1))
    return (input_grad, gate_grad, filter_grad, weight_grad)


def solution(mesh):
    in_specs = (P("tp", "ctx"), P("tp", "ctx"), P("tp", "ctx"), P("tp", "ctx"), P("ctx", "tp"))
    out_specs = (P("tp", "ctx"), P("tp", "ctx"), P("tp", "ctx"), P("ctx", "tp"))
    return jax.shard_map(
        on_device, mesh=mesh, in_specs=in_specs, out_specs=out_specs, check_vma=False
    )
```

```python
import functools

import jax
import jax.numpy as jnp
import ml_dtypes
import numpy as np
from jax import lax
from jax.experimental import pallas as pl
from jax.experimental.pallas import tpu as pltpu
from jax.sharding import PartitionSpec as P

CH = 256
TOK = 512
FEW = 16
SEQ = 8192
ROWS = 64
LANES = 128
GROUP = 4
BF = jnp.bfloat16
F32 = jnp.float32


def shift_pairs(stride, size, by):
    pairs = []
    for i in range(16):
        at = (i // stride) % size
        pairs.append((i, i + ((at + by) % size - at) * stride))
    return pairs


def send(value, axis, stride, size, by):
    return lax.ppermute(value, axis, shift_pairs(stride, size, by))


LINES_X = [[4 * x + i for x in range(4)] for i in range(4)]


def split_hi_lo(matrix):
    hi = matrix.astype(ml_dtypes.bfloat16)
    lo = (matrix - hi.astype(np.float64)).astype(ml_dtypes.bfloat16)
    return hi, lo


@functools.cache
def constants():
    n1 = np.arange(ROWS)
    k1 = np.arange(ROWS)
    n2 = np.arange(LANES)
    k2 = np.arange(LANES)
    first = np.exp(-2j * np.pi * np.outer(k1 + 0.25, n1) / ROWS)
    turn = np.exp(-2j * np.pi * np.outer(k1 + 0.25, n2) / SEQ)
    second = np.exp(-2j * np.pi * np.outer(n2, k2) / LANES)
    lhs = np.concatenate([first.real, first.imag], axis=0)
    hi, lo = split_hi_lo(lhs)
    first_c = np.concatenate([hi, lo], axis=1)

    def square(m):
        full = np.block([[m.real, m.imag], [-m.imag, m.real]])
        hi, lo = split_hi_lo(full)
        return np.concatenate([hi, hi, lo], axis=0)

    second_c = square(second)
    back_c = square(np.conj(second))
    scale = SEQ**-0.5 / SEQ
    last = np.conj(first).T * scale
    hi, lo = split_hi_lo(np.concatenate([last.real, -last.imag], axis=1))
    last_c = np.concatenate([hi, lo, hi], axis=1)
    turn_c = np.stack([turn.real, turn.imag]).astype(np.float32)
    return first_c, second_c, back_c, last_c, turn_c


def hi_lo(value):
    hi = value.astype(BF)
    lo = (value - hi.astype(F32)).astype(BF)
    return hi, lo


def dot(a, b):
    return jnp.dot(a, b, preferred_element_type=F32)


def spread(load, rows_ref):
    for s in range(16):
        block = load(s).astype(F32)
        for q in range(4):
            rows_ref[pl.ds((4 * s + q) * FEW, FEW), :] = block[:, q * LANES : (q + 1) * LANES]


def collect(rows_ref, store):
    for s in range(16):
        parts = [rows_ref[pl.ds((4 * s + q) * FEW, FEW), :] for q in range(4)]
        store(s, jnp.concatenate(parts, axis=1).astype(BF))


def forward_group(rows_ref, base, first_ref, second_ref, turn_ref):
    turn_re = turn_ref[0]
    turn_im = turn_ref[1]
    pieces = []
    for c in range(0, GROUP, 2):
        pair = [rows_ref[pl.ds(base + c + i, ROWS, stride=FEW), :].astype(BF) for i in range(2)]
        both = jnp.concatenate(pair, axis=1)
        out = dot(first_ref[...], jnp.concatenate([both, both], axis=0))
        for i in range(2):
            re = out[:ROWS, i * LANES : (i + 1) * LANES]
            im = out[ROWS:, i * LANES : (i + 1) * LANES]
            pieces.append(
                jnp.concatenate([re * turn_re - im * turn_im, re * turn_im + im * turn_re], axis=1)
            )
    hi, lo = hi_lo(jnp.concatenate(pieces, axis=0))
    spec = dot(jnp.concatenate([hi, lo, hi], axis=1), second_ref[...])
    return spec[:, :LANES], spec[:, LANES:]


def inverse_group(re, im, base, rows_ref, back_ref, last_ref, turn_ref):
    turn_re = turn_ref[0]
    turn_im = turn_ref[1]
    hi, lo = hi_lo(jnp.concatenate([re, im], axis=1))
    out = dot(jnp.concatenate([hi, lo, hi], axis=1), back_ref[...])
    for c in range(0, GROUP, 2):
        cols = []
        for i in range(2):
            d = out[(c + i) * ROWS : (c + i + 1) * ROWS]
            d_re, d_im = d[:, :LANES], d[:, LANES:]
            cols.append(
                jnp.concatenate([d_re * turn_re + d_im * turn_im, d_im * turn_re - d_re * turn_im], axis=0)
            )
        hi, lo = hi_lo(jnp.concatenate(cols, axis=1))
        time = dot(last_ref[...], jnp.concatenate([hi, hi, lo], axis=0))
        for i in range(2):
            rows_ref[pl.ds(base + c + i, ROWS, stride=FEW), :] = time[:, i * LANES : (i + 1) * LANES]


CONSTS = 5


def fetch(sources, targets, sems):
    copies = [pltpu.make_async_copy(src, dst, sems.at[i]) for i, (src, dst) in enumerate(zip(sources, targets))]
    for copy in copies:
        copy.start()
    return copies


def conv_kernel(xf_ref, *refs):
    hbm, (mixed_out, spec_out) = refs[:CONSTS], refs[CONSTS : CONSTS + 2]
    consts, (mixed_ref, spec_ref, x_rows, f_rows, m_rows, sems, mixed_sem, spec_sems) = (
        refs[CONSTS + 2 : 2 * CONSTS + 2],
        refs[2 * CONSTS + 2 :],
    )
    first_ref, second_ref, back_ref, last_ref, turn_ref = consts
    copies = fetch(hbm, consts, sems)
    spread(lambda s: xf_ref[s, :FEW], x_rows)
    spread(lambda s: xf_ref[s, FEW:], f_rows)
    for copy in copies:
        copy.wait()
    outs = []
    for base in range(0, FEW, GROUP):
        x_re, x_im = forward_group(x_rows, base, first_ref, second_ref, turn_ref)
        f_re, f_im = forward_group(f_rows, base, first_ref, second_ref, turn_ref)
        here = pl.ds(base * ROWS, GROUP * ROWS)
        spec_ref[0, here, :] = x_re
        spec_ref[1, here, :] = x_im
        spec_ref[2, here, :] = f_re
        spec_ref[3, here, :] = f_im
        out = pltpu.make_async_copy(spec_ref.at[:, here, :], spec_out.at[:, here, :], spec_sems.at[base // GROUP])
        out.start()
        outs.append(out)
        inverse_group(
            x_re * f_re - x_im * f_im, x_re * f_im + x_im * f_re, base, m_rows, back_ref, last_ref, turn_ref
        )

    def store(s, value):
        mixed_ref[s] = value

    collect(m_rows, store)
    out = pltpu.make_async_copy(mixed_ref, mixed_out, mixed_sem)
    out.start()
    outs.append(out)
    for out in outs:
        out.wait()


def grads_kernel(
    p_ref, first_ref, second_ref, back_ref, last_ref, turn_ref, spec_ref, out_ref, p_rows, i_rows, f_rows
):
    spread(lambda s: p_ref[s], p_rows)
    for base in range(0, FEW, GROUP):
        p_re, p_im = forward_group(p_rows, base, first_ref, second_ref, turn_ref)
        here = pl.ds(base * ROWS, GROUP * ROWS)
        for slot, rows in ((2, i_rows), (0, f_rows)):
            o_re = spec_ref[slot, here, :]
            o_im = spec_ref[slot + 1, here, :]
            inverse_group(
                p_re * o_re + p_im * o_im, p_im * o_re - p_re * o_im, base, rows, back_ref, last_ref, turn_ref
            )

    def store_at(first):
        def store(s, value):
            out_ref[s, first : first + FEW] = value

        return store

    collect(i_rows, store_at(0))
    collect(f_rows, store_at(FEW))


def params(mib):
    return pltpu.CompilerParams(vmem_limit_bytes=mib << 20)


def whole_vmem():
    return pl.BlockSpec(memory_space=pltpu.VMEM)


def in_hbm():
    return pl.BlockSpec(memory_space=pltpu.HBM)


ROWS_SCRATCH = pltpu.VMEM((ROWS * FEW, LANES), F32)
SPEC_SHAPE = (4, FEW * ROWS, LANES)
DMA = pltpu.SemaphoreType.DMA


def const_scratch():
    return [pltpu.VMEM(c.shape, c.dtype) for c in constants()]


def conv_call(xf):
    return pl.pallas_call(
        conv_kernel,
        out_shape=(jax.ShapeDtypeStruct((16, FEW, TOK), BF), jax.ShapeDtypeStruct(SPEC_SHAPE, F32)),
        in_specs=[whole_vmem()] + [in_hbm()] * CONSTS,
        out_specs=(in_hbm(), in_hbm()),
        scratch_shapes=const_scratch()
        + [pltpu.VMEM((16, FEW, TOK), BF), pltpu.VMEM(SPEC_SHAPE, F32)]
        + [ROWS_SCRATCH] * 3
        + [DMA((CONSTS,)), DMA, DMA((FEW // GROUP,))],
        compiler_params=params(60),
        cost_estimate=pl.CostEstimate(flops=10**9, bytes_accessed=4 << 20, transcendentals=0),
        name="conv",
    )(xf, *constants())


def grads_call(product, spec):
    return pl.pallas_call(
        grads_kernel,
        out_shape=jax.ShapeDtypeStruct((16, 2 * FEW, TOK), BF),
        in_specs=[whole_vmem()] * (CONSTS + 2),
        out_specs=whole_vmem(),
        scratch_shapes=[ROWS_SCRATCH] * 3,
        compiler_params=params(24),
        cost_estimate=pl.CostEstimate(flops=10**10, bytes_accessed=4 << 20, transcendentals=0),
        name="grads",
    )(product, *constants(), spec)


def fetch_grads(grads, held, sems):
    copies = []
    for dy in range(4):
        for part, target in enumerate((held.at[4 * dy], held.at[pl.ds(4 * dy + 1, 3)])):
            copies.append(pltpu.make_async_copy(grads[2 * dy + part], target, sems.at[2 * dy + part]))
    for copy in copies:
        copy.start()
    return copies


def weight_slot(where_ref, dy, dz):
    zh, core, y, zl = (where_ref[i] for i in range(1, 5))
    x_from = jnp.bitwise_and(y + 4 - dy, 3)
    zl_from = jnp.bitwise_and(zl + 4 - dz, 3)
    zh_from = jnp.right_shift(zl_from, 1)
    core_from = jnp.bitwise_and(zl_from, 1)
    return jnp.bitwise_xor(core, core_from) * 8 + jnp.bitwise_xor(zh, zh_from) * 4 + x_from


def grad_slot(where_ref, other, dx, dzh):
    x, zh, core, y, zl = (where_ref[i] for i in range(5))
    y_from = jnp.bitwise_and(x + dx, 3)
    zl_from = jnp.bitwise_xor(zh, dzh) * 2 + jnp.bitwise_xor(core, other)
    return jnp.bitwise_and(y + 4 - y_from, 3) * 4 + jnp.bitwise_and(zl + 4 - zl_from, 3)


def products_kernel(where_ref, *refs):
    grads, ins_hbm = refs[:8], refs[8:14]
    product_hbm, gate_grad_hbm, other_hbm, same_hbm = refs[14:18]
    held, weights, gates_ref, mixed_ref, product_ref, gate_grad_ref, sums, grad_sems, sems, out_sems = refs[18:]
    targets = [weights.at[pl.ds(4 * i, 4)] for i in range(4)] + [gates_ref, mixed_ref]
    ins = fetch(ins_hbm, targets, sems)
    copies = fetch_grads(grads, held, grad_sems)
    for copy in ins[:4]:
        copy.wait()
    total = None
    for dy in range(4):
        copies[2 * dy].wait()
        copies[2 * dy + 1].wait()
        weight = jnp.concatenate([weights[weight_slot(where_ref, dy, dz)] for dz in range(4)], axis=1)
        part = dot(weight, held[4 * dy : 4 * dy + 4].reshape(4 * CH, TOK))
        total = part if total is None else total + part
    slope = total.astype(BF).astype(F32)
    ins[4].wait()
    gates = gates_ref[...].astype(F32)
    product_ref[...] = (slope * gates).astype(BF)
    outs = [pltpu.make_async_copy(product_ref, product_hbm, out_sems.at[0])]
    outs[0].start()
    ins[5].wait()
    mixed = mixed_ref[...].astype(F32)
    gate_grad_ref[...] = (slope * mixed).astype(BF)
    outs.append(pltpu.make_async_copy(gate_grad_ref, gate_grad_hbm, out_sems.at[1]))
    outs[1].start()
    gated = (gates * mixed).astype(BF).T
    for other, target in ((1, other_hbm), (0, same_hbm)):
        for dx in range(4):
            at = other * 8 + 2 * dx
            for dzh in range(2):
                part = dot(held[grad_slot(where_ref, other, dx, dzh)], gated)
                sums[at + dzh] = (part * (SEQ**-0.5)).astype(BF)
            sem = out_sems.at[2 + other * 4 + dx]
            out = pltpu.make_async_copy(sums.at[pl.ds(at, 2)], target.at[pl.ds(2 * dx, 2)], sem)
            out.start()
            outs.append(out)
    for out in outs:
        out.wait()


HELD = pltpu.VMEM((16, CH, TOK), BF)
SQUARES = pltpu.VMEM((16, 256, 256), BF)
TILE = pltpu.VMEM((CH, TOK), BF)


def products_call(where, grads, weights, gates, mixed):
    tile = jax.ShapeDtypeStruct((CH, TOK), BF)
    eight = jax.ShapeDtypeStruct((8, 256, 256), BF)
    return pl.pallas_call(
        products_kernel,
        out_shape=(tile, tile, eight, eight),
        in_specs=[pl.BlockSpec(memory_space=pltpu.SMEM)] + [in_hbm()] * 14,
        out_specs=(in_hbm(),) * 4,
        scratch_shapes=[HELD, SQUARES, TILE, TILE, TILE, TILE, SQUARES, DMA((8,)), DMA((6,)), DMA((10,))],
        compiler_params=params(60),
        cost_estimate=pl.CostEstimate(flops=4 * CH * TOK * 4096, bytes_accessed=9 << 20, transcendentals=0),
        name="products",
    )(where, *grads, *weights, gates, mixed)


def exchange(value):
    return lax.all_to_all(value, "ctx", split_axis=0, concat_axis=0, tiled=True)


def add(*parts):
    total = parts[0].astype(F32)
    for part in parts[1:]:
        total = total + part.astype(F32)
    return total.astype(BF)


def on_device(inputs, gates, filters, out_grad, out_weight):
    ctx = lax.axis_index("ctx")
    tp = lax.axis_index("tp")
    where = jnp.stack([ctx // 4, (ctx // 2) % 2, ctx % 2, tp // 4, tp % 4]).astype(jnp.int32)

    w_line = lax.all_gather(out_weight.T, "ctx", axis_index_groups=LINES_X)

    rest = jnp.stack([send(out_grad, "tp", 1, 4, dz) for dz in (1, 2, 3)])
    up, down = send(out_grad, "tp", 4, 4, 1), send(out_grad, "tp", 4, 4, 3)
    up, w_line, own = lax.optimization_barrier((up, w_line, out_grad))
    near = [up, send(own, "tp", 4, 4, 2), down]
    rest, near, w_line = lax.optimization_barrier((rest, near, w_line))
    rests = [send(rest, "tp", 4, 4, dy) for dy in (1, 2, 3)]
    grads = [out_grad, rest]
    for n, r in zip(near, rests):
        grads += [n, r]

    w_far = send(w_line, "ctx", 2, 2, 1)
    weights = [w_line, w_far, send(w_line, "ctx", 1, 2, 1), send(w_far, "ctx", 1, 2, 1)]

    both = jnp.concatenate([inputs.reshape(16, FEW, TOK), filters.reshape(16, FEW, TOK)], axis=1)
    mixed_rows, spec = conv_call(exchange(both))
    mixed = exchange(mixed_rows).reshape(CH, TOK)

    product, gate_grad, part_other, part_same = products_call(where, grads, weights, gates, mixed)
    product_rows = exchange(product.reshape(16, FEW, TOK))
    received = send(part_other, "ctx", 1, 2, 1)
    chips = [add(part_same[2 * dx : 2 * dx + 2], received[2 * dx : 2 * dx + 2]) for dx in range(4)]
    product_rows, chips = lax.optimization_barrier((product_rows, chips))
    grad_rows = grads_call(product_rows, spec)
    both_grads = exchange(grad_rows)
    input_grad = both_grads[:, :FEW].reshape(CH, TOK)
    filter_grad = both_grads[:, FEW:].reshape(CH, TOK)

    line = add(chips[0], *[send(chips[dx], "ctx", 4, 4, dx) for dx in (1, 2, 3)])
    weight_grad = add(line[0], send(line[1], "ctx", 2, 2, 1))
    return (input_grad, gate_grad, filter_grad, weight_grad)


def solution(mesh):
    in_specs = (P("tp", "ctx"), P("tp", "ctx"), P("tp", "ctx"), P("tp", "ctx"), P("ctx", "tp"))
    out_specs = (P("tp", "ctx"), P("tp", "ctx"), P("tp", "ctx"), P("ctx", "tp"))
    return jax.shard_map(
        on_device, mesh=mesh, in_specs=in_specs, out_specs=out_specs, check_vma=False
    )
```

```python
import functools

import jax
import jax.numpy as jnp
import ml_dtypes
import numpy as np
from jax import lax
from jax.experimental import pallas as pl
from jax.experimental.pallas import tpu as pltpu
from jax.sharding import PartitionSpec as P

CH = 256
TOK = 512
FEW = 16
SEQ = 8192
ROWS = 64
LANES = 128
GROUP = 4
BF = jnp.bfloat16
F32 = jnp.float32


def shift_pairs(stride, size, by):
    pairs = []
    for i in range(16):
        at = (i // stride) % size
        pairs.append((i, i + ((at + by) % size - at) * stride))
    return pairs


def send(value, axis, stride, size, by):
    return lax.ppermute(value, axis, shift_pairs(stride, size, by))


LINES_X = [[4 * x + i for x in range(4)] for i in range(4)]
PLANES_X_CORE = [[4 * x + 2 * zh + core for x in range(4) for core in range(2)] for zh in range(2)]


def split_hi_lo(matrix):
    hi = matrix.astype(ml_dtypes.bfloat16)
    lo = (matrix - hi.astype(np.float64)).astype(ml_dtypes.bfloat16)
    return hi, lo


@functools.cache
def constants():
    n1 = np.arange(ROWS)
    k1 = np.arange(ROWS)
    n2 = np.arange(LANES)
    k2 = np.arange(LANES)
    first = np.exp(-2j * np.pi * np.outer(k1 + 0.25, n1) / ROWS)
    turn = np.exp(-2j * np.pi * np.outer(k1 + 0.25, n2) / SEQ)
    second = np.exp(-2j * np.pi * np.outer(n2, k2) / LANES)
    lhs = np.concatenate([first.real, first.imag], axis=0)
    hi, lo = split_hi_lo(lhs)
    first_c = np.concatenate([hi, lo], axis=1)

    def square(m):
        full = np.block([[m.real, m.imag], [-m.imag, m.real]])
        hi, lo = split_hi_lo(full)
        return np.concatenate([hi, hi, lo], axis=0)

    second_c = square(second)
    back_c = square(np.conj(second))
    scale = SEQ**-0.5 / SEQ
    last = np.conj(first).T * scale
    hi, lo = split_hi_lo(np.concatenate([last.real, -last.imag], axis=1))
    last_c = np.concatenate([hi, lo, hi], axis=1)
    turn_c = np.stack([turn.real, turn.imag]).astype(np.float32)
    return first_c, second_c, back_c, last_c, turn_c


def hi_lo(value):
    hi = value.astype(BF)
    lo = (value - hi.astype(F32)).astype(BF)
    return hi, lo


def dot(a, b):
    return jnp.dot(a, b, preferred_element_type=F32)


def spread(load, rows_ref):
    for s in range(16):
        block = load(s).astype(F32)
        for q in range(4):
            rows_ref[pl.ds((4 * s + q) * FEW, FEW), :] = block[:, q * LANES : (q + 1) * LANES]


def collect(rows_ref, store):
    for s in range(16):
        parts = [rows_ref[pl.ds((4 * s + q) * FEW, FEW), :] for q in range(4)]
        store(s, jnp.concatenate(parts, axis=1).astype(BF))


def forward_group(rows_ref, base, first_ref, second_ref, turn_ref):
    turn_re = turn_ref[0]
    turn_im = turn_ref[1]
    pieces = []
    for c in range(0, GROUP, 2):
        pair = [rows_ref[pl.ds(base + c + i, ROWS, stride=FEW), :].astype(BF) for i in range(2)]
        both = jnp.concatenate(pair, axis=1)
        out = dot(first_ref[...], jnp.concatenate([both, both], axis=0))
        for i in range(2):
            re = out[:ROWS, i * LANES : (i + 1) * LANES]
            im = out[ROWS:, i * LANES : (i + 1) * LANES]
            pieces.append(
                jnp.concatenate([re * turn_re - im * turn_im, re * turn_im + im * turn_re], axis=1)
            )
    hi, lo = hi_lo(jnp.concatenate(pieces, axis=0))
    spec = dot(jnp.concatenate([hi, lo, hi], axis=1), second_ref[...])
    return spec[:, :LANES], spec[:, LANES:]


def inverse_group(re, im, base, rows_ref, back_ref, last_ref, turn_ref):
    turn_re = turn_ref[0]
    turn_im = turn_ref[1]
    hi, lo = hi_lo(jnp.concatenate([re, im], axis=1))
    out = dot(jnp.concatenate([hi, lo, hi], axis=1), back_ref[...])
    for c in range(0, GROUP, 2):
        cols = []
        for i in range(2):
            d = out[(c + i) * ROWS : (c + i + 1) * ROWS]
            d_re, d_im = d[:, :LANES], d[:, LANES:]
            cols.append(
                jnp.concatenate([d_re * turn_re + d_im * turn_im, d_im * turn_re - d_re * turn_im], axis=0)
            )
        hi, lo = hi_lo(jnp.concatenate(cols, axis=1))
        time = dot(last_ref[...], jnp.concatenate([hi, hi, lo], axis=0))
        for i in range(2):
            rows_ref[pl.ds(base + c + i, ROWS, stride=FEW), :] = time[:, i * LANES : (i + 1) * LANES]


CONSTS = 5


def fetch(sources, targets, sems):
    copies = [pltpu.make_async_copy(src, dst, sems.at[i]) for i, (src, dst) in enumerate(zip(sources, targets))]
    for copy in copies:
        copy.start()
    return copies


def conv_kernel(xf_ref, *refs):
    hbm, (mixed_out, spec_out) = refs[:CONSTS], refs[CONSTS : CONSTS + 2]
    consts, (mixed_ref, spec_ref, x_rows, f_rows, m_rows, sems, mixed_sem, spec_sems) = (
        refs[CONSTS + 2 : 2 * CONSTS + 2],
        refs[2 * CONSTS + 2 :],
    )
    first_ref, second_ref, back_ref, last_ref, turn_ref = consts
    copies = fetch(hbm, consts, sems)
    spread(lambda s: xf_ref[s, :FEW], x_rows)
    spread(lambda s: xf_ref[s, FEW:], f_rows)
    for copy in copies:
        copy.wait()
    outs = []
    for base in range(0, FEW, GROUP):
        x_re, x_im = forward_group(x_rows, base, first_ref, second_ref, turn_ref)
        f_re, f_im = forward_group(f_rows, base, first_ref, second_ref, turn_ref)
        here = pl.ds(base * ROWS, GROUP * ROWS)
        spec_ref[0, here, :] = x_re
        spec_ref[1, here, :] = x_im
        spec_ref[2, here, :] = f_re
        spec_ref[3, here, :] = f_im
        out = pltpu.make_async_copy(spec_ref.at[:, here, :], spec_out.at[:, here, :], spec_sems.at[base // GROUP])
        out.start()
        outs.append(out)
        inverse_group(
            x_re * f_re - x_im * f_im, x_re * f_im + x_im * f_re, base, m_rows, back_ref, last_ref, turn_ref
        )

    def store(s, value):
        mixed_ref[s] = value

    collect(m_rows, store)
    out = pltpu.make_async_copy(mixed_ref, mixed_out, mixed_sem)
    out.start()
    outs.append(out)
    for out in outs:
        out.wait()


def grads_kernel(
    p_ref, first_ref, second_ref, back_ref, last_ref, turn_ref, spec_ref, out_ref, p_rows, i_rows, f_rows
):
    spread(lambda s: p_ref[s], p_rows)
    for base in range(0, FEW, GROUP):
        p_re, p_im = forward_group(p_rows, base, first_ref, second_ref, turn_ref)
        here = pl.ds(base * ROWS, GROUP * ROWS)
        for slot, rows in ((2, i_rows), (0, f_rows)):
            o_re = spec_ref[slot, here, :]
            o_im = spec_ref[slot + 1, here, :]
            inverse_group(
                p_re * o_re + p_im * o_im, p_im * o_re - p_re * o_im, base, rows, back_ref, last_ref, turn_ref
            )

    def store_at(first):
        def store(s, value):
            out_ref[s, first : first + FEW] = value

        return store

    collect(i_rows, store_at(0))
    collect(f_rows, store_at(FEW))


def params(mib):
    return pltpu.CompilerParams(vmem_limit_bytes=mib << 20)


def whole_vmem():
    return pl.BlockSpec(memory_space=pltpu.VMEM)


def in_hbm():
    return pl.BlockSpec(memory_space=pltpu.HBM)


ROWS_SCRATCH = pltpu.VMEM((ROWS * FEW, LANES), F32)
SPEC_SHAPE = (4, FEW * ROWS, LANES)
DMA = pltpu.SemaphoreType.DMA


def const_scratch():
    return [pltpu.VMEM(c.shape, c.dtype) for c in constants()]


def conv_call(xf):
    return pl.pallas_call(
        conv_kernel,
        out_shape=(jax.ShapeDtypeStruct((16, FEW, TOK), BF), jax.ShapeDtypeStruct(SPEC_SHAPE, F32)),
        in_specs=[whole_vmem()] + [in_hbm()] * CONSTS,
        out_specs=(in_hbm(), in_hbm()),
        scratch_shapes=const_scratch()
        + [pltpu.VMEM((16, FEW, TOK), BF), pltpu.VMEM(SPEC_SHAPE, F32)]
        + [ROWS_SCRATCH] * 3
        + [DMA((CONSTS,)), DMA, DMA((FEW // GROUP,))],
        compiler_params=params(60),
        cost_estimate=pl.CostEstimate(flops=10**9, bytes_accessed=4 << 20, transcendentals=0),
        name="conv",
    )(xf, *constants())


def grads_call(product, spec):
    return pl.pallas_call(
        grads_kernel,
        out_shape=jax.ShapeDtypeStruct((16, 2 * FEW, TOK), BF),
        in_specs=[whole_vmem()] * (CONSTS + 2),
        out_specs=whole_vmem(),
        scratch_shapes=[ROWS_SCRATCH] * 3,
        compiler_params=params(24),
        cost_estimate=pl.CostEstimate(flops=10**10, bytes_accessed=4 << 20, transcendentals=0),
        name="grads",
    )(product, *constants(), spec)


GRAD_SLOTS = ((0, 1), (1, 3), (4, 1), (5, 3), (8, 1), (9, 1), (10, 1), (11, 1), (12, 1), (13, 3))
GRAD_COUNTS = (2, 2, 4, 2)
GRADS = len(GRAD_SLOTS)


def fetch_grads(grads, held, sems):
    copies = []
    for i, (at, count) in enumerate(GRAD_SLOTS):
        target = held.at[at] if count == 1 else held.at[pl.ds(at, count)]
        copies.append(pltpu.make_async_copy(grads[i], target, sems.at[i]))
    for copy in copies:
        copy.start()
    return copies


def weight_slot(where_ref, dy, dz):
    zh, _, y, zl = (where_ref[i] for i in range(1, 5))
    x_from = jnp.bitwise_and(y + 4 - dy, 3)
    zl_from = jnp.bitwise_and(zl + 4 - dz, 3)
    zh_from = jnp.right_shift(zl_from, 1)
    core_from = jnp.bitwise_and(zl_from, 1)
    return x_from * 4 + core_from * 2 + jnp.bitwise_xor(zh, zh_from)


def grad_slot(where_ref, other, x_to, dzh):
    zh, core, y, zl = (where_ref[i] for i in range(1, 5))
    zl_from = jnp.bitwise_xor(zh, dzh) * 2 + jnp.bitwise_xor(core, other)
    return jnp.bitwise_and(y + 4 - x_to, 3) * 4 + jnp.bitwise_and(zl + 4 - zl_from, 3)


def products_kernel(where_ref, *refs):
    grads, refs = refs[:GRADS], refs[GRADS:]
    ins_hbm, (product_hbm, gate_grad_hbm, other_hbm, same_hbm) = refs[:3], refs[3:7]
    held, weights, gates_ref, mixed_ref, product_ref, gate_grad_ref, sums, grad_sems, sems, out_sems = refs[7:]
    targets = [weights, gates_ref, mixed_ref]
    ins = fetch(ins_hbm, targets, sems)
    copies = fetch_grads(grads, held, grad_sems)
    ins[0].wait()
    total = None
    for dy in range(4):
        for _ in range(GRAD_COUNTS[dy]):
            copies.pop(0).wait()
        weight = jnp.concatenate([weights[weight_slot(where_ref, dy, dz)] for dz in range(4)], axis=1)
        part = dot(weight, held[4 * dy : 4 * dy + 4].reshape(4 * CH, TOK))
        total = part if total is None else total + part
    slope = total.astype(BF).astype(F32)
    ins[1].wait()
    gates = gates_ref[...].astype(F32)
    product_ref[...] = (slope * gates).astype(BF)
    outs = [pltpu.make_async_copy(product_ref, product_hbm, out_sems.at[0])]
    outs[0].start()
    ins[2].wait()
    mixed = mixed_ref[...].astype(F32)
    gate_grad_ref[...] = (slope * mixed).astype(BF)
    outs.append(pltpu.make_async_copy(gate_grad_ref, gate_grad_hbm, out_sems.at[1]))
    outs[1].start()
    gated = (gates * mixed).astype(BF).T
    for other, target in ((1, other_hbm), (0, same_hbm)):
        for x_to in range(4):
            at = other * 8 + 2 * x_to
            for dzh in range(2):
                part = dot(held[grad_slot(where_ref, other, x_to, dzh)], gated)
                sums[at + dzh] = (part * (SEQ**-0.5)).astype(BF)
            sem = out_sems.at[2 + other * 4 + x_to]
            out = pltpu.make_async_copy(sums.at[pl.ds(at, 2)], target.at[pl.ds(2 * x_to, 2)], sem)
            out.start()
            outs.append(out)
    for out in outs:
        out.wait()


HELD = pltpu.VMEM((16, CH, TOK), BF)
SQUARES = pltpu.VMEM((16, 256, 256), BF)
TILE = pltpu.VMEM((CH, TOK), BF)


def products_call(where, grads, weights, gates, mixed):
    tile = jax.ShapeDtypeStruct((CH, TOK), BF)
    eight = jax.ShapeDtypeStruct((8, 256, 256), BF)
    return pl.pallas_call(
        products_kernel,
        out_shape=(tile, tile, eight, eight),
        in_specs=[pl.BlockSpec(memory_space=pltpu.SMEM)] + [in_hbm()] * (GRADS + 3),
        out_specs=(in_hbm(),) * 4,
        scratch_shapes=[HELD, SQUARES, TILE, TILE, TILE, TILE, SQUARES, DMA((GRADS,)), DMA((3,)), DMA((10,))],
        compiler_params=params(60),
        cost_estimate=pl.CostEstimate(flops=4 * CH * TOK * 4096, bytes_accessed=9 << 20, transcendentals=0),
        name="products",
    )(where, *grads, weights, gates, mixed)


def exchange(value):
    return lax.all_to_all(value, "ctx", split_axis=0, concat_axis=0, tiled=True)


def add(*parts):
    total = parts[0].astype(F32)
    for part in parts[1:]:
        total = total + part.astype(F32)
    return total.astype(BF)


def on_device(inputs, gates, filters, out_grad, out_weight):
    ctx = lax.axis_index("ctx")
    tp = lax.axis_index("tp")
    where = jnp.stack([ctx // 4, (ctx // 2) % 2, ctx % 2, tp // 4, tp % 4]).astype(jnp.int32)

    w_own = out_weight.T
    w_pair = jnp.stack([w_own, send(w_own, "ctx", 2, 2, 1)])
    weights = lax.all_gather(w_pair, "ctx", axis_index_groups=PLANES_X_CORE, tiled=True)

    both = jnp.concatenate([inputs.reshape(16, FEW, TOK), filters.reshape(16, FEW, TOK)], axis=1)
    mixed_rows, spec = conv_call(exchange(both))
    mixed = exchange(mixed_rows).reshape(CH, TOK)

    lines = [send(out_grad, "tp", 1, 4, dz) for dz in (1, 2, 3)]
    up, down = send(out_grad, "tp", 4, 4, 1), send(out_grad, "tp", 4, 4, 3)
    up, own = lax.optimization_barrier((up, out_grad))
    far = send(own, "tp", 4, 4, 2)
    lines, up, far, down, _ = lax.optimization_barrier((lines, up, far, down, mixed_rows))
    rest = jnp.stack(lines)
    grads = [out_grad, rest, up, send(rest, "tp", 4, 4, 1), far]
    grads += [send(far, "tp", 1, 4, dz) for dz in (1, 2, 3)]
    grads += [down, send(rest, "tp", 4, 4, 3)]

    product, gate_grad, part_other, part_same = products_call(where, grads, weights, gates, mixed)
    product_rows = exchange(product.reshape(16, FEW, TOK))
    chip = add(part_same, send(part_other, "ctx", 1, 2, 1))
    line = lax.psum_scatter(chip, "ctx", scatter_dimension=0, axis_index_groups=LINES_X, tiled=True)
    grad_rows = grads_call(product_rows, spec)
    both_grads = exchange(grad_rows)
    input_grad = both_grads[:, :FEW].reshape(CH, TOK)
    filter_grad = both_grads[:, FEW:].reshape(CH, TOK)

    weight_grad = add(line[0], send(line[1], "ctx", 2, 2, 1))
    return (input_grad, gate_grad, filter_grad, weight_grad)


def solution(mesh):
    in_specs = (P("tp", "ctx"), P("tp", "ctx"), P("tp", "ctx"), P("tp", "ctx"), P("ctx", "tp"))
    out_specs = (P("tp", "ctx"), P("tp", "ctx"), P("tp", "ctx"), P("ctx", "tp"))
    return jax.shard_map(
        on_device, mesh=mesh, in_specs=in_specs, out_specs=out_specs, check_vma=False
    )
```

```python
import functools

import jax
import jax.numpy as jnp
import ml_dtypes
import numpy as np
from jax import lax
from jax.experimental import pallas as pl
from jax.experimental.pallas import tpu as pltpu
from jax.sharding import PartitionSpec as P

CH = 256
TOK = 512
FEW = 16
SEQ = 8192
ROWS = 64
LANES = 128
GROUP = 4
BF = jnp.bfloat16
F32 = jnp.float32


def shift_pairs(stride, size, by):
    pairs = []
    for i in range(16):
        at = (i // stride) % size
        pairs.append((i, i + ((at + by) % size - at) * stride))
    return pairs


def send(value, axis, stride, size, by):
    return lax.ppermute(value, axis, shift_pairs(stride, size, by))


LINES_X = [[4 * x + i for x in range(4)] for i in range(4)]


def split_hi_lo(matrix):
    hi = matrix.astype(ml_dtypes.bfloat16)
    lo = (matrix - hi.astype(np.float64)).astype(ml_dtypes.bfloat16)
    return hi, lo


@functools.cache
def constants():
    n1 = np.arange(ROWS)
    k1 = np.arange(ROWS)
    n2 = np.arange(LANES)
    k2 = np.arange(LANES)
    first = np.exp(-2j * np.pi * np.outer(k1 + 0.25, n1) / ROWS)
    turn = np.exp(-2j * np.pi * np.outer(k1 + 0.25, n2) / SEQ)
    second = np.exp(-2j * np.pi * np.outer(n2, k2) / LANES)
    lhs = np.concatenate([first.real, first.imag], axis=0)
    hi, lo = split_hi_lo(lhs)
    first_c = np.concatenate([hi, lo], axis=1)

    def square(m):
        full = np.block([[m.real, m.imag], [-m.imag, m.real]])
        hi, lo = split_hi_lo(full)
        return np.concatenate([hi, hi, lo], axis=0)

    second_c = square(second)
    back_c = square(np.conj(second))
    scale = SEQ**-0.5 / SEQ
    last = np.conj(first).T * scale
    hi, lo = split_hi_lo(np.concatenate([last.real, -last.imag], axis=1))
    last_c = np.concatenate([hi, lo, hi], axis=1)
    turn_c = np.stack([turn.real, turn.imag]).astype(np.float32)
    return first_c, second_c, back_c, last_c, turn_c


def hi_lo(value):
    hi = value.astype(BF)
    lo = (value - hi.astype(F32)).astype(BF)
    return hi, lo


def dot(a, b):
    return jnp.dot(a, b, preferred_element_type=F32)


def spread(load, rows_ref):
    for s in range(16):
        block = load(s).astype(F32)
        for q in range(4):
            rows_ref[pl.ds((4 * s + q) * FEW, FEW), :] = block[:, q * LANES : (q + 1) * LANES]


def collect(rows_ref, store):
    for s in range(16):
        parts = [rows_ref[pl.ds((4 * s + q) * FEW, FEW), :] for q in range(4)]
        store(s, jnp.concatenate(parts, axis=1).astype(BF))


def forward_group(rows_ref, base, first_ref, second_ref, turn_ref):
    turn_re = turn_ref[0]
    turn_im = turn_ref[1]
    pieces = []
    for c in range(0, GROUP, 2):
        pair = [rows_ref[pl.ds(base + c + i, ROWS, stride=FEW), :].astype(BF) for i in range(2)]
        both = jnp.concatenate(pair, axis=1)
        out = dot(first_ref[...], jnp.concatenate([both, both], axis=0))
        for i in range(2):
            re = out[:ROWS, i * LANES : (i + 1) * LANES]
            im = out[ROWS:, i * LANES : (i + 1) * LANES]
            pieces.append(
                jnp.concatenate([re * turn_re - im * turn_im, re * turn_im + im * turn_re], axis=1)
            )
    hi, lo = hi_lo(jnp.concatenate(pieces, axis=0))
    spec = dot(jnp.concatenate([hi, lo, hi], axis=1), second_ref[...])
    return spec[:, :LANES], spec[:, LANES:]


def inverse_group(re, im, base, rows_ref, back_ref, last_ref, turn_ref):
    turn_re = turn_ref[0]
    turn_im = turn_ref[1]
    hi, lo = hi_lo(jnp.concatenate([re, im], axis=1))
    out = dot(jnp.concatenate([hi, lo, hi], axis=1), back_ref[...])
    for c in range(0, GROUP, 2):
        cols = []
        for i in range(2):
            d = out[(c + i) * ROWS : (c + i + 1) * ROWS]
            d_re, d_im = d[:, :LANES], d[:, LANES:]
            cols.append(
                jnp.concatenate([d_re * turn_re + d_im * turn_im, d_im * turn_re - d_re * turn_im], axis=0)
            )
        hi, lo = hi_lo(jnp.concatenate(cols, axis=1))
        time = dot(last_ref[...], jnp.concatenate([hi, hi, lo], axis=0))
        for i in range(2):
            rows_ref[pl.ds(base + c + i, ROWS, stride=FEW), :] = time[:, i * LANES : (i + 1) * LANES]


CONSTS = 5


def fetch(sources, targets, sems):
    copies = [pltpu.make_async_copy(src, dst, sems.at[i]) for i, (src, dst) in enumerate(zip(sources, targets))]
    for copy in copies:
        copy.start()
    return copies


def conv_kernel(xf_ref, *refs):
    hbm, (mixed_out, spec_out) = refs[:CONSTS], refs[CONSTS : CONSTS + 2]
    consts, (mixed_ref, spec_ref, x_rows, f_rows, m_rows, sems, mixed_sem, spec_sems) = (
        refs[CONSTS + 2 : 2 * CONSTS + 2],
        refs[2 * CONSTS + 2 :],
    )
    first_ref, second_ref, back_ref, last_ref, turn_ref = consts
    copies = fetch(hbm, consts, sems)
    spread(lambda s: xf_ref[s, :FEW], x_rows)
    spread(lambda s: xf_ref[s, FEW:], f_rows)
    for copy in copies:
        copy.wait()
    outs = []
    for base in range(0, FEW, GROUP):
        x_re, x_im = forward_group(x_rows, base, first_ref, second_ref, turn_ref)
        f_re, f_im = forward_group(f_rows, base, first_ref, second_ref, turn_ref)
        here = pl.ds(base * ROWS, GROUP * ROWS)
        spec_ref[0, here, :] = x_re
        spec_ref[1, here, :] = x_im
        spec_ref[2, here, :] = f_re
        spec_ref[3, here, :] = f_im
        out = pltpu.make_async_copy(spec_ref.at[:, here, :], spec_out.at[:, here, :], spec_sems.at[base // GROUP])
        out.start()
        outs.append(out)
        inverse_group(
            x_re * f_re - x_im * f_im, x_re * f_im + x_im * f_re, base, m_rows, back_ref, last_ref, turn_ref
        )

    def store(s, value):
        mixed_ref[s] = value

    collect(m_rows, store)
    out = pltpu.make_async_copy(mixed_ref, mixed_out, mixed_sem)
    out.start()
    outs.append(out)
    for out in outs:
        out.wait()


def grads_kernel(
    p_ref, first_ref, second_ref, back_ref, last_ref, turn_ref, spec_ref, out_ref, p_rows, i_rows, f_rows
):
    spread(lambda s: p_ref[s], p_rows)
    for base in range(0, FEW, GROUP):
        p_re, p_im = forward_group(p_rows, base, first_ref, second_ref, turn_ref)
        here = pl.ds(base * ROWS, GROUP * ROWS)
        for slot, rows in ((2, i_rows), (0, f_rows)):
            o_re = spec_ref[slot, here, :]
            o_im = spec_ref[slot + 1, here, :]
            inverse_group(
                p_re * o_re + p_im * o_im, p_im * o_re - p_re * o_im, base, rows, back_ref, last_ref, turn_ref
            )

    def store_at(first):
        def store(s, value):
            out_ref[s, first : first + FEW] = value

        return store

    collect(i_rows, store_at(0))
    collect(f_rows, store_at(FEW))


def params(mib):
    return pltpu.CompilerParams(vmem_limit_bytes=mib << 20)


def whole_vmem():
    return pl.BlockSpec(memory_space=pltpu.VMEM)


def in_hbm():
    return pl.BlockSpec(memory_space=pltpu.HBM)


ROWS_SCRATCH = pltpu.VMEM((ROWS * FEW, LANES), F32)
SPEC_SHAPE = (4, FEW * ROWS, LANES)
DMA = pltpu.SemaphoreType.DMA


def const_scratch():
    return [pltpu.VMEM(c.shape, c.dtype) for c in constants()]


def conv_call(xf):
    return pl.pallas_call(
        conv_kernel,
        out_shape=(jax.ShapeDtypeStruct((16, FEW, TOK), BF), jax.ShapeDtypeStruct(SPEC_SHAPE, F32)),
        in_specs=[whole_vmem()] + [in_hbm()] * CONSTS,
        out_specs=(in_hbm(), in_hbm()),
        scratch_shapes=const_scratch()
        + [pltpu.VMEM((16, FEW, TOK), BF), pltpu.VMEM(SPEC_SHAPE, F32)]
        + [ROWS_SCRATCH] * 3
        + [DMA((CONSTS,)), DMA, DMA((FEW // GROUP,))],
        compiler_params=params(60),
        cost_estimate=pl.CostEstimate(flops=10**9, bytes_accessed=4 << 20, transcendentals=0),
        name="conv",
    )(xf, *constants())


def grads_call(product, spec):
    return pl.pallas_call(
        grads_kernel,
        out_shape=jax.ShapeDtypeStruct((16, 2 * FEW, TOK), BF),
        in_specs=[whole_vmem()] * (CONSTS + 2),
        out_specs=whole_vmem(),
        scratch_shapes=[ROWS_SCRATCH] * 3,
        compiler_params=params(24),
        cost_estimate=pl.CostEstimate(flops=10**10, bytes_accessed=4 << 20, transcendentals=0),
        name="grads",
    )(product, *constants(), spec)


def fetch_grads(grads, held, sems):
    copies = []
    for dy in range(4):
        for part, target in enumerate((held.at[4 * dy], held.at[pl.ds(4 * dy + 1, 3)])):
            copies.append(pltpu.make_async_copy(grads[2 * dy + part], target, sems.at[2 * dy + part]))
    for copy in copies:
        copy.start()
    return copies


def weight_slot(where_ref, dy, dz):
    zh, core, y, zl = (where_ref[i] for i in range(1, 5))
    x_from = jnp.bitwise_and(y + 4 - dy, 3)
    zl_from = jnp.bitwise_and(zl + 4 - dz, 3)
    zh_from = jnp.right_shift(zl_from, 1)
    core_from = jnp.bitwise_and(zl_from, 1)
    return jnp.bitwise_xor(core, core_from) * 8 + jnp.bitwise_xor(zh, zh_from) * 4 + x_from


def grad_slot(where_ref, other, dx, dzh):
    x, zh, core, y, zl = (where_ref[i] for i in range(5))
    y_from = jnp.bitwise_and(x + dx, 3)
    zl_from = jnp.bitwise_xor(zh, dzh) * 2 + jnp.bitwise_xor(core, other)
    return jnp.bitwise_and(y + 4 - y_from, 3) * 4 + jnp.bitwise_and(zl + 4 - zl_from, 3)


def products_kernel(where_ref, *refs):
    grads, ins_hbm = refs[:8], refs[8:15]
    product_hbm, gate_grad_hbm, other_hbm, same_hbm = refs[15:19]
    held, weights, gates_ref, mixed_ref, product_ref, gate_grad_ref, sums, grad_sems, sems, out_sems = refs[19:]
    targets = [weights.at[pl.ds(4 * i, 4)] for i in range(3)] + [weights.at[pl.ds(12 + i, 2)] for i in (0, 2)]
    targets += [gates_ref, mixed_ref]
    ins = fetch(ins_hbm, targets, sems)
    copies = fetch_grads(grads, held, grad_sems)
    for copy in ins[:5]:
        copy.wait()
    total = None
    for dy in range(4):
        copies[2 * dy].wait()
        copies[2 * dy + 1].wait()
        weight = jnp.concatenate([weights[weight_slot(where_ref, dy, dz)] for dz in range(4)], axis=1)
        part = dot(weight, held[4 * dy : 4 * dy + 4].reshape(4 * CH, TOK))
        total = part if total is None else total + part
    slope = total.astype(BF).astype(F32)
    ins[5].wait()
    gates = gates_ref[...].astype(F32)
    product_ref[...] = (slope * gates).astype(BF)
    outs = [pltpu.make_async_copy(product_ref, product_hbm, out_sems.at[0])]
    outs[0].start()
    ins[6].wait()
    mixed = mixed_ref[...].astype(F32)
    gate_grad_ref[...] = (slope * mixed).astype(BF)
    outs.append(pltpu.make_async_copy(gate_grad_ref, gate_grad_hbm, out_sems.at[1]))
    outs[1].start()
    gated = (gates * mixed).astype(BF).T
    for other, target in ((1, other_hbm), (0, same_hbm)):
        for dx in range(4):
            at = other * 8 + 2 * dx
            for dzh in range(2):
                part = dot(held[grad_slot(where_ref, other, dx, dzh)], gated)
                sums[at + dzh] = (part * (SEQ**-0.5)).astype(BF)
            sem = out_sems.at[2 + other * 4 + dx]
            out = pltpu.make_async_copy(sums.at[pl.ds(at, 2)], target.at[pl.ds(2 * dx, 2)], sem)
            out.start()
            outs.append(out)
    for out in outs:
        out.wait()


def stack_kernel(*refs):
    ins, out, sems = refs[:-2], refs[-2], refs[-1]
    for copy in fetch(ins, [out.at[i] for i in range(len(ins))], sems):
        copy.wait()


def stack_call(parts):
    return pl.pallas_call(
        stack_kernel,
        out_shape=jax.ShapeDtypeStruct((len(parts),) + parts[0].shape, BF),
        in_specs=[in_hbm()] * len(parts),
        out_specs=in_hbm(),
        scratch_shapes=[DMA((len(parts),))],
        compiler_params=params(60),
        cost_estimate=pl.CostEstimate(flops=3 * 10**10, bytes_accessed=2 << 20, transcendentals=0),
        name="stack",
    )(*parts)


HELD = pltpu.VMEM((16, CH, TOK), BF)
SQUARES = pltpu.VMEM((16, 256, 256), BF)
TILE = pltpu.VMEM((CH, TOK), BF)


def products_call(where, grads, weights, gates, mixed):
    tile = jax.ShapeDtypeStruct((CH, TOK), BF)
    eight = jax.ShapeDtypeStruct((8, 256, 256), BF)
    return pl.pallas_call(
        products_kernel,
        out_shape=(tile, tile, eight, eight),
        in_specs=[pl.BlockSpec(memory_space=pltpu.SMEM)] + [in_hbm()] * 15,
        out_specs=(in_hbm(),) * 4,
        scratch_shapes=[HELD, SQUARES, TILE, TILE, TILE, TILE, SQUARES, DMA((8,)), DMA((7,)), DMA((10,))],
        compiler_params=params(60),
        cost_estimate=pl.CostEstimate(flops=4 * CH * TOK * 4096, bytes_accessed=9 << 20, transcendentals=0),
        name="products",
    )(where, *grads, *weights, gates, mixed)


def exchange(value):
    return lax.all_to_all(value, "ctx", split_axis=0, concat_axis=0, tiled=True)


def add(*parts):
    total = parts[0].astype(F32)
    for part in parts[1:]:
        total = total + part.astype(F32)
    return total.astype(BF)


def on_device(inputs, gates, filters, out_grad, out_weight):
    ctx = lax.axis_index("ctx")
    tp = lax.axis_index("tp")
    where = jnp.stack([ctx // 4, (ctx // 2) % 2, ctx % 2, tp // 4, tp % 4]).astype(jnp.int32)

    w_line = lax.all_gather(out_weight.T, "ctx", axis_index_groups=LINES_X)

    both = jnp.concatenate([inputs.reshape(16, FEW, TOK), filters.reshape(16, FEW, TOK)], axis=1)
    mixed_rows, spec = conv_call(exchange(both))
    mixed = exchange(mixed_rows).reshape(CH, TOK)

    rest = stack_call([send(out_grad, "tp", 1, 4, dz) for dz in (1, 2, 3)])
    up, far = send(out_grad, "tp", 4, 4, 1), send(out_grad, "tp", 4, 4, 2)
    up, own = lax.optimization_barrier((up, out_grad))
    near = [up, far, send(own, "tp", 4, 4, 3)]
    rest, near, w_line = lax.optimization_barrier((rest, near, w_line))
    rests = [send(rest, "tp", 4, 4, dy) for dy in (1, 2, 3)]
    grads = [out_grad, rest]
    for n, r in zip(near, rests):
        grads += [n, r]

    w_far = send(w_line, "ctx", 2, 2, 1)
    w_line, w_far, _ = lax.optimization_barrier((w_line, w_far, mixed_rows))
    weights = [w_line, w_far, send(w_line, "ctx", 1, 2, 1)]
    weights += [send(w_far[i : i + 2], "ctx", 1, 2, 1) for i in (0, 2)]

    product, gate_grad, part_other, part_same = products_call(where, grads, weights, gates, mixed)
    product_rows = exchange(product.reshape(16, FEW, TOK))
    received = send(part_other, "ctx", 1, 2, 1)
    chips = [add(part_same[2 * dx : 2 * dx + 2], received[2 * dx : 2 * dx + 2]) for dx in range(4)]
    product_rows, chips = lax.optimization_barrier((product_rows, chips))
    grad_rows = grads_call(product_rows, spec)
    both_grads = exchange(grad_rows)
    input_grad = both_grads[:, :FEW].reshape(CH, TOK)
    filter_grad = both_grads[:, FEW:].reshape(CH, TOK)

    line = add(chips[0], *[send(chips[dx], "ctx", 4, 4, dx) for dx in (1, 2, 3)])
    weight_grad = add(line[0], send(line[1], "ctx", 2, 2, 1))
    return (input_grad, gate_grad, filter_grad, weight_grad)


def solution(mesh):
    in_specs = (P("tp", "ctx"), P("tp", "ctx"), P("tp", "ctx"), P("tp", "ctx"), P("ctx", "tp"))
    out_specs = (P("tp", "ctx"), P("tp", "ctx"), P("tp", "ctx"), P("ctx", "tp"))
    return jax.shard_map(
        on_device, mesh=mesh, in_specs=in_specs, out_specs=out_specs, check_vma=False
    )
```

```python
import functools

import jax
import jax.numpy as jnp
import ml_dtypes
import numpy as np
from jax import lax
from jax.experimental import pallas as pl
from jax.experimental.pallas import tpu as pltpu
from jax.sharding import PartitionSpec as P

CH = 256
TOK = 512
FEW = 16
SEQ = 8192
ROWS = 64
LANES = 128
GROUP = 4
BF = jnp.bfloat16
F32 = jnp.float32


def shift_pairs(stride, size, by):
    pairs = []
    for i in range(16):
        at = (i // stride) % size
        pairs.append((i, i + ((at + by) % size - at) * stride))
    return pairs


def send(value, axis, stride, size, by):
    return lax.ppermute(value, axis, shift_pairs(stride, size, by))


LINES_X = [[4 * x + i for x in range(4)] for i in range(4)]


def split_hi_lo(matrix):
    hi = matrix.astype(ml_dtypes.bfloat16)
    lo = (matrix - hi.astype(np.float64)).astype(ml_dtypes.bfloat16)
    return hi, lo


@functools.cache
def constants():
    n1 = np.arange(ROWS)
    k1 = np.arange(ROWS)
    n2 = np.arange(LANES)
    k2 = np.arange(LANES)
    first = np.exp(-2j * np.pi * np.outer(k1 + 0.25, n1) / ROWS)
    turn = np.exp(-2j * np.pi * np.outer(k1 + 0.25, n2) / SEQ)
    second = np.exp(-2j * np.pi * np.outer(n2, k2) / LANES)
    lhs = np.concatenate([first.real, first.imag], axis=0)
    hi, lo = split_hi_lo(lhs)
    first_c = np.concatenate([hi, lo], axis=1)

    def square(m):
        full = np.block([[m.real, m.imag], [-m.imag, m.real]])
        hi, lo = split_hi_lo(full)
        return np.concatenate([hi, hi, lo], axis=0)

    second_c = square(second)
    back_c = square(np.conj(second))
    scale = SEQ**-0.5 / SEQ
    last = np.conj(first).T * scale
    hi, lo = split_hi_lo(np.concatenate([last.real, -last.imag], axis=1))
    last_c = np.concatenate([hi, lo, hi], axis=1)
    turn_c = np.stack([turn.real, turn.imag]).astype(np.float32)
    return first_c, second_c, back_c, last_c, turn_c


def hi_lo(value):
    hi = value.astype(BF)
    lo = (value - hi.astype(F32)).astype(BF)
    return hi, lo


def dot(a, b):
    return jnp.dot(a, b, preferred_element_type=F32)


def spread(load, rows_ref):
    for s in range(16):
        block = load(s).astype(F32)
        for q in range(4):
            rows_ref[pl.ds((4 * s + q) * FEW, FEW), :] = block[:, q * LANES : (q + 1) * LANES]


def collect(rows_ref, store):
    for s in range(16):
        parts = [rows_ref[pl.ds((4 * s + q) * FEW, FEW), :] for q in range(4)]
        store(s, jnp.concatenate(parts, axis=1).astype(BF))


def forward_group(rows_ref, base, first_ref, second_ref, turn_ref):
    turn_re = turn_ref[0]
    turn_im = turn_ref[1]
    pieces = []
    for c in range(0, GROUP, 2):
        pair = [rows_ref[pl.ds(base + c + i, ROWS, stride=FEW), :].astype(BF) for i in range(2)]
        both = jnp.concatenate(pair, axis=1)
        out = dot(first_ref[...], jnp.concatenate([both, both], axis=0))
        for i in range(2):
            re = out[:ROWS, i * LANES : (i + 1) * LANES]
            im = out[ROWS:, i * LANES : (i + 1) * LANES]
            pieces.append(
                jnp.concatenate([re * turn_re - im * turn_im, re * turn_im + im * turn_re], axis=1)
            )
    hi, lo = hi_lo(jnp.concatenate(pieces, axis=0))
    spec = dot(jnp.concatenate([hi, lo, hi], axis=1), second_ref[...])
    return spec[:, :LANES], spec[:, LANES:]


def inverse_group(re, im, base, rows_ref, back_ref, last_ref, turn_ref):
    turn_re = turn_ref[0]
    turn_im = turn_ref[1]
    hi, lo = hi_lo(jnp.concatenate([re, im], axis=1))
    out = dot(jnp.concatenate([hi, lo, hi], axis=1), back_ref[...])
    for c in range(0, GROUP, 2):
        cols = []
        for i in range(2):
            d = out[(c + i) * ROWS : (c + i + 1) * ROWS]
            d_re, d_im = d[:, :LANES], d[:, LANES:]
            cols.append(
                jnp.concatenate([d_re * turn_re + d_im * turn_im, d_im * turn_re - d_re * turn_im], axis=0)
            )
        hi, lo = hi_lo(jnp.concatenate(cols, axis=1))
        time = dot(last_ref[...], jnp.concatenate([hi, hi, lo], axis=0))
        for i in range(2):
            rows_ref[pl.ds(base + c + i, ROWS, stride=FEW), :] = time[:, i * LANES : (i + 1) * LANES]


CONSTS = 5


def fetch(sources, targets, sems):
    copies = [pltpu.make_async_copy(src, dst, sems.at[i]) for i, (src, dst) in enumerate(zip(sources, targets))]
    for copy in copies:
        copy.start()
    return copies


def conv_kernel(xf_ref, *refs):
    hbm, (mixed_out, spec_out) = refs[:CONSTS], refs[CONSTS : CONSTS + 2]
    consts, (mixed_ref, spec_ref, x_rows, f_rows, m_rows, sems, mixed_sem, spec_sems) = (
        refs[CONSTS + 2 : 2 * CONSTS + 2],
        refs[2 * CONSTS + 2 :],
    )
    first_ref, second_ref, back_ref, last_ref, turn_ref = consts
    copies = fetch(hbm, consts, sems)
    spread(lambda s: xf_ref[s, :FEW], x_rows)
    spread(lambda s: xf_ref[s, FEW:], f_rows)
    for copy in copies:
        copy.wait()
    outs = []
    for base in range(0, FEW, GROUP):
        x_re, x_im = forward_group(x_rows, base, first_ref, second_ref, turn_ref)
        f_re, f_im = forward_group(f_rows, base, first_ref, second_ref, turn_ref)
        here = pl.ds(base * ROWS, GROUP * ROWS)
        spec_ref[0, here, :] = x_re
        spec_ref[1, here, :] = x_im
        spec_ref[2, here, :] = f_re
        spec_ref[3, here, :] = f_im
        out = pltpu.make_async_copy(spec_ref.at[:, here, :], spec_out.at[:, here, :], spec_sems.at[base // GROUP])
        out.start()
        outs.append(out)
        inverse_group(
            x_re * f_re - x_im * f_im, x_re * f_im + x_im * f_re, base, m_rows, back_ref, last_ref, turn_ref
        )

    def store(s, value):
        mixed_ref[s] = value

    collect(m_rows, store)
    out = pltpu.make_async_copy(mixed_ref, mixed_out, mixed_sem)
    out.start()
    outs.append(out)
    for out in outs:
        out.wait()


def grads_kernel(
    p_ref, first_ref, second_ref, back_ref, last_ref, turn_ref, spec_ref, out_ref, p_rows, i_rows, f_rows
):
    spread(lambda s: p_ref[s], p_rows)
    for base in range(0, FEW, GROUP):
        p_re, p_im = forward_group(p_rows, base, first_ref, second_ref, turn_ref)
        here = pl.ds(base * ROWS, GROUP * ROWS)
        for slot, rows in ((2, i_rows), (0, f_rows)):
            o_re = spec_ref[slot, here, :]
            o_im = spec_ref[slot + 1, here, :]
            inverse_group(
                p_re * o_re + p_im * o_im, p_im * o_re - p_re * o_im, base, rows, back_ref, last_ref, turn_ref
            )

    def store_at(first):
        def store(s, value):
            out_ref[s, first : first + FEW] = value

        return store

    collect(i_rows, store_at(0))
    collect(f_rows, store_at(FEW))


def params(mib):
    return pltpu.CompilerParams(vmem_limit_bytes=mib << 20)


def whole_vmem():
    return pl.BlockSpec(memory_space=pltpu.VMEM)


def in_hbm():
    return pl.BlockSpec(memory_space=pltpu.HBM)


ROWS_SCRATCH = pltpu.VMEM((ROWS * FEW, LANES), F32)
SPEC_SHAPE = (4, FEW * ROWS, LANES)
DMA = pltpu.SemaphoreType.DMA


def const_scratch():
    return [pltpu.VMEM(c.shape, c.dtype) for c in constants()]


def conv_call(xf):
    return pl.pallas_call(
        conv_kernel,
        out_shape=(jax.ShapeDtypeStruct((16, FEW, TOK), BF), jax.ShapeDtypeStruct(SPEC_SHAPE, F32)),
        in_specs=[whole_vmem()] + [in_hbm()] * CONSTS,
        out_specs=(in_hbm(), in_hbm()),
        scratch_shapes=const_scratch()
        + [pltpu.VMEM((16, FEW, TOK), BF), pltpu.VMEM(SPEC_SHAPE, F32)]
        + [ROWS_SCRATCH] * 3
        + [DMA((CONSTS,)), DMA, DMA((FEW // GROUP,))],
        compiler_params=params(60),
        cost_estimate=pl.CostEstimate(flops=10**9, bytes_accessed=4 << 20, transcendentals=0),
        name="conv",
    )(xf, *constants())


def grads_call(product, spec):
    return pl.pallas_call(
        grads_kernel,
        out_shape=jax.ShapeDtypeStruct((16, 2 * FEW, TOK), BF),
        in_specs=[whole_vmem()] * (CONSTS + 2),
        out_specs=whole_vmem(),
        scratch_shapes=[ROWS_SCRATCH] * 3,
        compiler_params=params(24),
        cost_estimate=pl.CostEstimate(flops=1 * 10**10, bytes_accessed=4 << 20, transcendentals=0),
        name="grads",
    )(product, *constants(), spec)


def fetch_grads(grads, held, sems):
    copies = []
    for dy in range(4):
        for part, target in enumerate((held.at[4 * dy], held.at[pl.ds(4 * dy + 1, 3)])):
            copies.append(pltpu.make_async_copy(grads[2 * dy + part], target, sems.at[2 * dy + part]))
    for copy in copies:
        copy.start()
    return copies


def weight_slot(where_ref, dy, dz):
    zh, core, y, zl = (where_ref[i] for i in range(1, 5))
    x_from = jnp.bitwise_and(y + 4 - dy, 3)
    zl_from = jnp.bitwise_and(zl + 4 - dz, 3)
    zh_from = jnp.right_shift(zl_from, 1)
    core_from = jnp.bitwise_and(zl_from, 1)
    return jnp.bitwise_xor(core, core_from) * 8 + jnp.bitwise_xor(zh, zh_from) * 4 + x_from


def grad_slot(where_ref, other, dx, dzh):
    x, zh, core, y, zl = (where_ref[i] for i in range(5))
    y_from = jnp.bitwise_and(x + dx, 3)
    zl_from = jnp.bitwise_xor(zh, dzh) * 2 + jnp.bitwise_xor(core, other)
    return jnp.bitwise_and(y + 4 - y_from, 3) * 4 + jnp.bitwise_and(zl + 4 - zl_from, 3)


def products_kernel(where_ref, *refs):
    grads, ins_hbm = refs[:8], refs[8:15]
    product_hbm, gate_grad_hbm, other_hbm, same_hbm = refs[15:19]
    held, weights, gates_ref, mixed_ref, product_ref, gate_grad_ref, sums, grad_sems, sems, out_sems = refs[19:]
    targets = [weights.at[pl.ds(4 * i, 4)] for i in range(3)] + [weights.at[pl.ds(12 + i, 2)] for i in (0, 2)]
    targets += [gates_ref, mixed_ref]
    ins = fetch(ins_hbm, targets, sems)
    copies = fetch_grads(grads, held, grad_sems)
    for copy in ins[:5]:
        copy.wait()
    total = None
    for dy in range(4):
        copies[2 * dy].wait()
        copies[2 * dy + 1].wait()
        weight = jnp.concatenate([weights[weight_slot(where_ref, dy, dz)] for dz in range(4)], axis=1)
        part = dot(weight, held[4 * dy : 4 * dy + 4].reshape(4 * CH, TOK))
        total = part if total is None else total + part
    slope = total.astype(BF).astype(F32)
    ins[5].wait()
    gates = gates_ref[...].astype(F32)
    product_ref[...] = (slope * gates).astype(BF)
    outs = [pltpu.make_async_copy(product_ref, product_hbm, out_sems.at[0])]
    outs[0].start()
    ins[6].wait()
    mixed = mixed_ref[...].astype(F32)
    gate_grad_ref[...] = (slope * mixed).astype(BF)
    outs.append(pltpu.make_async_copy(gate_grad_ref, gate_grad_hbm, out_sems.at[1]))
    outs[1].start()
    gated = (gates * mixed).astype(BF).T
    for other, target in ((1, other_hbm), (0, same_hbm)):
        for dx in range(4):
            at = other * 8 + 2 * dx
            for dzh in range(2):
                part = dot(held[grad_slot(where_ref, other, dx, dzh)], gated)
                sums[at + dzh] = (part * (SEQ**-0.5)).astype(BF)
            sem = out_sems.at[2 + other * 4 + dx]
            out = pltpu.make_async_copy(sums.at[pl.ds(at, 2)], target.at[pl.ds(2 * dx, 2)], sem)
            out.start()
            outs.append(out)
    for out in outs:
        out.wait()


def stack_kernel(*refs):
    for i, ref in enumerate(refs[:-1]):
        refs[-1][i] = ref[...]


def stack_call(parts):
    return pl.pallas_call(
        stack_kernel,
        out_shape=jax.ShapeDtypeStruct((len(parts),) + parts[0].shape, BF),
        in_specs=[whole_vmem()] * len(parts),
        out_specs=whole_vmem(),
        compiler_params=params(8),
        cost_estimate=pl.CostEstimate(flops=3 * 10**10, bytes_accessed=2 << 20, transcendentals=0),
        name="stack",
    )(*parts)


HELD = pltpu.VMEM((16, CH, TOK), BF)
SQUARES = pltpu.VMEM((16, 256, 256), BF)
TILE = pltpu.VMEM((CH, TOK), BF)


def products_call(where, grads, weights, gates, mixed):
    tile = jax.ShapeDtypeStruct((CH, TOK), BF)
    eight = jax.ShapeDtypeStruct((8, 256, 256), BF)
    return pl.pallas_call(
        products_kernel,
        out_shape=(tile, tile, eight, eight),
        in_specs=[pl.BlockSpec(memory_space=pltpu.SMEM)] + [in_hbm()] * 15,
        out_specs=(in_hbm(),) * 4,
        scratch_shapes=[HELD, SQUARES, TILE, TILE, TILE, TILE, SQUARES, DMA((8,)), DMA((7,)), DMA((10,))],
        compiler_params=params(60),
        cost_estimate=pl.CostEstimate(flops=4 * CH * TOK * 4096, bytes_accessed=9 << 20, transcendentals=0),
        name="products",
    )(where, *grads, *weights, gates, mixed)


def exchange(value):
    return lax.all_to_all(value, "ctx", split_axis=0, concat_axis=0, tiled=True)


def add(*parts):
    total = parts[0].astype(F32)
    for part in parts[1:]:
        total = total + part.astype(F32)
    return total.astype(BF)


def on_device(inputs, gates, filters, out_grad, out_weight):
    ctx = lax.axis_index("ctx")
    tp = lax.axis_index("tp")
    where = jnp.stack([ctx // 4, (ctx // 2) % 2, ctx % 2, tp // 4, tp % 4]).astype(jnp.int32)

    w_line = lax.all_gather(out_weight.T, "ctx", axis_index_groups=LINES_X)

    both = jnp.concatenate([inputs.reshape(16, FEW, TOK), filters.reshape(16, FEW, TOK)], axis=1)
    mixed_rows, spec = conv_call(exchange(both))
    mixed = exchange(mixed_rows).reshape(CH, TOK)

    rest = stack_call([send(out_grad, "tp", 1, 4, dz) for dz in (1, 2, 3)])
    up, far = send(out_grad, "tp", 4, 4, 1), send(out_grad, "tp", 4, 4, 2)
    up, own = lax.optimization_barrier((up, out_grad))
    near = [up, far, send(own, "tp", 4, 4, 3)]
    rest, near, w_line = lax.optimization_barrier((rest, near, w_line))
    rests = [send(rest, "tp", 4, 4, dy) for dy in (1, 2, 3)]
    grads = [out_grad, rest]
    for n, r in zip(near, rests):
        grads += [n, r]

    w_far = send(w_line, "ctx", 2, 2, 1)
    w_line, w_far, _ = lax.optimization_barrier((w_line, w_far, mixed_rows))
    weights = [w_line, w_far, send(w_line, "ctx", 1, 2, 1)]
    weights += [send(w_far[i : i + 2], "ctx", 1, 2, 1) for i in (0, 2)]

    product, gate_grad, part_other, part_same = products_call(where, grads, weights, gates, mixed)
    product_rows = exchange(product.reshape(16, FEW, TOK))
    received = send(part_other, "ctx", 1, 2, 1)
    chips = [add(part_same[2 * dx : 2 * dx + 2], received[2 * dx : 2 * dx + 2]) for dx in range(4)]

    grad_rows = grads_call(product_rows, spec)
    both_grads = exchange(grad_rows)
    input_grad = both_grads[:, :FEW].reshape(CH, TOK)
    filter_grad = both_grads[:, FEW:].reshape(CH, TOK)

    line = add(chips[0], *[send(chips[dx], "ctx", 4, 4, dx) for dx in (1, 2, 3)])
    weight_grad = add(line[0], send(line[1], "ctx", 2, 2, 1))
    return (input_grad, gate_grad, filter_grad, weight_grad)


def solution(mesh):
    in_specs = (P("tp", "ctx"), P("tp", "ctx"), P("tp", "ctx"), P("tp", "ctx"), P("ctx", "tp"))
    out_specs = (P("tp", "ctx"), P("tp", "ctx"), P("tp", "ctx"), P("ctx", "tp"))
    return jax.shard_map(
        on_device, mesh=mesh, in_specs=in_specs, out_specs=out_specs, check_vma=False
    )
```

```python
import functools

import jax
import jax.numpy as jnp
import ml_dtypes
import numpy as np
from jax import lax
from jax.experimental import pallas as pl
from jax.experimental.pallas import tpu as pltpu
from jax.sharding import PartitionSpec as P

CH = 256
TOK = 512
FEW = 16
SEQ = 8192
ROWS = 64
LANES = 128
GROUP = 4
BF = jnp.bfloat16
F32 = jnp.float32


def shift_pairs(stride, size, by):
    pairs = []
    for i in range(16):
        at = (i // stride) % size
        pairs.append((i, i + ((at + by) % size - at) * stride))
    return pairs


def send(value, axis, stride, size, by):
    return lax.ppermute(value, axis, shift_pairs(stride, size, by))


LINES_X = [[4 * x + i for x in range(4)] for i in range(4)]


def split_hi_lo(matrix):
    hi = matrix.astype(ml_dtypes.bfloat16)
    lo = (matrix - hi.astype(np.float64)).astype(ml_dtypes.bfloat16)
    return hi, lo


@functools.cache
def constants():
    n1 = np.arange(ROWS)
    k1 = np.arange(ROWS)
    n2 = np.arange(LANES)
    k2 = np.arange(LANES)
    first = np.exp(-2j * np.pi * np.outer(k1 + 0.25, n1) / ROWS)
    turn = np.exp(-2j * np.pi * np.outer(k1 + 0.25, n2) / SEQ)
    second = np.exp(-2j * np.pi * np.outer(n2, k2) / LANES)
    lhs = np.concatenate([first.real, first.imag], axis=0)
    hi, lo = split_hi_lo(lhs)
    first_c = np.concatenate([hi, lo], axis=1)

    def square(m):
        full = np.block([[m.real, m.imag], [-m.imag, m.real]])
        hi, lo = split_hi_lo(full)
        return np.concatenate([hi, hi, lo], axis=0)

    second_c = square(second)
    back_c = square(np.conj(second))
    scale = SEQ**-0.5 / SEQ
    last = np.conj(first).T * scale
    hi, lo = split_hi_lo(np.concatenate([last.real, -last.imag], axis=1))
    last_c = np.concatenate([hi, lo, hi], axis=1)
    turn_c = np.stack([turn.real, turn.imag]).astype(np.float32)
    return first_c, second_c, back_c, last_c, turn_c


def hi_lo(value):
    hi = value.astype(BF)
    lo = (value - hi.astype(F32)).astype(BF)
    return hi, lo


def dot(a, b):
    return jnp.dot(a, b, preferred_element_type=F32)


def spread(load, rows_ref):
    for s in range(16):
        block = load(s).astype(F32)
        for q in range(4):
            rows_ref[pl.ds((4 * s + q) * FEW, FEW), :] = block[:, q * LANES : (q + 1) * LANES]


def collect(rows_ref, store):
    for s in range(16):
        parts = [rows_ref[pl.ds((4 * s + q) * FEW, FEW), :] for q in range(4)]
        store(s, jnp.concatenate(parts, axis=1).astype(BF))


def forward_group(rows_ref, base, first_ref, second_ref, turn_ref):
    turn_re = turn_ref[0]
    turn_im = turn_ref[1]
    pieces = []
    for c in range(0, GROUP, 2):
        pair = [rows_ref[pl.ds(base + c + i, ROWS, stride=FEW), :].astype(BF) for i in range(2)]
        both = jnp.concatenate(pair, axis=1)
        out = dot(first_ref[...], jnp.concatenate([both, both], axis=0))
        for i in range(2):
            re = out[:ROWS, i * LANES : (i + 1) * LANES]
            im = out[ROWS:, i * LANES : (i + 1) * LANES]
            pieces.append(
                jnp.concatenate([re * turn_re - im * turn_im, re * turn_im + im * turn_re], axis=1)
            )
    hi, lo = hi_lo(jnp.concatenate(pieces, axis=0))
    spec = dot(jnp.concatenate([hi, lo, hi], axis=1), second_ref[...])
    return spec[:, :LANES], spec[:, LANES:]


def inverse_group(re, im, base, rows_ref, back_ref, last_ref, turn_ref):
    turn_re = turn_ref[0]
    turn_im = turn_ref[1]
    hi, lo = hi_lo(jnp.concatenate([re, im], axis=1))
    out = dot(jnp.concatenate([hi, lo, hi], axis=1), back_ref[...])
    for c in range(0, GROUP, 2):
        cols = []
        for i in range(2):
            d = out[(c + i) * ROWS : (c + i + 1) * ROWS]
            d_re, d_im = d[:, :LANES], d[:, LANES:]
            cols.append(
                jnp.concatenate([d_re * turn_re + d_im * turn_im, d_im * turn_re - d_re * turn_im], axis=0)
            )
        hi, lo = hi_lo(jnp.concatenate(cols, axis=1))
        time = dot(last_ref[...], jnp.concatenate([hi, hi, lo], axis=0))
        for i in range(2):
            rows_ref[pl.ds(base + c + i, ROWS, stride=FEW), :] = time[:, i * LANES : (i + 1) * LANES]


CONSTS = 5


def fetch(sources, targets, sems):
    copies = [pltpu.make_async_copy(src, dst, sems.at[i]) for i, (src, dst) in enumerate(zip(sources, targets))]
    for copy in copies:
        copy.start()
    return copies


def conv_kernel(xf_ref, *refs):
    hbm, (mixed_out, spec_out) = refs[:CONSTS], refs[CONSTS : CONSTS + 2]
    consts, (mixed_ref, spec_ref, x_rows, f_rows, m_rows, sems, mixed_sem, spec_sems) = (
        refs[CONSTS + 2 : 2 * CONSTS + 2],
        refs[2 * CONSTS + 2 :],
    )
    first_ref, second_ref, back_ref, last_ref, turn_ref = consts
    copies = fetch(hbm, consts, sems)
    spread(lambda s: xf_ref[s, :FEW], x_rows)
    spread(lambda s: xf_ref[s, FEW:], f_rows)
    for copy in copies:
        copy.wait()
    outs = []
    for base in range(0, FEW, GROUP):
        x_re, x_im = forward_group(x_rows, base, first_ref, second_ref, turn_ref)
        f_re, f_im = forward_group(f_rows, base, first_ref, second_ref, turn_ref)
        here = pl.ds(base * ROWS, GROUP * ROWS)
        spec_ref[0, here, :] = x_re
        spec_ref[1, here, :] = x_im
        spec_ref[2, here, :] = f_re
        spec_ref[3, here, :] = f_im
        out = pltpu.make_async_copy(spec_ref.at[:, here, :], spec_out.at[:, here, :], spec_sems.at[base // GROUP])
        out.start()
        outs.append(out)
        inverse_group(
            x_re * f_re - x_im * f_im, x_re * f_im + x_im * f_re, base, m_rows, back_ref, last_ref, turn_ref
        )

    def store(s, value):
        mixed_ref[s] = value

    collect(m_rows, store)
    out = pltpu.make_async_copy(mixed_ref, mixed_out, mixed_sem)
    out.start()
    outs.append(out)
    for out in outs:
        out.wait()


def grads_kernel(
    p_ref, first_ref, second_ref, back_ref, last_ref, turn_ref, spec_ref, out_ref, p_rows, i_rows, f_rows
):
    spread(lambda s: p_ref[s], p_rows)
    for base in range(0, FEW, GROUP):
        p_re, p_im = forward_group(p_rows, base, first_ref, second_ref, turn_ref)
        here = pl.ds(base * ROWS, GROUP * ROWS)
        for slot, rows in ((2, i_rows), (0, f_rows)):
            o_re = spec_ref[slot, here, :]
            o_im = spec_ref[slot + 1, here, :]
            inverse_group(
                p_re * o_re + p_im * o_im, p_im * o_re - p_re * o_im, base, rows, back_ref, last_ref, turn_ref
            )

    def store_at(first):
        def store(s, value):
            out_ref[s, first : first + FEW] = value

        return store

    collect(i_rows, store_at(0))
    collect(f_rows, store_at(FEW))


def params(mib):
    return pltpu.CompilerParams(vmem_limit_bytes=mib << 20)


def whole_vmem():
    return pl.BlockSpec(memory_space=pltpu.VMEM)


def in_hbm():
    return pl.BlockSpec(memory_space=pltpu.HBM)


ROWS_SCRATCH = pltpu.VMEM((ROWS * FEW, LANES), F32)
SPEC_SHAPE = (4, FEW * ROWS, LANES)
DMA = pltpu.SemaphoreType.DMA


def const_scratch():
    return [pltpu.VMEM(c.shape, c.dtype) for c in constants()]


def conv_call(xf):
    return pl.pallas_call(
        conv_kernel,
        out_shape=(jax.ShapeDtypeStruct((16, FEW, TOK), BF), jax.ShapeDtypeStruct(SPEC_SHAPE, F32)),
        in_specs=[whole_vmem()] + [in_hbm()] * CONSTS,
        out_specs=(in_hbm(), in_hbm()),
        scratch_shapes=const_scratch()
        + [pltpu.VMEM((16, FEW, TOK), BF), pltpu.VMEM(SPEC_SHAPE, F32)]
        + [ROWS_SCRATCH] * 3
        + [DMA((CONSTS,)), DMA, DMA((FEW // GROUP,))],
        compiler_params=params(60),
        cost_estimate=pl.CostEstimate(flops=10**9, bytes_accessed=4 << 20, transcendentals=0),
        name="conv",
    )(xf, *constants())


def grads_call(product, spec):
    return pl.pallas_call(
        grads_kernel,
        out_shape=jax.ShapeDtypeStruct((16, 2 * FEW, TOK), BF),
        in_specs=[whole_vmem()] * (CONSTS + 2),
        out_specs=whole_vmem(),
        scratch_shapes=[ROWS_SCRATCH] * 3,
        compiler_params=params(24),
        cost_estimate=pl.CostEstimate(flops=1 * 10**10, bytes_accessed=4 << 20, transcendentals=0),
        name="grads",
    )(product, *constants(), spec)


def fetch_grads(grads, held, sems):
    copies = []
    for dy in range(4):
        for part, target in enumerate((held.at[4 * dy], held.at[pl.ds(4 * dy + 1, 3)])):
            copies.append(pltpu.make_async_copy(grads[2 * dy + part], target, sems.at[2 * dy + part]))
    for copy in copies:
        copy.start()
    return copies


def weight_slot(where_ref, dy, dz):
    zh, core, y, zl = (where_ref[i] for i in range(1, 5))
    x_from = jnp.bitwise_and(y + 4 - dy, 3)
    zl_from = jnp.bitwise_and(zl + 4 - dz, 3)
    zh_from = jnp.right_shift(zl_from, 1)
    core_from = jnp.bitwise_and(zl_from, 1)
    return jnp.bitwise_xor(core, core_from) * 8 + jnp.bitwise_xor(zh, zh_from) * 4 + x_from


def grad_slot(where_ref, other, dx, dzh):
    x, zh, core, y, zl = (where_ref[i] for i in range(5))
    y_from = jnp.bitwise_and(x + dx, 3)
    zl_from = jnp.bitwise_xor(zh, dzh) * 2 + jnp.bitwise_xor(core, other)
    return jnp.bitwise_and(y + 4 - y_from, 3) * 4 + jnp.bitwise_and(zl + 4 - zl_from, 3)


def products_kernel(where_ref, *refs):
    grads, ins_hbm = refs[:8], refs[8:15]
    product_hbm, gate_grad_hbm, other_hbm, same_hbm = refs[15:19]
    held, weights, gates_ref, mixed_ref, product_ref, gate_grad_ref, sums, grad_sems, sems, out_sems = refs[19:]
    targets = [weights.at[pl.ds(4 * i, 4)] for i in range(3)] + [weights.at[pl.ds(12 + i, 2)] for i in (0, 2)]
    targets += [gates_ref, mixed_ref]
    ins = fetch(ins_hbm, targets, sems)
    copies = fetch_grads(grads, held, grad_sems)
    for copy in ins[:5]:
        copy.wait()
    total = None
    for dy in range(4):
        copies[2 * dy].wait()
        copies[2 * dy + 1].wait()
        weight = jnp.concatenate([weights[weight_slot(where_ref, dy, dz)] for dz in range(4)], axis=1)
        part = dot(weight, held[4 * dy : 4 * dy + 4].reshape(4 * CH, TOK))
        total = part if total is None else total + part
    slope = total.astype(BF).astype(F32)
    ins[5].wait()
    gates = gates_ref[...].astype(F32)
    product_ref[...] = (slope * gates).astype(BF)
    outs = [pltpu.make_async_copy(product_ref, product_hbm, out_sems.at[0])]
    outs[0].start()
    ins[6].wait()
    mixed = mixed_ref[...].astype(F32)
    gate_grad_ref[...] = (slope * mixed).astype(BF)
    outs.append(pltpu.make_async_copy(gate_grad_ref, gate_grad_hbm, out_sems.at[1]))
    outs[1].start()
    gated = (gates * mixed).astype(BF).T
    for other, target in ((1, other_hbm), (0, same_hbm)):
        for dx in range(4):
            at = other * 8 + 2 * dx
            for dzh in range(2):
                part = dot(held[grad_slot(where_ref, other, dx, dzh)], gated)
                sums[at + dzh] = (part * (SEQ**-0.5)).astype(BF)
            sem = out_sems.at[2 + other * 4 + dx]
            out = pltpu.make_async_copy(sums.at[pl.ds(at, 2)], target.at[pl.ds(2 * dx, 2)], sem)
            out.start()
            outs.append(out)
    for out in outs:
        out.wait()


def stack_kernel(*refs):
    for i, ref in enumerate(refs[:-1]):
        refs[-1][i] = ref[...]


def stack_call(parts):
    return pl.pallas_call(
        stack_kernel,
        out_shape=jax.ShapeDtypeStruct((len(parts),) + parts[0].shape, BF),
        in_specs=[whole_vmem()] * len(parts),
        out_specs=whole_vmem(),
        compiler_params=params(8),
        cost_estimate=pl.CostEstimate(flops=3 * 10**10, bytes_accessed=2 << 20, transcendentals=0),
        name="stack",
    )(*parts)


HELD = pltpu.VMEM((16, CH, TOK), BF)
SQUARES = pltpu.VMEM((16, 256, 256), BF)
TILE = pltpu.VMEM((CH, TOK), BF)


def products_call(where, grads, weights, gates, mixed):
    tile = jax.ShapeDtypeStruct((CH, TOK), BF)
    eight = jax.ShapeDtypeStruct((8, 256, 256), BF)
    return pl.pallas_call(
        products_kernel,
        out_shape=(tile, tile, eight, eight),
        in_specs=[pl.BlockSpec(memory_space=pltpu.SMEM)] + [in_hbm()] * 15,
        out_specs=(in_hbm(),) * 4,
        scratch_shapes=[HELD, SQUARES, TILE, TILE, TILE, TILE, SQUARES, DMA((8,)), DMA((7,)), DMA((10,))],
        compiler_params=params(60),
        cost_estimate=pl.CostEstimate(flops=4 * CH * TOK * 4096, bytes_accessed=9 << 20, transcendentals=0),
        name="products",
    )(where, *grads, *weights, gates, mixed)


def exchange(value):
    return lax.all_to_all(value, "ctx", split_axis=0, concat_axis=0, tiled=True)


def add(*parts):
    total = parts[0].astype(F32)
    for part in parts[1:]:
        total = total + part.astype(F32)
    return total.astype(BF)


def on_device(inputs, gates, filters, out_grad, out_weight):
    ctx = lax.axis_index("ctx")
    tp = lax.axis_index("tp")
    where = jnp.stack([ctx // 4, (ctx // 2) % 2, ctx % 2, tp // 4, tp % 4]).astype(jnp.int32)

    w_line = lax.all_gather(out_weight.T, "ctx", axis_index_groups=LINES_X)

    both = jnp.concatenate([inputs.reshape(16, FEW, TOK), filters.reshape(16, FEW, TOK)], axis=1)
    arrived = exchange(both)
    mixed_rows, spec = conv_call(arrived)
    mixed = exchange(mixed_rows).reshape(CH, TOK)

    rest = stack_call([send(out_grad, "tp", 1, 4, dz) for dz in (1, 2, 3)])
    up, far = send(out_grad, "tp", 4, 4, 1), send(out_grad, "tp", 4, 4, 2)
    up, own = lax.optimization_barrier((up, out_grad))
    near = [up, far, send(own, "tp", 4, 4, 3)]
    rest, near, w_line = lax.optimization_barrier((rest, near, w_line))
    rests = [send(rest, "tp", 4, 4, dy) for dy in (1, 2, 3)]
    grads = [out_grad, rest]
    for n, r in zip(near, rests):
        grads += [n, r]

    w_line, _ = lax.optimization_barrier((w_line, arrived))
    w_far = send(w_line, "ctx", 2, 2, 1)
    weights = [w_line, w_far, send(w_line, "ctx", 1, 2, 1)]
    weights += [send(w_far[i : i + 2], "ctx", 1, 2, 1) for i in (0, 2)]

    product, gate_grad, part_other, part_same = products_call(where, grads, weights, gates, mixed)
    product_rows = exchange(product.reshape(16, FEW, TOK))
    received = send(part_other, "ctx", 1, 2, 1)
    chips = [add(part_same[2 * dx : 2 * dx + 2], received[2 * dx : 2 * dx + 2]) for dx in range(4)]

    grad_rows = grads_call(product_rows, spec)
    both_grads = exchange(grad_rows)
    input_grad = both_grads[:, :FEW].reshape(CH, TOK)
    filter_grad = both_grads[:, FEW:].reshape(CH, TOK)

    line = add(chips[0], *[send(chips[dx], "ctx", 4, 4, dx) for dx in (1, 2, 3)])
    weight_grad = add(line[0], send(line[1], "ctx", 2, 2, 1))
    return (input_grad, gate_grad, filter_grad, weight_grad)


def solution(mesh):
    in_specs = (P("tp", "ctx"), P("tp", "ctx"), P("tp", "ctx"), P("tp", "ctx"), P("ctx", "tp"))
    out_specs = (P("tp", "ctx"), P("tp", "ctx"), P("tp", "ctx"), P("ctx", "tp"))
    return jax.shard_map(
        on_device, mesh=mesh, in_specs=in_specs, out_specs=out_specs, check_vma=False
    )
```

```python
import functools

import jax
import jax.numpy as jnp
import ml_dtypes
import numpy as np
from jax import lax
from jax.experimental import pallas as pl
from jax.experimental.pallas import tpu as pltpu
from jax.sharding import PartitionSpec as P

CH = 256
TOK = 512
FEW = 16
SEQ = 8192
ROWS = 64
LANES = 128
GROUP = 4
BF = jnp.bfloat16
F32 = jnp.float32


def shift_pairs(stride, size, by):
    pairs = []
    for i in range(16):
        at = (i // stride) % size
        pairs.append((i, i + ((at + by) % size - at) * stride))
    return pairs


def send(value, axis, stride, size, by):
    return lax.ppermute(value, axis, shift_pairs(stride, size, by))


LINES_X = [[4 * x + i for x in range(4)] for i in range(4)]


def split_hi_lo(matrix):
    hi = matrix.astype(ml_dtypes.bfloat16)
    lo = (matrix - hi.astype(np.float64)).astype(ml_dtypes.bfloat16)
    return hi, lo


@functools.cache
def constants():
    n1 = np.arange(ROWS)
    k1 = np.arange(ROWS)
    n2 = np.arange(LANES)
    k2 = np.arange(LANES)
    first = np.exp(-2j * np.pi * np.outer(k1 + 0.25, n1) / ROWS)
    turn = np.exp(-2j * np.pi * np.outer(k1 + 0.25, n2) / SEQ)
    second = np.exp(-2j * np.pi * np.outer(n2, k2) / LANES)
    lhs = np.concatenate([first.real, first.imag], axis=0)
    hi, lo = split_hi_lo(lhs)
    first_c = np.concatenate([hi, lo], axis=1)

    def square(m):
        full = np.block([[m.real, m.imag], [-m.imag, m.real]])
        hi, lo = split_hi_lo(full)
        return np.concatenate([hi, hi, lo], axis=0)

    second_c = square(second)
    back_c = square(np.conj(second))
    scale = SEQ**-0.5 / SEQ
    last = np.conj(first).T * scale
    hi, lo = split_hi_lo(np.concatenate([last.real, -last.imag], axis=1))
    last_c = np.concatenate([hi, lo, hi], axis=1)
    turn_c = np.stack([turn.real, turn.imag]).astype(np.float32)
    return first_c, second_c, back_c, last_c, turn_c


def hi_lo(value):
    hi = value.astype(BF)
    lo = (value - hi.astype(F32)).astype(BF)
    return hi, lo


def dot(a, b):
    return jnp.dot(a, b, preferred_element_type=F32)


def spread(load, rows_ref):
    for s in range(16):
        block = load(s).astype(F32)
        for q in range(4):
            rows_ref[pl.ds((4 * s + q) * FEW, FEW), :] = block[:, q * LANES : (q + 1) * LANES]


def collect(rows_ref, store):
    for s in range(16):
        parts = [rows_ref[pl.ds((4 * s + q) * FEW, FEW), :] for q in range(4)]
        store(s, jnp.concatenate(parts, axis=1).astype(BF))


def forward_group(rows_ref, base, first_ref, second_ref, turn_ref):
    turn_re = turn_ref[0]
    turn_im = turn_ref[1]
    pieces = []
    for c in range(0, GROUP, 2):
        pair = [rows_ref[pl.ds(base + c + i, ROWS, stride=FEW), :].astype(BF) for i in range(2)]
        both = jnp.concatenate(pair, axis=1)
        out = dot(first_ref[...], jnp.concatenate([both, both], axis=0))
        for i in range(2):
            re = out[:ROWS, i * LANES : (i + 1) * LANES]
            im = out[ROWS:, i * LANES : (i + 1) * LANES]
            pieces.append(
                jnp.concatenate([re * turn_re - im * turn_im, re * turn_im + im * turn_re], axis=1)
            )
    hi, lo = hi_lo(jnp.concatenate(pieces, axis=0))
    spec = dot(jnp.concatenate([hi, lo, hi], axis=1), second_ref[...])
    return spec[:, :LANES], spec[:, LANES:]


def inverse_group(re, im, base, rows_ref, back_ref, last_ref, turn_ref):
    turn_re = turn_ref[0]
    turn_im = turn_ref[1]
    hi, lo = hi_lo(jnp.concatenate([re, im], axis=1))
    out = dot(jnp.concatenate([hi, lo, hi], axis=1), back_ref[...])
    for c in range(0, GROUP, 2):
        cols = []
        for i in range(2):
            d = out[(c + i) * ROWS : (c + i + 1) * ROWS]
            d_re, d_im = d[:, :LANES], d[:, LANES:]
            cols.append(
                jnp.concatenate([d_re * turn_re + d_im * turn_im, d_im * turn_re - d_re * turn_im], axis=0)
            )
        hi, lo = hi_lo(jnp.concatenate(cols, axis=1))
        time = dot(last_ref[...], jnp.concatenate([hi, hi, lo], axis=0))
        for i in range(2):
            rows_ref[pl.ds(base + c + i, ROWS, stride=FEW), :] = time[:, i * LANES : (i + 1) * LANES]


CONSTS = 5


def fetch(sources, targets, sems):
    copies = [pltpu.make_async_copy(src, dst, sems.at[i]) for i, (src, dst) in enumerate(zip(sources, targets))]
    for copy in copies:
        copy.start()
    return copies


def conv_kernel(xf_ref, *refs):
    hbm, (mixed_out, spec_out) = refs[:CONSTS], refs[CONSTS : CONSTS + 2]
    consts, (mixed_ref, spec_ref, x_rows, f_rows, m_rows, sems, mixed_sem, spec_sems) = (
        refs[CONSTS + 2 : 2 * CONSTS + 2],
        refs[2 * CONSTS + 2 :],
    )
    first_ref, second_ref, back_ref, last_ref, turn_ref = consts
    copies = fetch(hbm, consts, sems)
    spread(lambda s: xf_ref[s, :FEW], x_rows)
    spread(lambda s: xf_ref[s, FEW:], f_rows)
    for copy in copies:
        copy.wait()
    outs = []
    for base in range(0, FEW, GROUP):
        x_re, x_im = forward_group(x_rows, base, first_ref, second_ref, turn_ref)
        f_re, f_im = forward_group(f_rows, base, first_ref, second_ref, turn_ref)
        here = pl.ds(base * ROWS, GROUP * ROWS)
        spec_ref[0, here, :] = x_re
        spec_ref[1, here, :] = x_im
        spec_ref[2, here, :] = f_re
        spec_ref[3, here, :] = f_im
        out = pltpu.make_async_copy(spec_ref.at[:, here, :], spec_out.at[:, here, :], spec_sems.at[base // GROUP])
        out.start()
        outs.append(out)
        inverse_group(
            x_re * f_re - x_im * f_im, x_re * f_im + x_im * f_re, base, m_rows, back_ref, last_ref, turn_ref
        )

    def store(s, value):
        mixed_ref[s] = value

    collect(m_rows, store)
    out = pltpu.make_async_copy(mixed_ref, mixed_out, mixed_sem)
    out.start()
    outs.append(out)
    for out in outs:
        out.wait()


def grads_kernel(
    p_ref, first_ref, second_ref, back_ref, last_ref, turn_ref, spec_ref, out_ref, p_rows, i_rows, f_rows
):
    spread(lambda s: p_ref[s], p_rows)
    for base in range(0, FEW, GROUP):
        p_re, p_im = forward_group(p_rows, base, first_ref, second_ref, turn_ref)
        here = pl.ds(base * ROWS, GROUP * ROWS)
        for slot, rows in ((2, i_rows), (0, f_rows)):
            o_re = spec_ref[slot, here, :]
            o_im = spec_ref[slot + 1, here, :]
            inverse_group(
                p_re * o_re + p_im * o_im, p_im * o_re - p_re * o_im, base, rows, back_ref, last_ref, turn_ref
            )

    def store_at(first):
        def store(s, value):
            out_ref[s, first : first + FEW] = value

        return store

    collect(i_rows, store_at(0))
    collect(f_rows, store_at(FEW))


def params(mib):
    return pltpu.CompilerParams(vmem_limit_bytes=mib << 20)


def whole_vmem():
    return pl.BlockSpec(memory_space=pltpu.VMEM)


def in_hbm():
    return pl.BlockSpec(memory_space=pltpu.HBM)


ROWS_SCRATCH = pltpu.VMEM((ROWS * FEW, LANES), F32)
SPEC_SHAPE = (4, FEW * ROWS, LANES)
DMA = pltpu.SemaphoreType.DMA


def const_scratch():
    return [pltpu.VMEM(c.shape, c.dtype) for c in constants()]


def conv_call(xf):
    return pl.pallas_call(
        conv_kernel,
        out_shape=(jax.ShapeDtypeStruct((16, FEW, TOK), BF), jax.ShapeDtypeStruct(SPEC_SHAPE, F32)),
        in_specs=[whole_vmem()] + [in_hbm()] * CONSTS,
        out_specs=(in_hbm(), in_hbm()),
        scratch_shapes=const_scratch()
        + [pltpu.VMEM((16, FEW, TOK), BF), pltpu.VMEM(SPEC_SHAPE, F32)]
        + [ROWS_SCRATCH] * 3
        + [DMA((CONSTS,)), DMA, DMA((FEW // GROUP,))],
        compiler_params=params(60),
        cost_estimate=pl.CostEstimate(flops=10**9, bytes_accessed=4 << 20, transcendentals=0),
        name="conv",
    )(xf, *constants())


def grads_call(product, spec):
    return pl.pallas_call(
        grads_kernel,
        out_shape=jax.ShapeDtypeStruct((16, 2 * FEW, TOK), BF),
        in_specs=[whole_vmem()] * (CONSTS + 2),
        out_specs=whole_vmem(),
        scratch_shapes=[ROWS_SCRATCH] * 3,
        compiler_params=params(24),
        cost_estimate=pl.CostEstimate(flops=1 * 10**10, bytes_accessed=4 << 20, transcendentals=0),
        name="grads",
    )(product, *constants(), spec)


def fetch_grads(grads, held, sems):
    copies = []
    for dy in range(4):
        for part, target in enumerate((held.at[4 * dy], held.at[pl.ds(4 * dy + 1, 3)])):
            copies.append(pltpu.make_async_copy(grads[2 * dy + part], target, sems.at[2 * dy + part]))
    for copy in copies:
        copy.start()
    return copies


def weight_slot(where_ref, dy, dz):
    zh, core, y, zl = (where_ref[i] for i in range(1, 5))
    x_from = jnp.bitwise_and(y + 4 - dy, 3)
    zl_from = jnp.bitwise_and(zl + 4 - dz, 3)
    zh_from = jnp.right_shift(zl_from, 1)
    core_from = jnp.bitwise_and(zl_from, 1)
    return jnp.bitwise_xor(core, core_from) * 8 + jnp.bitwise_xor(zh, zh_from) * 4 + x_from


def grad_slot(where_ref, other, dx, dzh):
    x, zh, core, y, zl = (where_ref[i] for i in range(5))
    y_from = jnp.bitwise_and(x + dx, 3)
    zl_from = jnp.bitwise_xor(zh, dzh) * 2 + jnp.bitwise_xor(core, other)
    return jnp.bitwise_and(y + 4 - y_from, 3) * 4 + jnp.bitwise_and(zl + 4 - zl_from, 3)


def products_kernel(where_ref, *refs):
    grads, ins_hbm = [refs[i] for i in (0, 1, 2, 3, 6, 7, 4, 5)], refs[8:15]
    product_hbm, gate_grad_hbm, other_hbm, same_hbm = refs[15:19]
    held, weights, gates_ref, mixed_ref, product_ref, gate_grad_ref, sums, grad_sems, sems, out_sems = refs[19:]
    targets = [weights.at[pl.ds(4 * i, 4)] for i in range(3)] + [weights.at[pl.ds(12 + i, 2)] for i in (0, 2)]
    targets += [gates_ref, mixed_ref]
    ins = fetch(ins_hbm, targets, sems)
    copies = fetch_grads(grads, held, grad_sems)
    for copy in ins[:5]:
        copy.wait()
    total = None
    for dy in range(4):
        copies[2 * dy].wait()
        copies[2 * dy + 1].wait()
        weight = jnp.concatenate([weights[weight_slot(where_ref, dy, dz)] for dz in range(4)], axis=1)
        part = dot(weight, held[4 * dy : 4 * dy + 4].reshape(4 * CH, TOK))
        total = part if total is None else total + part
    slope = total.astype(BF).astype(F32)
    ins[5].wait()
    gates = gates_ref[...].astype(F32)
    product_ref[...] = (slope * gates).astype(BF)
    outs = [pltpu.make_async_copy(product_ref, product_hbm, out_sems.at[0])]
    outs[0].start()
    ins[6].wait()
    mixed = mixed_ref[...].astype(F32)
    gate_grad_ref[...] = (slope * mixed).astype(BF)
    outs.append(pltpu.make_async_copy(gate_grad_ref, gate_grad_hbm, out_sems.at[1]))
    outs[1].start()
    gated = (gates * mixed).astype(BF).T
    for other, target in ((1, other_hbm), (0, same_hbm)):
        for dx in range(4):
            at = other * 8 + 2 * dx
            for dzh in range(2):
                part = dot(held[grad_slot(where_ref, other, dx, dzh)], gated)
                sums[at + dzh] = (part * (SEQ**-0.5)).astype(BF)
            sem = out_sems.at[2 + other * 4 + dx]
            out = pltpu.make_async_copy(sums.at[pl.ds(at, 2)], target.at[pl.ds(2 * dx, 2)], sem)
            out.start()
            outs.append(out)
    for out in outs:
        out.wait()


def stack_kernel(*refs):
    for i, ref in enumerate(refs[:-1]):
        refs[-1][i] = ref[...]


def stack_call(parts):
    return pl.pallas_call(
        stack_kernel,
        out_shape=jax.ShapeDtypeStruct((len(parts),) + parts[0].shape, BF),
        in_specs=[whole_vmem()] * len(parts),
        out_specs=whole_vmem(),
        compiler_params=params(8),
        cost_estimate=pl.CostEstimate(flops=3 * 10**10, bytes_accessed=2 << 20, transcendentals=0),
        name="stack",
    )(*parts)


HELD = pltpu.VMEM((16, CH, TOK), BF)
SQUARES = pltpu.VMEM((16, 256, 256), BF)
TILE = pltpu.VMEM((CH, TOK), BF)


def products_call(where, grads, weights, gates, mixed):
    tile = jax.ShapeDtypeStruct((CH, TOK), BF)
    eight = jax.ShapeDtypeStruct((8, 256, 256), BF)
    return pl.pallas_call(
        products_kernel,
        out_shape=(tile, tile, eight, eight),
        in_specs=[pl.BlockSpec(memory_space=pltpu.SMEM)] + [in_hbm()] * 15,
        out_specs=(in_hbm(),) * 4,
        scratch_shapes=[HELD, SQUARES, TILE, TILE, TILE, TILE, SQUARES, DMA((8,)), DMA((7,)), DMA((10,))],
        compiler_params=params(60),
        cost_estimate=pl.CostEstimate(flops=4 * CH * TOK * 4096, bytes_accessed=9 << 20, transcendentals=0),
        name="products",
    )(where, *grads, *weights, gates, mixed)


def exchange(value):
    return lax.all_to_all(value, "ctx", split_axis=0, concat_axis=0, tiled=True)


def add(*parts):
    total = parts[0].astype(F32)
    for part in parts[1:]:
        total = total + part.astype(F32)
    return total.astype(BF)


def on_device(inputs, gates, filters, out_grad, out_weight):
    ctx = lax.axis_index("ctx")
    tp = lax.axis_index("tp")
    where = jnp.stack([ctx // 4, (ctx // 2) % 2, ctx % 2, tp // 4, tp % 4]).astype(jnp.int32)


    both = jnp.concatenate([inputs.reshape(16, FEW, TOK), filters.reshape(16, FEW, TOK)], axis=1)
    arrived = exchange(both)
    mixed_rows, spec = conv_call(arrived)
    mixed = exchange(mixed_rows).reshape(CH, TOK)

    lines = [send(out_grad, "tp", 1, 4, dz) for dz in (1, 2, 3)]
    up, far = send(out_grad, "tp", 4, 4, 1), send(out_grad, "tp", 4, 4, 2)
    up, own, w_own = lax.optimization_barrier((up, out_grad, out_weight))
    w_line = lax.all_gather(w_own.T, "ctx", axis_index_groups=LINES_X)
    near = [up, far, send(own, "tp", 4, 4, 3)]
    lines, w_line = lax.optimization_barrier((lines, w_line))
    rest, near = lax.optimization_barrier((stack_call(lines), near))
    rests = [send(rest, "tp", 4, 4, dy) for dy in (1, 2, 3)]
    grads = [out_grad, rest]
    for dy in (1, 3, 2):
        grads += [near[dy - 1], rests[dy - 1]]

    w_line, _ = lax.optimization_barrier((w_line, arrived))
    w_far = send(w_line, "ctx", 2, 2, 1)
    weights = [w_line, w_far, send(w_line, "ctx", 1, 2, 1)]
    weights += [send(w_far[i : i + 2], "ctx", 1, 2, 1) for i in (0, 2)]

    product, gate_grad, part_other, part_same = products_call(where, grads, weights, gates, mixed)
    product_rows = exchange(product.reshape(16, FEW, TOK))
    received = send(part_other, "ctx", 1, 2, 1)
    chips = [add(part_same[2 * dx : 2 * dx + 2], received[2 * dx : 2 * dx + 2]) for dx in range(4)]

    grad_rows = grads_call(product_rows, spec)
    both_grads = exchange(grad_rows)
    input_grad = both_grads[:, :FEW].reshape(CH, TOK)
    filter_grad = both_grads[:, FEW:].reshape(CH, TOK)

    line = add(chips[0], *[send(chips[dx], "ctx", 4, 4, dx) for dx in (1, 2, 3)])
    weight_grad = add(line[0], send(line[1], "ctx", 2, 2, 1))
    return (input_grad, gate_grad, filter_grad, weight_grad)


def solution(mesh):
    in_specs = (P("tp", "ctx"), P("tp", "ctx"), P("tp", "ctx"), P("tp", "ctx"), P("ctx", "tp"))
    out_specs = (P("tp", "ctx"), P("tp", "ctx"), P("tp", "ctx"), P("ctx", "tp"))
    return jax.shard_map(
        on_device, mesh=mesh, in_specs=in_specs, out_specs=out_specs, check_vma=False
    )
```

```python
import functools

import jax
import jax.numpy as jnp
import ml_dtypes
import numpy as np
from jax import lax
from jax.experimental import pallas as pl
from jax.experimental.pallas import tpu as pltpu
from jax.sharding import PartitionSpec as P

CH = 256
TOK = 512
FEW = 16
SEQ = 8192
ROWS = 64
LANES = 128
GROUP = 4
BF = jnp.bfloat16
F32 = jnp.float32


def shift_pairs(stride, size, by):
    pairs = []
    for i in range(16):
        at = (i // stride) % size
        pairs.append((i, i + ((at + by) % size - at) * stride))
    return pairs


def send(value, axis, stride, size, by):
    return lax.ppermute(value, axis, shift_pairs(stride, size, by))


LINES_X = [[4 * x + i for x in range(4)] for i in range(4)]


def split_hi_lo(matrix):
    hi = matrix.astype(ml_dtypes.bfloat16)
    lo = (matrix - hi.astype(np.float64)).astype(ml_dtypes.bfloat16)
    return hi, lo


@functools.cache
def constants():
    n1 = np.arange(ROWS)
    k1 = np.arange(ROWS)
    n2 = np.arange(LANES)
    k2 = np.arange(LANES)
    first = np.exp(-2j * np.pi * np.outer(k1 + 0.25, n1) / ROWS)
    turn = np.exp(-2j * np.pi * np.outer(k1 + 0.25, n2) / SEQ)
    second = np.exp(-2j * np.pi * np.outer(n2, k2) / LANES)
    lhs = np.concatenate([first.real, first.imag], axis=0)
    hi, lo = split_hi_lo(lhs)
    first_c = np.concatenate([hi, lo], axis=1)

    def square(m):
        full = np.block([[m.real, m.imag], [-m.imag, m.real]])
        hi, lo = split_hi_lo(full)
        return np.concatenate([hi, hi, lo], axis=0)

    second_c = square(second)
    back_c = square(np.conj(second))
    scale = SEQ**-0.5 / SEQ
    last = np.conj(first).T * scale
    hi, lo = split_hi_lo(np.concatenate([last.real, -last.imag], axis=1))
    last_c = np.concatenate([hi, lo, hi], axis=1)
    turn_c = np.stack([turn.real, turn.imag]).astype(np.float32)
    return first_c, second_c, back_c, last_c, turn_c


def hi_lo(value):
    hi = value.astype(BF)
    lo = (value - hi.astype(F32)).astype(BF)
    return hi, lo


def dot(a, b):
    return jnp.dot(a, b, preferred_element_type=F32)


def spread(load, rows_ref):
    for s in range(16):
        block = load(s).astype(F32)
        for q in range(4):
            rows_ref[pl.ds((4 * s + q) * FEW, FEW), :] = block[:, q * LANES : (q + 1) * LANES]


def collect(rows_ref, store):
    for s in range(16):
        parts = [rows_ref[pl.ds((4 * s + q) * FEW, FEW), :] for q in range(4)]
        store(s, jnp.concatenate(parts, axis=1).astype(BF))


def forward_group(rows_ref, base, first_ref, second_ref, turn_ref):
    turn_re = turn_ref[0]
    turn_im = turn_ref[1]
    pieces = []
    for c in range(0, GROUP, 2):
        pair = [rows_ref[pl.ds(base + c + i, ROWS, stride=FEW), :].astype(BF) for i in range(2)]
        both = jnp.concatenate(pair, axis=1)
        out = dot(first_ref[...], jnp.concatenate([both, both], axis=0))
        for i in range(2):
            re = out[:ROWS, i * LANES : (i + 1) * LANES]
            im = out[ROWS:, i * LANES : (i + 1) * LANES]
            pieces.append(
                jnp.concatenate([re * turn_re - im * turn_im, re * turn_im + im * turn_re], axis=1)
            )
    hi, lo = hi_lo(jnp.concatenate(pieces, axis=0))
    spec = dot(jnp.concatenate([hi, lo, hi], axis=1), second_ref[...])
    return spec[:, :LANES], spec[:, LANES:]


def inverse_group(re, im, base, rows_ref, back_ref, last_ref, turn_ref):
    turn_re = turn_ref[0]
    turn_im = turn_ref[1]
    hi, lo = hi_lo(jnp.concatenate([re, im], axis=1))
    out = dot(jnp.concatenate([hi, lo, hi], axis=1), back_ref[...])
    for c in range(0, GROUP, 2):
        cols = []
        for i in range(2):
            d = out[(c + i) * ROWS : (c + i + 1) * ROWS]
            d_re, d_im = d[:, :LANES], d[:, LANES:]
            cols.append(
                jnp.concatenate([d_re * turn_re + d_im * turn_im, d_im * turn_re - d_re * turn_im], axis=0)
            )
        hi, lo = hi_lo(jnp.concatenate(cols, axis=1))
        time = dot(last_ref[...], jnp.concatenate([hi, hi, lo], axis=0))
        for i in range(2):
            rows_ref[pl.ds(base + c + i, ROWS, stride=FEW), :] = time[:, i * LANES : (i + 1) * LANES]


CONSTS = 5


def fetch(sources, targets, sems):
    copies = [pltpu.make_async_copy(src, dst, sems.at[i]) for i, (src, dst) in enumerate(zip(sources, targets))]
    for copy in copies:
        copy.start()
    return copies


def conv_kernel(xf_ref, *refs):
    hbm, (mixed_out, spec_out) = refs[:CONSTS], refs[CONSTS : CONSTS + 2]
    consts, (mixed_ref, spec_ref, x_rows, f_rows, m_rows, sems, mixed_sem, spec_sems) = (
        refs[CONSTS + 2 : 2 * CONSTS + 2],
        refs[2 * CONSTS + 2 :],
    )
    first_ref, second_ref, back_ref, last_ref, turn_ref = consts
    copies = fetch(hbm, consts, sems)
    spread(lambda s: xf_ref[s, :FEW], x_rows)
    spread(lambda s: xf_ref[s, FEW:], f_rows)
    for copy in copies:
        copy.wait()
    outs = []
    for base in range(0, FEW, GROUP):
        x_re, x_im = forward_group(x_rows, base, first_ref, second_ref, turn_ref)
        f_re, f_im = forward_group(f_rows, base, first_ref, second_ref, turn_ref)
        here = pl.ds(base * ROWS, GROUP * ROWS)
        spec_ref[0, here, :] = x_re
        spec_ref[1, here, :] = x_im
        spec_ref[2, here, :] = f_re
        spec_ref[3, here, :] = f_im
        out = pltpu.make_async_copy(spec_ref.at[:, here, :], spec_out.at[:, here, :], spec_sems.at[base // GROUP])
        out.start()
        outs.append(out)
        inverse_group(
            x_re * f_re - x_im * f_im, x_re * f_im + x_im * f_re, base, m_rows, back_ref, last_ref, turn_ref
        )

    def store(s, value):
        mixed_ref[s] = value

    collect(m_rows, store)
    out = pltpu.make_async_copy(mixed_ref, mixed_out, mixed_sem)
    out.start()
    outs.append(out)
    for out in outs:
        out.wait()


def grads_kernel(
    p_ref, first_ref, second_ref, back_ref, last_ref, turn_ref, spec_ref, out_ref, p_rows, i_rows, f_rows
):
    spread(lambda s: p_ref[s], p_rows)
    for base in range(0, FEW, GROUP):
        p_re, p_im = forward_group(p_rows, base, first_ref, second_ref, turn_ref)
        here = pl.ds(base * ROWS, GROUP * ROWS)
        for slot, rows in ((2, i_rows), (0, f_rows)):
            o_re = spec_ref[slot, here, :]
            o_im = spec_ref[slot + 1, here, :]
            inverse_group(
                p_re * o_re + p_im * o_im, p_im * o_re - p_re * o_im, base, rows, back_ref, last_ref, turn_ref
            )

    def store_at(first):
        def store(s, value):
            out_ref[s, first : first + FEW] = value

        return store

    collect(i_rows, store_at(0))
    collect(f_rows, store_at(FEW))


def params(mib):
    return pltpu.CompilerParams(vmem_limit_bytes=mib << 20)


def whole_vmem():
    return pl.BlockSpec(memory_space=pltpu.VMEM)


def in_hbm():
    return pl.BlockSpec(memory_space=pltpu.HBM)


ROWS_SCRATCH = pltpu.VMEM((ROWS * FEW, LANES), F32)
SPEC_SHAPE = (4, FEW * ROWS, LANES)
DMA = pltpu.SemaphoreType.DMA


def const_scratch():
    return [pltpu.VMEM(c.shape, c.dtype) for c in constants()]


def conv_call(xf):
    return pl.pallas_call(
        conv_kernel,
        out_shape=(jax.ShapeDtypeStruct((16, FEW, TOK), BF), jax.ShapeDtypeStruct(SPEC_SHAPE, F32)),
        in_specs=[whole_vmem()] + [in_hbm()] * CONSTS,
        out_specs=(in_hbm(), in_hbm()),
        scratch_shapes=const_scratch()
        + [pltpu.VMEM((16, FEW, TOK), BF), pltpu.VMEM(SPEC_SHAPE, F32)]
        + [ROWS_SCRATCH] * 3
        + [DMA((CONSTS,)), DMA, DMA((FEW // GROUP,))],
        compiler_params=params(60),
        cost_estimate=pl.CostEstimate(flops=10**9, bytes_accessed=4 << 20, transcendentals=0),
        name="conv",
    )(xf, *constants())


def grads_call(product, spec):
    return pl.pallas_call(
        grads_kernel,
        out_shape=jax.ShapeDtypeStruct((16, 2 * FEW, TOK), BF),
        in_specs=[whole_vmem()] * (CONSTS + 2),
        out_specs=whole_vmem(),
        scratch_shapes=[ROWS_SCRATCH] * 3,
        compiler_params=params(24),
        cost_estimate=pl.CostEstimate(flops=1 * 10**10, bytes_accessed=4 << 20, transcendentals=0),
        name="grads",
    )(product, *constants(), spec)


def fetch_grads(grads, held, sems):
    copies = []
    for dy in range(4):
        for part, target in enumerate((held.at[4 * dy], held.at[pl.ds(4 * dy + 1, 3)])):
            copies.append(pltpu.make_async_copy(grads[2 * dy + part], target, sems.at[2 * dy + part]))
    for copy in copies:
        copy.start()
    return copies


def weight_slot(where_ref, dy, dz):
    zh, core, y, zl = (where_ref[i] for i in range(1, 5))
    x_from = jnp.bitwise_and(y + 4 - dy, 3)
    zl_from = jnp.bitwise_and(zl + 4 - dz, 3)
    zh_from = jnp.right_shift(zl_from, 1)
    core_from = jnp.bitwise_and(zl_from, 1)
    return jnp.bitwise_xor(core, core_from) * 8 + jnp.bitwise_xor(zh, zh_from) * 4 + x_from


def grad_slot(where_ref, other, dx, dzh):
    x, zh, core, y, zl = (where_ref[i] for i in range(5))
    y_from = jnp.bitwise_and(x + dx, 3)
    zl_from = jnp.bitwise_xor(zh, dzh) * 2 + jnp.bitwise_xor(core, other)
    return jnp.bitwise_and(y + 4 - y_from, 3) * 4 + jnp.bitwise_and(zl + 4 - zl_from, 3)


def products_kernel(where_ref, *refs):
    grads, ins_hbm = [refs[i] for i in (0, 1, 2, 3, 6, 7, 4, 5)], refs[8:15]
    product_hbm, gate_grad_hbm, other_hbm, same_hbm = refs[15:19]
    held, weights, gates_ref, mixed_ref, product_ref, gate_grad_ref, sums, grad_sems, sems, out_sems = refs[19:]
    targets = [weights.at[pl.ds(4 * i, 4)] for i in range(3)] + [weights.at[pl.ds(12 + i, 2)] for i in (0, 2)]
    targets += [gates_ref, mixed_ref]
    ins = fetch(ins_hbm, targets, sems)
    copies = fetch_grads(grads, held, grad_sems)
    for copy in ins[:5]:
        copy.wait()
    total = None
    for dy in range(4):
        copies[2 * dy].wait()
        copies[2 * dy + 1].wait()
        weight = jnp.concatenate([weights[weight_slot(where_ref, dy, dz)] for dz in range(4)], axis=1)
        part = dot(weight, held[4 * dy : 4 * dy + 4].reshape(4 * CH, TOK))
        total = part if total is None else total + part
    slope = total.astype(BF).astype(F32)
    ins[5].wait()
    gates = gates_ref[...].astype(F32)
    product_ref[...] = (slope * gates).astype(BF)
    outs = [pltpu.make_async_copy(product_ref, product_hbm, out_sems.at[0])]
    outs[0].start()
    ins[6].wait()
    mixed = mixed_ref[...].astype(F32)
    gate_grad_ref[...] = (slope * mixed).astype(BF)
    outs.append(pltpu.make_async_copy(gate_grad_ref, gate_grad_hbm, out_sems.at[1]))
    outs[1].start()
    gated = (gates * mixed).astype(BF).T
    for other, target in ((1, other_hbm), (0, same_hbm)):
        for dx in range(4):
            at = other * 8 + 2 * dx
            for dzh in range(2):
                part = dot(held[grad_slot(where_ref, other, dx, dzh)], gated)
                sums[at + dzh] = (part * (SEQ**-0.5)).astype(BF)
            sem = out_sems.at[2 + other * 4 + dx]
            out = pltpu.make_async_copy(sums.at[pl.ds(at, 2)], target.at[pl.ds(2 * dx, 2)], sem)
            out.start()
            outs.append(out)
    for out in outs:
        out.wait()


def stack_kernel(*refs):
    for i, ref in enumerate(refs[:-1]):
        refs[-1][i] = ref[...]


def stack_call(parts):
    return pl.pallas_call(
        stack_kernel,
        out_shape=jax.ShapeDtypeStruct((len(parts),) + parts[0].shape, BF),
        in_specs=[whole_vmem()] * len(parts),
        out_specs=whole_vmem(),
        compiler_params=params(8),
        cost_estimate=pl.CostEstimate(flops=3 * 10**10, bytes_accessed=2 << 20, transcendentals=0),
        name="stack",
    )(*parts)


HELD = pltpu.VMEM((16, CH, TOK), BF)
SQUARES = pltpu.VMEM((16, 256, 256), BF)
TILE = pltpu.VMEM((CH, TOK), BF)


def products_call(where, grads, weights, gates, mixed):
    tile = jax.ShapeDtypeStruct((CH, TOK), BF)
    eight = jax.ShapeDtypeStruct((8, 256, 256), BF)
    return pl.pallas_call(
        products_kernel,
        out_shape=(tile, tile, eight, eight),
        in_specs=[pl.BlockSpec(memory_space=pltpu.SMEM)] + [in_hbm()] * 15,
        out_specs=(in_hbm(),) * 4,
        scratch_shapes=[HELD, SQUARES, TILE, TILE, TILE, TILE, SQUARES, DMA((8,)), DMA((7,)), DMA((10,))],
        compiler_params=params(60),
        cost_estimate=pl.CostEstimate(flops=4 * CH * TOK * 4096, bytes_accessed=9 << 20, transcendentals=0),
        name="products",
    )(where, *grads, *weights, gates, mixed)


def exchange(value):
    return lax.all_to_all(value, "ctx", split_axis=0, concat_axis=0, tiled=True)


def add(*parts):
    total = parts[0].astype(F32)
    for part in parts[1:]:
        total = total + part.astype(F32)
    return total.astype(BF)


def on_device(inputs, gates, filters, out_grad, out_weight):
    ctx = lax.axis_index("ctx")
    tp = lax.axis_index("tp")
    where = jnp.stack([ctx // 4, (ctx // 2) % 2, ctx % 2, tp // 4, tp % 4]).astype(jnp.int32)


    both = jnp.concatenate([inputs.reshape(16, FEW, TOK), filters.reshape(16, FEW, TOK)], axis=1)
    arrived = exchange(both)
    mixed_rows, spec = conv_call(arrived)
    mixed = exchange(mixed_rows).reshape(CH, TOK)

    lines = [send(out_grad, "tp", 1, 4, dz) for dz in (1, 2, 3)]
    up, far = send(out_grad, "tp", 4, 4, 1), send(out_grad, "tp", 4, 4, 2)
    w_swap = send(out_weight, "ctx", 2, 2, 1)
    up, own, w_own = lax.optimization_barrier((up, out_grad, out_weight))
    w_line = lax.all_gather(w_own.T, "ctx", axis_index_groups=LINES_X)
    near = [up, far, send(own, "tp", 4, 4, 3)]
    lines, w_line = lax.optimization_barrier((lines, w_line))
    rest, near[0], near[1], w_swap = lax.optimization_barrier((stack_call(lines), near[0], near[1], w_swap))
    w_swap, _ = lax.optimization_barrier((w_swap, mixed_rows))
    rests = [send(rest, "tp", 4, 4, dy) for dy in (1, 2, 3)]
    grads = [out_grad, rest]
    for dy in (1, 3, 2):
        grads += [near[dy - 1], rests[dy - 1]]

    w_far = lax.all_gather(w_swap.T, "ctx", axis_index_groups=LINES_X)
    weights = [w_line, w_far, send(w_line, "ctx", 1, 2, 1)]
    weights += [send(w_far[i : i + 2], "ctx", 1, 2, 1) for i in (0, 2)]

    product, gate_grad, part_other, part_same = products_call(where, grads, weights, gates, mixed)
    product_rows = exchange(product.reshape(16, FEW, TOK))
    received = send(part_other, "ctx", 1, 2, 1)
    chips = [add(part_same[2 * dx : 2 * dx + 2], received[2 * dx : 2 * dx + 2]) for dx in range(4)]

    grad_rows = grads_call(product_rows, spec)
    both_grads = exchange(grad_rows)
    input_grad = both_grads[:, :FEW].reshape(CH, TOK)
    filter_grad = both_grads[:, FEW:].reshape(CH, TOK)

    line = add(chips[0], *[send(chips[dx], "ctx", 4, 4, dx) for dx in (1, 2, 3)])
    weight_grad = add(line[0], send(line[1], "ctx", 2, 2, 1))
    return (input_grad, gate_grad, filter_grad, weight_grad)


def solution(mesh):
    in_specs = (P("tp", "ctx"), P("tp", "ctx"), P("tp", "ctx"), P("tp", "ctx"), P("ctx", "tp"))
    out_specs = (P("tp", "ctx"), P("tp", "ctx"), P("tp", "ctx"), P("ctx", "tp"))
    return jax.shard_map(
        on_device, mesh=mesh, in_specs=in_specs, out_specs=out_specs, check_vma=False
    )
```

```python
import functools

import jax
import jax.numpy as jnp
import ml_dtypes
import numpy as np
from jax import lax
from jax.experimental import pallas as pl
from jax.experimental.pallas import tpu as pltpu
from jax.sharding import PartitionSpec as P

CH = 256
TOK = 512
FEW = 16
SEQ = 8192
ROWS = 64
LANES = 128
GROUP = 8
BF = jnp.bfloat16
F32 = jnp.float32


def shift_pairs(stride, size, by):
    pairs = []
    for i in range(16):
        at = (i // stride) % size
        pairs.append((i, i + ((at + by) % size - at) * stride))
    return pairs


def send(value, axis, stride, size, by):
    return lax.ppermute(value, axis, shift_pairs(stride, size, by))


LINES_X = [[4 * x + i for x in range(4)] for i in range(4)]


def split_hi_lo(matrix):
    hi = matrix.astype(ml_dtypes.bfloat16)
    lo = (matrix - hi.astype(np.float64)).astype(ml_dtypes.bfloat16)
    return hi, lo


@functools.cache
def constants():
    n1 = np.arange(ROWS)
    k1 = np.arange(ROWS)
    n2 = np.arange(LANES)
    k2 = np.arange(LANES)
    first = np.exp(-2j * np.pi * np.outer(k1 + 0.25, n1) / ROWS)
    turn = np.exp(-2j * np.pi * np.outer(k1 + 0.25, n2) / SEQ)
    second = np.exp(-2j * np.pi * np.outer(n2, k2) / LANES)
    lhs = np.concatenate([first.real, first.imag], axis=0)
    hi, lo = split_hi_lo(lhs)
    first_c = np.concatenate([hi, lo], axis=1)

    def square(m):
        full = np.block([[m.real, m.imag], [-m.imag, m.real]])
        hi, lo = split_hi_lo(full)
        return np.concatenate([hi, hi, lo], axis=0)

    second_c = square(second)
    back_c = square(np.conj(second))
    scale = SEQ**-0.5 / SEQ
    last = np.conj(first).T * scale
    hi, lo = split_hi_lo(np.concatenate([last.real, -last.imag], axis=1))
    last_c = np.concatenate([hi, lo, hi], axis=1)
    turn_c = np.stack([turn.real, turn.imag]).astype(np.float32)
    return first_c, second_c, back_c, last_c, turn_c


def hi_lo(value):
    hi = value.astype(BF)
    lo = (value - hi.astype(F32)).astype(BF)
    return hi, lo


def dot(a, b):
    return jnp.dot(a, b, preferred_element_type=F32)


def spread(load, rows_ref):
    for s in range(16):
        block = load(s).astype(F32)
        for q in range(4):
            rows_ref[pl.ds((4 * s + q) * FEW, FEW), :] = block[:, q * LANES : (q + 1) * LANES]


def collect(rows_ref, store):
    for s in range(16):
        parts = [rows_ref[pl.ds((4 * s + q) * FEW, FEW), :] for q in range(4)]
        store(s, jnp.concatenate(parts, axis=1).astype(BF))


def forward_group(rows_ref, base, first_ref, second_ref, turn_ref):
    turn_re = turn_ref[0]
    turn_im = turn_ref[1]
    pieces = []
    for c in range(0, GROUP, 2):
        pair = [rows_ref[pl.ds(base + c + i, ROWS, stride=FEW), :].astype(BF) for i in range(2)]
        both = jnp.concatenate(pair, axis=1)
        out = dot(first_ref[...], jnp.concatenate([both, both], axis=0))
        for i in range(2):
            re = out[:ROWS, i * LANES : (i + 1) * LANES]
            im = out[ROWS:, i * LANES : (i + 1) * LANES]
            pieces.append(
                jnp.concatenate([re * turn_re - im * turn_im, re * turn_im + im * turn_re], axis=1)
            )
    hi, lo = hi_lo(jnp.concatenate(pieces, axis=0))
    spec = dot(jnp.concatenate([hi, lo, hi], axis=1), second_ref[...])
    return spec[:, :LANES], spec[:, LANES:]


def inverse_group(re, im, base, rows_ref, back_ref, last_ref, turn_ref):
    turn_re = turn_ref[0]
    turn_im = turn_ref[1]
    hi, lo = hi_lo(jnp.concatenate([re, im], axis=1))
    out = dot(jnp.concatenate([hi, lo, hi], axis=1), back_ref[...])
    for c in range(0, GROUP, 2):
        cols = []
        for i in range(2):
            d = out[(c + i) * ROWS : (c + i + 1) * ROWS]
            d_re, d_im = d[:, :LANES], d[:, LANES:]
            cols.append(
                jnp.concatenate([d_re * turn_re + d_im * turn_im, d_im * turn_re - d_re * turn_im], axis=0)
            )
        hi, lo = hi_lo(jnp.concatenate(cols, axis=1))
        time = dot(last_ref[...], jnp.concatenate([hi, hi, lo], axis=0))
        for i in range(2):
            rows_ref[pl.ds(base + c + i, ROWS, stride=FEW), :] = time[:, i * LANES : (i + 1) * LANES]


CONSTS = 5


def fetch(sources, targets, sems):
    copies = [pltpu.make_async_copy(src, dst, sems.at[i]) for i, (src, dst) in enumerate(zip(sources, targets))]
    for copy in copies:
        copy.start()
    return copies


def conv_kernel(xf_ref, *refs):
    hbm, (mixed_out, spec_out) = refs[:CONSTS], refs[CONSTS : CONSTS + 2]
    consts, (mixed_ref, spec_ref, x_rows, f_rows, m_rows, sems, mixed_sem, spec_sems) = (
        refs[CONSTS + 2 : 2 * CONSTS + 2],
        refs[2 * CONSTS + 2 :],
    )
    first_ref, second_ref, back_ref, last_ref, turn_ref = consts
    copies = fetch(hbm, consts, sems)
    spread(lambda s: xf_ref[s, :FEW], x_rows)
    spread(lambda s: xf_ref[s, FEW:], f_rows)
    for copy in copies:
        copy.wait()
    outs = []
    for base in range(0, FEW, GROUP):
        x_re, x_im = forward_group(x_rows, base, first_ref, second_ref, turn_ref)
        f_re, f_im = forward_group(f_rows, base, first_ref, second_ref, turn_ref)
        here = pl.ds(base * ROWS, GROUP * ROWS)
        spec_ref[0, here, :] = x_re
        spec_ref[1, here, :] = x_im
        spec_ref[2, here, :] = f_re
        spec_ref[3, here, :] = f_im
        out = pltpu.make_async_copy(spec_ref.at[:, here, :], spec_out.at[:, here, :], spec_sems.at[base // GROUP])
        out.start()
        outs.append(out)
        inverse_group(
            x_re * f_re - x_im * f_im, x_re * f_im + x_im * f_re, base, m_rows, back_ref, last_ref, turn_ref
        )

    def store(s, value):
        mixed_ref[s] = value

    collect(m_rows, store)
    out = pltpu.make_async_copy(mixed_ref, mixed_out, mixed_sem)
    out.start()
    outs.append(out)
    for out in outs:
        out.wait()


def grads_kernel(
    p_ref, first_ref, second_ref, back_ref, last_ref, turn_ref, spec_ref, out_ref, p_rows, i_rows, f_rows
):
    spread(lambda s: p_ref[s], p_rows)
    for base in range(0, FEW, GROUP):
        p_re, p_im = forward_group(p_rows, base, first_ref, second_ref, turn_ref)
        here = pl.ds(base * ROWS, GROUP * ROWS)
        for slot, rows in ((2, i_rows), (0, f_rows)):
            o_re = spec_ref[slot, here, :]
            o_im = spec_ref[slot + 1, here, :]
            inverse_group(
                p_re * o_re + p_im * o_im, p_im * o_re - p_re * o_im, base, rows, back_ref, last_ref, turn_ref
            )

    def store_at(first):
        def store(s, value):
            out_ref[s, first : first + FEW] = value

        return store

    collect(i_rows, store_at(0))
    collect(f_rows, store_at(FEW))


def params(mib):
    return pltpu.CompilerParams(vmem_limit_bytes=mib << 20)


def whole_vmem():
    return pl.BlockSpec(memory_space=pltpu.VMEM)


def in_hbm():
    return pl.BlockSpec(memory_space=pltpu.HBM)


ROWS_SCRATCH = pltpu.VMEM((ROWS * FEW, LANES), F32)
SPEC_SHAPE = (4, FEW * ROWS, LANES)
DMA = pltpu.SemaphoreType.DMA


def const_scratch():
    return [pltpu.VMEM(c.shape, c.dtype) for c in constants()]


def conv_call(xf):
    return pl.pallas_call(
        conv_kernel,
        out_shape=(jax.ShapeDtypeStruct((16, FEW, TOK), BF), jax.ShapeDtypeStruct(SPEC_SHAPE, F32)),
        in_specs=[whole_vmem()] + [in_hbm()] * CONSTS,
        out_specs=(in_hbm(), in_hbm()),
        scratch_shapes=const_scratch()
        + [pltpu.VMEM((16, FEW, TOK), BF), pltpu.VMEM(SPEC_SHAPE, F32)]
        + [ROWS_SCRATCH] * 3
        + [DMA((CONSTS,)), DMA, DMA((FEW // GROUP,))],
        compiler_params=params(60),
        cost_estimate=pl.CostEstimate(flops=10**9, bytes_accessed=4 << 20, transcendentals=0),
        name="conv",
    )(xf, *constants())


def grads_call(product, spec):
    return pl.pallas_call(
        grads_kernel,
        out_shape=jax.ShapeDtypeStruct((16, 2 * FEW, TOK), BF),
        in_specs=[whole_vmem()] * (CONSTS + 2),
        out_specs=whole_vmem(),
        scratch_shapes=[ROWS_SCRATCH] * 3,
        compiler_params=params(24),
        cost_estimate=pl.CostEstimate(flops=1 * 10**10, bytes_accessed=4 << 20, transcendentals=0),
        name="grads",
    )(product, *constants(), spec)


def fetch_grads(grads, held, sems):
    copies = []
    for dy in range(4):
        for part, target in enumerate((held.at[4 * dy], held.at[pl.ds(4 * dy + 1, 3)])):
            copies.append(pltpu.make_async_copy(grads[2 * dy + part], target, sems.at[2 * dy + part]))
    for copy in copies:
        copy.start()
    return copies


def weight_slot(where_ref, dy, dz):
    zh, core, y, zl = (where_ref[i] for i in range(1, 5))
    x_from = jnp.bitwise_and(y + 4 - dy, 3)
    zl_from = jnp.bitwise_and(zl + 4 - dz, 3)
    zh_from = jnp.right_shift(zl_from, 1)
    core_from = jnp.bitwise_and(zl_from, 1)
    return jnp.bitwise_xor(core, core_from) * 8 + jnp.bitwise_xor(zh, zh_from) * 4 + x_from


def grad_slot(where_ref, other, dx, dzh):
    x, zh, core, y, zl = (where_ref[i] for i in range(5))
    y_from = jnp.bitwise_and(x + dx, 3)
    zl_from = jnp.bitwise_xor(zh, dzh) * 2 + jnp.bitwise_xor(core, other)
    return jnp.bitwise_and(y + 4 - y_from, 3) * 4 + jnp.bitwise_and(zl + 4 - zl_from, 3)


def products_kernel(where_ref, *refs):
    grads, ins_hbm = [refs[i] for i in (0, 1, 2, 3, 6, 7, 4, 5)], refs[8:17]
    product_hbm, gate_grad_hbm, other_hbm, same_hbm = refs[17:21]
    held, weights, gates_ref, mixed_ref, product_ref, gate_grad_ref, sums, grad_sems, sems, out_sems = refs[21:]
    targets = [weights.at[pl.ds(4 * i, 4)] for i in range(3)] + [weights.at[pl.ds(12 + i, 1)] for i in range(4)]
    targets += [gates_ref, mixed_ref]
    ins = fetch(ins_hbm, targets, sems)
    copies = fetch_grads(grads, held, grad_sems)
    for copy in ins[:7]:
        copy.wait()
    total = None
    for dy in range(4):
        copies[2 * dy].wait()
        copies[2 * dy + 1].wait()
        weight = jnp.concatenate([weights[weight_slot(where_ref, dy, dz)] for dz in range(4)], axis=1)
        part = dot(weight, held[4 * dy : 4 * dy + 4].reshape(4 * CH, TOK))
        total = part if total is None else total + part
    slope = total.astype(BF).astype(F32)
    ins[7].wait()
    gates = gates_ref[...].astype(F32)
    product_ref[...] = (slope * gates).astype(BF)
    outs = [pltpu.make_async_copy(product_ref, product_hbm, out_sems.at[0])]
    outs[0].start()
    ins[8].wait()
    mixed = mixed_ref[...].astype(F32)
    gate_grad_ref[...] = (slope * mixed).astype(BF)
    outs.append(pltpu.make_async_copy(gate_grad_ref, gate_grad_hbm, out_sems.at[1]))
    outs[1].start()
    gated = (gates * mixed).astype(BF).T
    for other, target in ((1, other_hbm), (0, same_hbm)):
        for dx in range(4):
            at = other * 8 + 2 * dx
            for dzh in range(2):
                part = dot(held[grad_slot(where_ref, other, dx, dzh)], gated)
                sums[at + dzh] = (part * (SEQ**-0.5)).astype(BF)
            sem = out_sems.at[2 + other * 4 + dx]
            out = pltpu.make_async_copy(sums.at[pl.ds(at, 2)], target.at[pl.ds(2 * dx, 2)], sem)
            out.start()
            outs.append(out)
    for out in outs:
        out.wait()


def stack_kernel(*refs):
    for i, ref in enumerate(refs[:-1]):
        refs[-1][i] = ref[...]


def stack_call(parts):
    return pl.pallas_call(
        stack_kernel,
        out_shape=jax.ShapeDtypeStruct((len(parts),) + parts[0].shape, BF),
        in_specs=[whole_vmem()] * len(parts),
        out_specs=whole_vmem(),
        compiler_params=params(8),
        cost_estimate=pl.CostEstimate(flops=3 * 10**10, bytes_accessed=2 << 20, transcendentals=0),
        name="stack",
    )(*parts)


HELD = pltpu.VMEM((16, CH, TOK), BF)
SQUARES = pltpu.VMEM((16, 256, 256), BF)
TILE = pltpu.VMEM((CH, TOK), BF)


def products_call(where, grads, weights, gates, mixed):
    tile = jax.ShapeDtypeStruct((CH, TOK), BF)
    eight = jax.ShapeDtypeStruct((8, 256, 256), BF)
    return pl.pallas_call(
        products_kernel,
        out_shape=(tile, tile, eight, eight),
        in_specs=[pl.BlockSpec(memory_space=pltpu.SMEM)] + [in_hbm()] * 17,
        out_specs=(in_hbm(),) * 4,
        scratch_shapes=[HELD, SQUARES, TILE, TILE, TILE, TILE, SQUARES, DMA((8,)), DMA((9,)), DMA((10,))],
        compiler_params=params(60),
        cost_estimate=pl.CostEstimate(flops=4 * CH * TOK * 4096, bytes_accessed=9 << 20, transcendentals=0),
        name="products",
    )(where, *grads, *weights, gates, mixed)


def exchange(value):
    return lax.all_to_all(value, "ctx", split_axis=0, concat_axis=0, tiled=True)


def add(*parts):
    total = parts[0].astype(F32)
    for part in parts[1:]:
        total = total + part.astype(F32)
    return total.astype(BF)


def on_device(inputs, gates, filters, out_grad, out_weight):
    ctx = lax.axis_index("ctx")
    tp = lax.axis_index("tp")
    where = jnp.stack([ctx // 4, (ctx // 2) % 2, ctx % 2, tp // 4, tp % 4]).astype(jnp.int32)


    both = jnp.concatenate([inputs.reshape(16, FEW, TOK), filters.reshape(16, FEW, TOK)], axis=1)
    arrived = exchange(both)
    mixed_rows, spec = conv_call(arrived)
    mixed = exchange(mixed_rows).reshape(CH, TOK)

    lines = [send(out_grad, "tp", 1, 4, dz) for dz in (1, 2, 3)]
    up, far = send(out_grad, "tp", 4, 4, 1), send(out_grad, "tp", 4, 4, 2)
    up, own, w_own = lax.optimization_barrier((up, out_grad, out_weight))
    w_line = lax.all_gather(w_own.T, "ctx", axis_index_groups=LINES_X)
    near = [up, far, send(own, "tp", 4, 4, 3)]
    lines, w_line = lax.optimization_barrier((lines, w_line))
    rest, near = lax.optimization_barrier((stack_call(lines), near))
    rests = [send(rest, "tp", 4, 4, dy) for dy in (1, 2, 3)]
    grads = [out_grad, rest]
    for dy in (1, 3, 2):
        grads += [near[dy - 1], rests[dy - 1]]

    w_line, _ = lax.optimization_barrier((w_line, arrived))
    w_far = send(w_line, "ctx", 2, 2, 1)
    weights = [w_line, w_far, send(w_line, "ctx", 1, 2, 1)]
    weights += [send(w_far[i : i + 1], "ctx", 1, 2, 1) for i in range(4)]

    product, gate_grad, part_other, part_same = products_call(where, grads, weights, gates, mixed)
    product_rows = exchange(product.reshape(16, FEW, TOK))
    received = send(part_other, "ctx", 1, 2, 1)
    chips = [add(part_same[2 * dx : 2 * dx + 2], received[2 * dx : 2 * dx + 2]) for dx in range(4)]

    grad_rows = grads_call(product_rows, spec)
    both_grads = exchange(grad_rows)
    input_grad = both_grads[:, :FEW].reshape(CH, TOK)
    filter_grad = both_grads[:, FEW:].reshape(CH, TOK)

    line = add(chips[0], *[send(chips[dx], "ctx", 4, 4, dx) for dx in (1, 2, 3)])
    weight_grad = add(line[0], send(line[1], "ctx", 2, 2, 1))
    return (input_grad, gate_grad, filter_grad, weight_grad)


def solution(mesh):
    in_specs = (P("tp", "ctx"), P("tp", "ctx"), P("tp", "ctx"), P("tp", "ctx"), P("ctx", "tp"))
    out_specs = (P("tp", "ctx"), P("tp", "ctx"), P("tp", "ctx"), P("ctx", "tp"))
    return jax.shard_map(
        on_device, mesh=mesh, in_specs=in_specs, out_specs=out_specs, check_vma=False
    )
```

```python
import functools

import jax
import jax.numpy as jnp
import ml_dtypes
import numpy as np
from jax import lax
from jax.experimental import pallas as pl
from jax.experimental.pallas import tpu as pltpu
from jax.sharding import PartitionSpec as P

CH = 256
TOK = 512
FEW = 16
SEQ = 8192
ROWS = 64
LANES = 128
GROUP = 16
BF = jnp.bfloat16
F32 = jnp.float32


def shift_pairs(stride, size, by):
    pairs = []
    for i in range(16):
        at = (i // stride) % size
        pairs.append((i, i + ((at + by) % size - at) * stride))
    return pairs


def send(value, axis, stride, size, by):
    return lax.ppermute(value, axis, shift_pairs(stride, size, by))


LINES_X = [[4 * x + i for x in range(4)] for i in range(4)]


def split_hi_lo(matrix):
    hi = matrix.astype(ml_dtypes.bfloat16)
    lo = (matrix - hi.astype(np.float64)).astype(ml_dtypes.bfloat16)
    return hi, lo


@functools.cache
def constants():
    n1 = np.arange(ROWS)
    k1 = np.arange(ROWS)
    n2 = np.arange(LANES)
    k2 = np.arange(LANES)
    first = np.exp(-2j * np.pi * np.outer(k1 + 0.25, n1) / ROWS)
    turn = np.exp(-2j * np.pi * np.outer(k1 + 0.25, n2) / SEQ)
    second = np.exp(-2j * np.pi * np.outer(n2, k2) / LANES)
    lhs = np.concatenate([first.real, first.imag], axis=0)
    hi, lo = split_hi_lo(lhs)
    first_c = np.concatenate([hi, lo], axis=1)

    def square(m):
        full = np.block([[m.real, m.imag], [-m.imag, m.real]])
        hi, lo = split_hi_lo(full)
        return np.concatenate([hi, hi, lo], axis=0)

    second_c = square(second)
    back_c = square(np.conj(second))
    scale = SEQ**-0.5 / SEQ
    last = np.conj(first).T * scale
    hi, lo = split_hi_lo(np.concatenate([last.real, -last.imag], axis=1))
    last_c = np.concatenate([hi, lo, hi], axis=1)
    turn_c = np.stack([turn.real, turn.imag]).astype(np.float32)
    return first_c, second_c, back_c, last_c, turn_c


def hi_lo(value):
    hi = value.astype(BF)
    lo = (value - hi.astype(F32)).astype(BF)
    return hi, lo


def dot(a, b):
    return jnp.dot(a, b, preferred_element_type=F32)


def spread(load, rows_ref):
    for s in range(16):
        block = load(s).astype(F32)
        for q in range(4):
            rows_ref[pl.ds((4 * s + q) * FEW, FEW), :] = block[:, q * LANES : (q + 1) * LANES]


def collect(rows_ref, store):
    for s in range(16):
        parts = [rows_ref[pl.ds((4 * s + q) * FEW, FEW), :] for q in range(4)]
        store(s, jnp.concatenate(parts, axis=1).astype(BF))


def forward_group(rows_ref, base, first_ref, second_ref, turn_ref):
    turn_re = turn_ref[0]
    turn_im = turn_ref[1]
    pieces = []
    for c in range(0, GROUP, 2):
        pair = [rows_ref[pl.ds(base + c + i, ROWS, stride=FEW), :].astype(BF) for i in range(2)]
        both = jnp.concatenate(pair, axis=1)
        out = dot(first_ref[...], jnp.concatenate([both, both], axis=0))
        for i in range(2):
            re = out[:ROWS, i * LANES : (i + 1) * LANES]
            im = out[ROWS:, i * LANES : (i + 1) * LANES]
            pieces.append(
                jnp.concatenate([re * turn_re - im * turn_im, re * turn_im + im * turn_re], axis=1)
            )
    hi, lo = hi_lo(jnp.concatenate(pieces, axis=0))
    spec = dot(jnp.concatenate([hi, lo, hi], axis=1), second_ref[...])
    return spec[:, :LANES], spec[:, LANES:]


def inverse_group(re, im, base, rows_ref, back_ref, last_ref, turn_ref):
    turn_re = turn_ref[0]
    turn_im = turn_ref[1]
    hi, lo = hi_lo(jnp.concatenate([re, im], axis=1))
    out = dot(jnp.concatenate([hi, lo, hi], axis=1), back_ref[...])
    for c in range(0, GROUP, 2):
        cols = []
        for i in range(2):
            d = out[(c + i) * ROWS : (c + i + 1) * ROWS]
            d_re, d_im = d[:, :LANES], d[:, LANES:]
            cols.append(
                jnp.concatenate([d_re * turn_re + d_im * turn_im, d_im * turn_re - d_re * turn_im], axis=0)
            )
        hi, lo = hi_lo(jnp.concatenate(cols, axis=1))
        time = dot(last_ref[...], jnp.concatenate([hi, hi, lo], axis=0))
        for i in range(2):
            rows_ref[pl.ds(base + c + i, ROWS, stride=FEW), :] = time[:, i * LANES : (i + 1) * LANES]


CONSTS = 5


def fetch(sources, targets, sems):
    copies = [pltpu.make_async_copy(src, dst, sems.at[i]) for i, (src, dst) in enumerate(zip(sources, targets))]
    for copy in copies:
        copy.start()
    return copies


def conv_kernel(xf_ref, *refs):
    hbm, (mixed_out, spec_out) = refs[:CONSTS], refs[CONSTS : CONSTS + 2]
    consts, (mixed_ref, spec_ref, x_rows, f_rows, m_rows, sems, mixed_sem, spec_sems) = (
        refs[CONSTS + 2 : 2 * CONSTS + 2],
        refs[2 * CONSTS + 2 :],
    )
    first_ref, second_ref, back_ref, last_ref, turn_ref = consts
    copies = fetch(hbm, consts, sems)
    spread(lambda s: xf_ref[s, :FEW], x_rows)
    spread(lambda s: xf_ref[s, FEW:], f_rows)
    for copy in copies:
        copy.wait()
    outs = []
    for base in range(0, FEW, GROUP):
        x_re, x_im = forward_group(x_rows, base, first_ref, second_ref, turn_ref)
        f_re, f_im = forward_group(f_rows, base, first_ref, second_ref, turn_ref)
        here = pl.ds(base * ROWS, GROUP * ROWS)
        spec_ref[0, here, :] = x_re
        spec_ref[1, here, :] = x_im
        spec_ref[2, here, :] = f_re
        spec_ref[3, here, :] = f_im
        out = pltpu.make_async_copy(spec_ref.at[:, here, :], spec_out.at[:, here, :], spec_sems.at[base // GROUP])
        out.start()
        outs.append(out)
        inverse_group(
            x_re * f_re - x_im * f_im, x_re * f_im + x_im * f_re, base, m_rows, back_ref, last_ref, turn_ref
        )

    def store(s, value):
        mixed_ref[s] = value

    collect(m_rows, store)
    out = pltpu.make_async_copy(mixed_ref, mixed_out, mixed_sem)
    out.start()
    outs.append(out)
    for out in outs:
        out.wait()


def grads_kernel(
    p_ref, first_ref, second_ref, back_ref, last_ref, turn_ref, spec_ref, out_ref, p_rows, i_rows, f_rows
):
    spread(lambda s: p_ref[s], p_rows)
    for base in range(0, FEW, GROUP):
        p_re, p_im = forward_group(p_rows, base, first_ref, second_ref, turn_ref)
        here = pl.ds(base * ROWS, GROUP * ROWS)
        for slot, rows in ((2, i_rows), (0, f_rows)):
            o_re = spec_ref[slot, here, :]
            o_im = spec_ref[slot + 1, here, :]
            inverse_group(
                p_re * o_re + p_im * o_im, p_im * o_re - p_re * o_im, base, rows, back_ref, last_ref, turn_ref
            )

    def store_at(first):
        def store(s, value):
            out_ref[s, first : first + FEW] = value

        return store

    collect(i_rows, store_at(0))
    collect(f_rows, store_at(FEW))


def params(mib):
    return pltpu.CompilerParams(vmem_limit_bytes=mib << 20)


def whole_vmem():
    return pl.BlockSpec(memory_space=pltpu.VMEM)


def in_hbm():
    return pl.BlockSpec(memory_space=pltpu.HBM)


ROWS_SCRATCH = pltpu.VMEM((ROWS * FEW, LANES), F32)
SPEC_SHAPE = (4, FEW * ROWS, LANES)
DMA = pltpu.SemaphoreType.DMA


def const_scratch():
    return [pltpu.VMEM(c.shape, c.dtype) for c in constants()]


def conv_call(xf):
    return pl.pallas_call(
        conv_kernel,
        out_shape=(jax.ShapeDtypeStruct((16, FEW, TOK), BF), jax.ShapeDtypeStruct(SPEC_SHAPE, F32)),
        in_specs=[whole_vmem()] + [in_hbm()] * CONSTS,
        out_specs=(in_hbm(), in_hbm()),
        scratch_shapes=const_scratch()
        + [pltpu.VMEM((16, FEW, TOK), BF), pltpu.VMEM(SPEC_SHAPE, F32)]
        + [ROWS_SCRATCH] * 3
        + [DMA((CONSTS,)), DMA, DMA((FEW // GROUP,))],
        compiler_params=params(60),
        cost_estimate=pl.CostEstimate(flops=10**9, bytes_accessed=4 << 20, transcendentals=0),
        name="conv",
    )(xf, *constants())


def grads_call(product, spec):
    return pl.pallas_call(
        grads_kernel,
        out_shape=jax.ShapeDtypeStruct((16, 2 * FEW, TOK), BF),
        in_specs=[whole_vmem()] * (CONSTS + 2),
        out_specs=whole_vmem(),
        scratch_shapes=[ROWS_SCRATCH] * 3,
        compiler_params=params(24),
        cost_estimate=pl.CostEstimate(flops=1 * 10**10, bytes_accessed=4 << 20, transcendentals=0),
        name="grads",
    )(product, *constants(), spec)


def fetch_grads(grads, held, sems):
    copies = []
    for dy in range(4):
        for part, target in enumerate((held.at[4 * dy], held.at[pl.ds(4 * dy + 1, 3)])):
            copies.append(pltpu.make_async_copy(grads[2 * dy + part], target, sems.at[2 * dy + part]))
    for copy in copies:
        copy.start()
    return copies


def weight_slot(where_ref, dy, dz):
    zh, core, y, zl = (where_ref[i] for i in range(1, 5))
    x_from = jnp.bitwise_and(y + 4 - dy, 3)
    zl_from = jnp.bitwise_and(zl + 4 - dz, 3)
    zh_from = jnp.right_shift(zl_from, 1)
    core_from = jnp.bitwise_and(zl_from, 1)
    return jnp.bitwise_xor(core, core_from) * 8 + jnp.bitwise_xor(zh, zh_from) * 4 + x_from


def grad_slot(where_ref, other, dx, dzh):
    x, zh, core, y, zl = (where_ref[i] for i in range(5))
    y_from = jnp.bitwise_and(x + dx, 3)
    zl_from = jnp.bitwise_xor(zh, dzh) * 2 + jnp.bitwise_xor(core, other)
    return jnp.bitwise_and(y + 4 - y_from, 3) * 4 + jnp.bitwise_and(zl + 4 - zl_from, 3)


def products_kernel(where_ref, *refs):
    grads, ins_hbm = [refs[i] for i in (0, 1, 2, 3, 6, 7, 4, 5)], refs[8:17]
    product_hbm, gate_grad_hbm, other_hbm, same_hbm = refs[17:21]
    held, weights, gates_ref, mixed_ref, product_ref, gate_grad_ref, sums, grad_sems, sems, out_sems = refs[21:]
    targets = [weights.at[pl.ds(4 * i, 4)] for i in range(3)] + [weights.at[pl.ds(12 + i, 1)] for i in range(4)]
    targets += [gates_ref, mixed_ref]
    ins = fetch(ins_hbm, targets, sems)
    copies = fetch_grads(grads, held, grad_sems)
    for copy in ins[:7]:
        copy.wait()
    total = None
    for dy in range(4):
        copies[2 * dy].wait()
        copies[2 * dy + 1].wait()
        weight = jnp.concatenate([weights[weight_slot(where_ref, dy, dz)] for dz in range(4)], axis=1)
        part = dot(weight, held[4 * dy : 4 * dy + 4].reshape(4 * CH, TOK))
        total = part if total is None else total + part
    slope = total.astype(BF).astype(F32)
    ins[7].wait()
    gates = gates_ref[...].astype(F32)
    product_ref[...] = (slope * gates).astype(BF)
    outs = [pltpu.make_async_copy(product_ref, product_hbm, out_sems.at[0])]
    outs[0].start()
    ins[8].wait()
    mixed = mixed_ref[...].astype(F32)
    gate_grad_ref[...] = (slope * mixed).astype(BF)
    outs.append(pltpu.make_async_copy(gate_grad_ref, gate_grad_hbm, out_sems.at[1]))
    outs[1].start()
    gated = (gates * mixed).astype(BF).T
    for other, target in ((1, other_hbm), (0, same_hbm)):
        for dx in range(4):
            at = other * 8 + 2 * dx
            for dzh in range(2):
                part = dot(held[grad_slot(where_ref, other, dx, dzh)], gated)
                sums[at + dzh] = (part * (SEQ**-0.5)).astype(BF)
            sem = out_sems.at[2 + other * 4 + dx]
            out = pltpu.make_async_copy(sums.at[pl.ds(at, 2)], target.at[pl.ds(2 * dx, 2)], sem)
            out.start()
            outs.append(out)
    for out in outs:
        out.wait()


def stack_kernel(*refs):
    for i, ref in enumerate(refs[:-1]):
        refs[-1][i] = ref[...]


def stack_call(parts):
    return pl.pallas_call(
        stack_kernel,
        out_shape=jax.ShapeDtypeStruct((len(parts),) + parts[0].shape, BF),
        in_specs=[whole_vmem()] * len(parts),
        out_specs=whole_vmem(),
        compiler_params=params(8),
        cost_estimate=pl.CostEstimate(flops=3 * 10**10, bytes_accessed=2 << 20, transcendentals=0),
        name="stack",
    )(*parts)


HELD = pltpu.VMEM((16, CH, TOK), BF)
SQUARES = pltpu.VMEM((16, 256, 256), BF)
TILE = pltpu.VMEM((CH, TOK), BF)


def products_call(where, grads, weights, gates, mixed):
    tile = jax.ShapeDtypeStruct((CH, TOK), BF)
    eight = jax.ShapeDtypeStruct((8, 256, 256), BF)
    return pl.pallas_call(
        products_kernel,
        out_shape=(tile, tile, eight, eight),
        in_specs=[pl.BlockSpec(memory_space=pltpu.SMEM)] + [in_hbm()] * 17,
        out_specs=(in_hbm(),) * 4,
        scratch_shapes=[HELD, SQUARES, TILE, TILE, TILE, TILE, SQUARES, DMA((8,)), DMA((9,)), DMA((10,))],
        compiler_params=params(60),
        cost_estimate=pl.CostEstimate(flops=4 * CH * TOK * 4096, bytes_accessed=9 << 20, transcendentals=0),
        name="products",
    )(where, *grads, *weights, gates, mixed)


def exchange(value):
    return lax.all_to_all(value, "ctx", split_axis=0, concat_axis=0, tiled=True)


def add(*parts):
    total = parts[0].astype(F32)
    for part in parts[1:]:
        total = total + part.astype(F32)
    return total.astype(BF)


def on_device(inputs, gates, filters, out_grad, out_weight):
    ctx = lax.axis_index("ctx")
    tp = lax.axis_index("tp")
    where = jnp.stack([ctx // 4, (ctx // 2) % 2, ctx % 2, tp // 4, tp % 4]).astype(jnp.int32)


    both = jnp.concatenate([inputs.reshape(16, FEW, TOK), filters.reshape(16, FEW, TOK)], axis=1)
    arrived = exchange(both)
    mixed_rows, spec = conv_call(arrived)
    mixed = exchange(mixed_rows).reshape(CH, TOK)

    lines = [send(out_grad, "tp", 1, 4, dz) for dz in (1, 2, 3)]
    up, far = send(out_grad, "tp", 4, 4, 1), send(out_grad, "tp", 4, 4, 2)
    up, own, w_own = lax.optimization_barrier((up, out_grad, out_weight))
    w_line = lax.all_gather(w_own.T, "ctx", axis_index_groups=LINES_X)
    near = [up, far, send(own, "tp", 4, 4, 3)]
    lines, w_line = lax.optimization_barrier((lines, w_line))
    rest, near = lax.optimization_barrier((stack_call(lines), near))
    rests = [send(rest, "tp", 4, 4, dy) for dy in (1, 2, 3)]
    grads = [out_grad, rest]
    for dy in (1, 3, 2):
        grads += [near[dy - 1], rests[dy - 1]]

    w_line, _ = lax.optimization_barrier((w_line, arrived))
    w_far = send(w_line, "ctx", 2, 2, 1)
    weights = [w_line, w_far, send(w_line, "ctx", 1, 2, 1)]
    weights += [send(w_far[i : i + 1], "ctx", 1, 2, 1) for i in range(4)]

    product, gate_grad, part_other, part_same = products_call(where, grads, weights, gates, mixed)
    product_rows = exchange(product.reshape(16, FEW, TOK))
    received = send(part_other, "ctx", 1, 2, 1)
    chips = [add(part_same[2 * dx : 2 * dx + 2], received[2 * dx : 2 * dx + 2]) for dx in range(4)]

    grad_rows = grads_call(product_rows, spec)
    both_grads = exchange(grad_rows)
    input_grad = both_grads[:, :FEW].reshape(CH, TOK)
    filter_grad = both_grads[:, FEW:].reshape(CH, TOK)

    line = add(chips[0], *[send(chips[dx], "ctx", 4, 4, dx) for dx in (1, 2, 3)])
    weight_grad = add(line[0], send(line[1], "ctx", 2, 2, 1))
    return (input_grad, gate_grad, filter_grad, weight_grad)


def solution(mesh):
    in_specs = (P("tp", "ctx"), P("tp", "ctx"), P("tp", "ctx"), P("tp", "ctx"), P("ctx", "tp"))
    out_specs = (P("tp", "ctx"), P("tp", "ctx"), P("tp", "ctx"), P("ctx", "tp"))
    return jax.shard_map(
        on_device, mesh=mesh, in_specs=in_specs, out_specs=out_specs, check_vma=False
    )
```

```python
import functools

import jax
import jax.numpy as jnp
import ml_dtypes
import numpy as np
from jax import lax
from jax.experimental import pallas as pl
from jax.experimental.pallas import tpu as pltpu
from jax.sharding import PartitionSpec as P

CH = 256
TOK = 512
FEW = 16
SEQ = 8192
ROWS = 64
LANES = 128
GROUP = 16
BF = jnp.bfloat16
F32 = jnp.float32


def shift_pairs(stride, size, by):
    pairs = []
    for i in range(16):
        at = (i // stride) % size
        pairs.append((i, i + ((at + by) % size - at) * stride))
    return pairs


def send(value, axis, stride, size, by):
    return lax.ppermute(value, axis, shift_pairs(stride, size, by))


LINES_X = [[4 * x + i for x in range(4)] for i in range(4)]


def split_hi_lo(matrix):
    hi = matrix.astype(ml_dtypes.bfloat16)
    lo = (matrix - hi.astype(np.float64)).astype(ml_dtypes.bfloat16)
    return hi, lo


@functools.cache
def constants():
    n1 = np.arange(ROWS)
    k1 = np.arange(ROWS)
    n2 = np.arange(LANES)
    k2 = np.arange(LANES)
    first = np.exp(-2j * np.pi * np.outer(k1 + 0.25, n1) / ROWS)
    turn = np.exp(-2j * np.pi * np.outer(k1 + 0.25, n2) / SEQ)
    second = np.exp(-2j * np.pi * np.outer(n2, k2) / LANES)
    lhs = np.concatenate([first.real, first.imag], axis=0)
    hi, lo = split_hi_lo(lhs)
    first_c = np.concatenate([hi, lo], axis=1)

    def square(m):
        full = np.block([[m.real, m.imag], [-m.imag, m.real]])
        hi, lo = split_hi_lo(full)
        return np.concatenate([hi, hi, lo], axis=0)

    second_c = square(second)
    back_c = square(np.conj(second))
    scale = SEQ**-0.5 / SEQ
    last = np.conj(first).T * scale
    hi, lo = split_hi_lo(np.concatenate([last.real, -last.imag], axis=1))
    last_c = np.concatenate([hi, lo, hi], axis=1)
    turn_c = np.stack([turn.real, turn.imag]).astype(np.float32)
    return first_c, second_c, back_c, last_c, turn_c


def hi_lo(value):
    hi = value.astype(BF)
    lo = (value - hi.astype(F32)).astype(BF)
    return hi, lo


def dot(a, b):
    return jnp.dot(a, b, preferred_element_type=F32)


def spread(load, rows_ref):
    for s in range(16):
        block = load(s).astype(F32)
        for q in range(4):
            rows_ref[pl.ds((4 * s + q) * FEW, FEW), :] = block[:, q * LANES : (q + 1) * LANES]


def collect(rows_ref, store):
    for s in range(16):
        parts = [rows_ref[pl.ds((4 * s + q) * FEW, FEW), :] for q in range(4)]
        store(s, jnp.concatenate(parts, axis=1).astype(BF))


def forward_group(rows_ref, base, first_ref, second_ref, turn_ref):
    turn_re = turn_ref[0]
    turn_im = turn_ref[1]
    pieces = []
    for c in range(0, GROUP, 2):
        pair = [rows_ref[pl.ds(base + c + i, ROWS, stride=FEW), :].astype(BF) for i in range(2)]
        both = jnp.concatenate(pair, axis=1)
        out = dot(first_ref[...], jnp.concatenate([both, both], axis=0))
        for i in range(2):
            re = out[:ROWS, i * LANES : (i + 1) * LANES]
            im = out[ROWS:, i * LANES : (i + 1) * LANES]
            pieces.append(
                jnp.concatenate([re * turn_re - im * turn_im, re * turn_im + im * turn_re], axis=1)
            )
    hi, lo = hi_lo(jnp.concatenate(pieces, axis=0))
    spec = dot(jnp.concatenate([hi, lo, hi], axis=1), second_ref[...])
    return spec[:, :LANES], spec[:, LANES:]


def inverse_group(re, im, base, rows_ref, back_ref, last_ref, turn_ref):
    turn_re = turn_ref[0]
    turn_im = turn_ref[1]
    hi, lo = hi_lo(jnp.concatenate([re, im], axis=1))
    out = dot(jnp.concatenate([hi, lo, hi], axis=1), back_ref[...])
    for c in range(0, GROUP, 2):
        cols = []
        for i in range(2):
            d = out[(c + i) * ROWS : (c + i + 1) * ROWS]
            d_re, d_im = d[:, :LANES], d[:, LANES:]
            cols.append(
                jnp.concatenate([d_re * turn_re + d_im * turn_im, d_im * turn_re - d_re * turn_im], axis=0)
            )
        hi, lo = hi_lo(jnp.concatenate(cols, axis=1))
        time = dot(last_ref[...], jnp.concatenate([hi, hi, lo], axis=0))
        for i in range(2):
            rows_ref[pl.ds(base + c + i, ROWS, stride=FEW), :] = time[:, i * LANES : (i + 1) * LANES]


CONSTS = 5


def fetch(sources, targets, sems):
    copies = [pltpu.make_async_copy(src, dst, sems.at[i]) for i, (src, dst) in enumerate(zip(sources, targets))]
    for copy in copies:
        copy.start()
    return copies


def conv_kernel(xf_ref, *refs):
    hbm, (mixed_out, spec_out) = refs[:CONSTS], refs[CONSTS : CONSTS + 2]
    consts, (mixed_ref, spec_ref, x_rows, f_rows, m_rows, sems, mixed_sem, spec_sems) = (
        refs[CONSTS + 2 : 2 * CONSTS + 2],
        refs[2 * CONSTS + 2 :],
    )
    first_ref, second_ref, back_ref, last_ref, turn_ref = consts
    copies = fetch(hbm, consts, sems)
    spread(lambda s: xf_ref[s, :FEW], x_rows)
    spread(lambda s: xf_ref[s, FEW:], f_rows)
    for copy in copies:
        copy.wait()
    outs = []
    for base in range(0, FEW, GROUP):
        x_re, x_im = forward_group(x_rows, base, first_ref, second_ref, turn_ref)
        f_re, f_im = forward_group(f_rows, base, first_ref, second_ref, turn_ref)
        here = pl.ds(base * ROWS, GROUP * ROWS)
        spec_ref[0, here, :] = x_re
        spec_ref[1, here, :] = x_im
        spec_ref[2, here, :] = f_re
        spec_ref[3, here, :] = f_im
        out = pltpu.make_async_copy(spec_ref.at[:, here, :], spec_out.at[:, here, :], spec_sems.at[base // GROUP])
        out.start()
        outs.append(out)
        inverse_group(
            x_re * f_re - x_im * f_im, x_re * f_im + x_im * f_re, base, m_rows, back_ref, last_ref, turn_ref
        )

    def store(s, value):
        mixed_ref[s] = value

    collect(m_rows, store)
    out = pltpu.make_async_copy(mixed_ref, mixed_out, mixed_sem)
    out.start()
    outs.append(out)
    for out in outs:
        out.wait()


def grads_kernel(
    p_ref, first_ref, second_ref, back_ref, last_ref, turn_ref, spec_ref, out_ref, p_rows, i_rows, f_rows
):
    spread(lambda s: p_ref[s], p_rows)
    for base in range(0, FEW, GROUP):
        p_re, p_im = forward_group(p_rows, base, first_ref, second_ref, turn_ref)
        here = pl.ds(base * ROWS, GROUP * ROWS)
        for slot, rows in ((2, i_rows), (0, f_rows)):
            o_re = spec_ref[slot, here, :]
            o_im = spec_ref[slot + 1, here, :]
            inverse_group(
                p_re * o_re + p_im * o_im, p_im * o_re - p_re * o_im, base, rows, back_ref, last_ref, turn_ref
            )

    def store_at(first):
        def store(s, value):
            out_ref[s, first : first + FEW] = value

        return store

    collect(i_rows, store_at(0))
    collect(f_rows, store_at(FEW))


def params(mib):
    return pltpu.CompilerParams(vmem_limit_bytes=mib << 20)


def whole_vmem():
    return pl.BlockSpec(memory_space=pltpu.VMEM)


def in_hbm():
    return pl.BlockSpec(memory_space=pltpu.HBM)


ROWS_SCRATCH = pltpu.VMEM((ROWS * FEW, LANES), F32)
SPEC_SHAPE = (4, FEW * ROWS, LANES)
DMA = pltpu.SemaphoreType.DMA


def const_scratch():
    return [pltpu.VMEM(c.shape, c.dtype) for c in constants()]


def conv_call(xf):
    return pl.pallas_call(
        conv_kernel,
        out_shape=(jax.ShapeDtypeStruct((16, FEW, TOK), BF), jax.ShapeDtypeStruct(SPEC_SHAPE, F32)),
        in_specs=[whole_vmem()] + [in_hbm()] * CONSTS,
        out_specs=(in_hbm(), in_hbm()),
        scratch_shapes=const_scratch()
        + [pltpu.VMEM((16, FEW, TOK), BF), pltpu.VMEM(SPEC_SHAPE, F32)]
        + [ROWS_SCRATCH] * 3
        + [DMA((CONSTS,)), DMA, DMA((FEW // GROUP,))],
        compiler_params=params(60),
        cost_estimate=pl.CostEstimate(flops=10**9, bytes_accessed=4 << 20, transcendentals=0),
        name="conv",
    )(xf, *constants())


def grads_call(product, spec):
    return pl.pallas_call(
        grads_kernel,
        out_shape=jax.ShapeDtypeStruct((16, 2 * FEW, TOK), BF),
        in_specs=[whole_vmem()] * (CONSTS + 2),
        out_specs=whole_vmem(),
        scratch_shapes=[ROWS_SCRATCH] * 3,
        compiler_params=params(24),
        cost_estimate=pl.CostEstimate(flops=1 * 10**10, bytes_accessed=4 << 20, transcendentals=0),
        name="grads",
    )(product, *constants(), spec)


def fetch_grads(grads, held, sems):
    copies = []
    for dy in range(4):
        for part, target in enumerate((held.at[4 * dy], held.at[pl.ds(4 * dy + 1, 3)])):
            copies.append(pltpu.make_async_copy(grads[2 * dy + part], target, sems.at[2 * dy + part]))
    for copy in copies:
        copy.start()
    return copies


def weight_slot(where_ref, dy, dz):
    zh, core, y, zl = (where_ref[i] for i in range(1, 5))
    x_from = jnp.bitwise_and(y + 4 - dy, 3)
    zl_from = jnp.bitwise_and(zl + 4 - dz, 3)
    zh_from = jnp.right_shift(zl_from, 1)
    core_from = jnp.bitwise_and(zl_from, 1)
    return jnp.bitwise_xor(core, core_from) * 8 + jnp.bitwise_xor(zh, zh_from) * 4 + x_from


def grad_slot(where_ref, other, dx, dzh):
    x, zh, core, y, zl = (where_ref[i] for i in range(5))
    y_from = jnp.bitwise_and(x + dx, 3)
    zl_from = jnp.bitwise_xor(zh, dzh) * 2 + jnp.bitwise_xor(core, other)
    return jnp.bitwise_and(y + 4 - y_from, 3) * 4 + jnp.bitwise_and(zl + 4 - zl_from, 3)


def products_kernel(where_ref, *refs):
    grads, ins_hbm = [refs[i] for i in (0, 1, 2, 3, 6, 7, 4, 5)], refs[8:17]
    product_hbm, gate_grad_hbm, other_hbm, same_hbm = refs[17:21]
    held, weights, gates_ref, mixed_ref, product_ref, gate_grad_ref, sums, grad_sems, sems, out_sems = refs[21:]
    targets = [weights.at[pl.ds(4 * i, 4)] for i in range(3)] + [weights.at[pl.ds(12 + i, 1)] for i in range(4)]
    targets += [gates_ref, mixed_ref]
    ins = fetch(ins_hbm, targets, sems)
    copies = fetch_grads(grads, held, grad_sems)
    for copy in ins[:7]:
        copy.wait()
    total = None
    for dy in range(4):
        copies[2 * dy].wait()
        copies[2 * dy + 1].wait()
        weight = jnp.concatenate([weights[weight_slot(where_ref, dy, dz)] for dz in range(4)], axis=1)
        part = dot(weight, held[4 * dy : 4 * dy + 4].reshape(4 * CH, TOK))
        total = part if total is None else total + part
    slope = total.astype(BF).astype(F32)
    ins[7].wait()
    gates = gates_ref[...].astype(F32)
    product_ref[...] = (slope * gates).astype(BF)
    outs = [pltpu.make_async_copy(product_ref, product_hbm, out_sems.at[0])]
    outs[0].start()
    ins[8].wait()
    mixed = mixed_ref[...].astype(F32)
    gate_grad_ref[...] = (slope * mixed).astype(BF)
    outs.append(pltpu.make_async_copy(gate_grad_ref, gate_grad_hbm, out_sems.at[1]))
    outs[1].start()
    gated = (gates * mixed).astype(BF).T
    for other, target in ((1, other_hbm), (0, same_hbm)):
        for half in range(2):
            places = [(2 * half + i, dzh) for i in range(2) for dzh in range(2)]
            blocks = [held[grad_slot(where_ref, other, dx, dzh)] for dx, dzh in places]
            part = dot(jnp.concatenate(blocks, axis=0), gated)
            at = other * 8 + 4 * half
            sums[at : at + 4] = (part * (SEQ**-0.5)).astype(BF).reshape(4, 256, 256)
            sem = out_sems.at[2 + other * 2 + half]
            out = pltpu.make_async_copy(sums.at[pl.ds(at, 4)], target.at[pl.ds(4 * half, 4)], sem)
            out.start()
            outs.append(out)
    for out in outs:
        out.wait()


def stack_kernel(*refs):
    for i, ref in enumerate(refs[:-1]):
        refs[-1][i] = ref[...]


def stack_call(parts):
    return pl.pallas_call(
        stack_kernel,
        out_shape=jax.ShapeDtypeStruct((len(parts),) + parts[0].shape, BF),
        in_specs=[whole_vmem()] * len(parts),
        out_specs=whole_vmem(),
        compiler_params=params(8),
        cost_estimate=pl.CostEstimate(flops=3 * 10**10, bytes_accessed=2 << 20, transcendentals=0),
        name="stack",
    )(*parts)


HELD = pltpu.VMEM((16, CH, TOK), BF)
SQUARES = pltpu.VMEM((16, 256, 256), BF)
TILE = pltpu.VMEM((CH, TOK), BF)


def products_call(where, grads, weights, gates, mixed):
    tile = jax.ShapeDtypeStruct((CH, TOK), BF)
    eight = jax.ShapeDtypeStruct((8, 256, 256), BF)
    return pl.pallas_call(
        products_kernel,
        out_shape=(tile, tile, eight, eight),
        in_specs=[pl.BlockSpec(memory_space=pltpu.SMEM)] + [in_hbm()] * 17,
        out_specs=(in_hbm(),) * 4,
        scratch_shapes=[HELD, SQUARES, TILE, TILE, TILE, TILE, SQUARES, DMA((8,)), DMA((9,)), DMA((6,))],
        compiler_params=params(60),
        cost_estimate=pl.CostEstimate(flops=4 * CH * TOK * 4096, bytes_accessed=9 << 20, transcendentals=0),
        name="products",
    )(where, *grads, *weights, gates, mixed)


def exchange(value):
    return lax.all_to_all(value, "ctx", split_axis=0, concat_axis=0, tiled=True)


def add(*parts):
    total = parts[0].astype(F32)
    for part in parts[1:]:
        total = total + part.astype(F32)
    return total.astype(BF)


def on_device(inputs, gates, filters, out_grad, out_weight):
    ctx = lax.axis_index("ctx")
    tp = lax.axis_index("tp")
    where = jnp.stack([ctx // 4, (ctx // 2) % 2, ctx % 2, tp // 4, tp % 4]).astype(jnp.int32)


    both = jnp.concatenate([inputs.reshape(16, FEW, TOK), filters.reshape(16, FEW, TOK)], axis=1)
    arrived = exchange(both)
    mixed_rows, spec = conv_call(arrived)
    mixed = exchange(mixed_rows).reshape(CH, TOK)

    lines = [send(out_grad, "tp", 1, 4, dz) for dz in (1, 2, 3)]
    up, far = send(out_grad, "tp", 4, 4, 1), send(out_grad, "tp", 4, 4, 2)
    up, own, w_own = lax.optimization_barrier((up, out_grad, out_weight))
    w_line = lax.all_gather(w_own.T, "ctx", axis_index_groups=LINES_X)
    near = [up, far, send(own, "tp", 4, 4, 3)]
    lines, w_line = lax.optimization_barrier((lines, w_line))
    rest, near = lax.optimization_barrier((stack_call(lines), near))
    rests = [send(rest, "tp", 4, 4, dy) for dy in (1, 2, 3)]
    grads = [out_grad, rest]
    for dy in (1, 3, 2):
        grads += [near[dy - 1], rests[dy - 1]]

    w_line, _ = lax.optimization_barrier((w_line, arrived))
    w_far = send(w_line, "ctx", 2, 2, 1)
    weights = [w_line, w_far, send(w_line, "ctx", 1, 2, 1)]
    weights += [send(w_far[i : i + 1], "ctx", 1, 2, 1) for i in range(4)]

    product, gate_grad, part_other, part_same = products_call(where, grads, weights, gates, mixed)
    product_rows = exchange(product.reshape(16, FEW, TOK))
    received = send(part_other, "ctx", 1, 2, 1)
    chips = [add(part_same[2 * dx : 2 * dx + 2], received[2 * dx : 2 * dx + 2]) for dx in range(4)]

    grad_rows = grads_call(product_rows, spec)
    both_grads = exchange(grad_rows)
    input_grad = both_grads[:, :FEW].reshape(CH, TOK)
    filter_grad = both_grads[:, FEW:].reshape(CH, TOK)

    line = add(chips[0], *[send(chips[dx], "ctx", 4, 4, dx) for dx in (1, 2, 3)])
    weight_grad = add(line[0], send(line[1], "ctx", 2, 2, 1))
    return (input_grad, gate_grad, filter_grad, weight_grad)


def solution(mesh):
    in_specs = (P("tp", "ctx"), P("tp", "ctx"), P("tp", "ctx"), P("tp", "ctx"), P("ctx", "tp"))
    out_specs = (P("tp", "ctx"), P("tp", "ctx"), P("tp", "ctx"), P("ctx", "tp"))
    return jax.shard_map(
        on_device, mesh=mesh, in_specs=in_specs, out_specs=out_specs, check_vma=False
    )
```
